32 devices in a mesh: dp: 8 (over z, y), tensor: 4 (over x, core).
Axes of the slice: x: 2, y: 2, z: 4, core: 2. Of those that a mesh axis runs over, the one named last changes fastest.
Arguments:
- hidden_in: bfloat16 [8192, 1536], P(('dp', 'tensor')), may hold values from -6 to 6
- cotangent: bfloat16 [8192, 1536], P(('dp', 'tensor')), may hold values from -6 to 6
- lengths: int32 [8], P('dp'), may hold values from 256 to 1024, as said below
- routes: int32 [8192, 8], P(('dp', 'tensor')), may hold values from 0 to 63, all different within a row
- gate_values: float32 [8192, 8], P(('dp', 'tensor')), may hold values from 0.05 to 0.25
- pair_order: int32 [32, 2048], P(('dp', 'tensor')), may hold values from 0 to 2047, each once within a row
- query_weight: float32 [1536, 1536], P('dp', 'tensor'), may hold values from -0.15625 to 0.15625
- keyvalue_matrix: float32 [2, 1536, 512], P(None, 'dp', 'tensor'), may hold values from -0.15625 to 0.15625
- outproj_weight: float32 [1536, 1536], P('tensor', 'dp'), may hold values from -1.75 to 1.75
- norm_gains: float32 [2, 1536], P(None, 'dp'), may hold values from 0.5 to 1.5
- upgate_weight: float32 [2, 64, 1536, 512], P(None, 'dp', None, 'tensor'), may hold values from -0.15625 to 0.15625
- downproj_weight: float32 [64, 512, 1536], P('dp', 'tensor'), may hold values from -0.25 to 0.25
- query_mean: float32 [1536, 1536], P('dp', 'tensor'), may hold values from -32 to 32
- query_sqmean: float32 [1536, 1536], P('dp', 'tensor'), may hold values from 49.152 to 229.376
- keyvalue_first_moment: float32 [2, 1536, 512], P(None, 'dp', 'tensor'), may hold values from -32 to 32
- keyvalue_second_moment: float32 [2, 1536, 512], P(None, 'dp', 'tensor'), may hold values from 49.152 to 229.376
- outproj_mean: float32 [1536, 1536], P('tensor', 'dp'), may hold values from -3 to 3
- outproj_sqmean: float32 [1536, 1536], P('tensor', 'dp'), may hold values from 0.49152 to 2.29376
- gains_mean: float32 [2, 1536], P(None, 'dp'), may hold values from -32 to 32
- gains_sqmean: float32 [2, 1536], P(None, 'dp'), may hold values from 49.152 to 229.376
- upgate_mean: float32 [2, 64, 1536, 512], P(None, 'dp', None, 'tensor'), may hold values from -2 to 2
- upgate_sqmean: float32 [2, 64, 1536, 512], P(None, 'dp', None, 'tensor'), may hold values from 0.256 to 1.1264
- downproj_mean: float32 [64, 512, 1536], P('dp', 'tensor'), may hold values from -1.5 to 1.5
- downproj_sqmean: float32 [64, 512, 1536], P('dp', 'tensor'), may hold values from 0.12288 to 0.55296
Outputs:
- block_out: bfloat16 [8192, 1536], P(('dp', 'tensor'))
- input_grad: float32 [8192, 1536], P(('dp', 'tensor'))
- gate_grad: float32 [8192, 8], P(('dp', 'tensor'))
- query_grad: float32 [1536, 1536], P('dp', 'tensor')
- query_newmean: float32 [1536, 1536], P('dp', 'tensor')
- query_newsq: float32 [1536, 1536], P('dp', 'tensor')
- query_update: float32 [1536, 1536], P('dp', 'tensor')
- keyval_grad: float32 [2, 1536, 512], P(None, 'dp', 'tensor')
- keyval_newmean: float32 [2, 1536, 512], P(None, 'dp', 'tensor')
- keyval_newsq: float32 [2, 1536, 512], P(None, 'dp', 'tensor')
- keyval_update: float32 [2, 1536, 512], P(None, 'dp', 'tensor')
- outproj_grad: float32 [1536, 1536], P('tensor', 'dp')
- outproj_newmean: float32 [1536, 1536], P('tensor', 'dp')
- outproj_newsq: float32 [1536, 1536], P('tensor', 'dp')
- outproj_update: float32 [1536, 1536], P('tensor', 'dp')
- gains_grad: float32 [2, 1536], P(None, 'dp')
- gains_newmean: float32 [2, 1536], P(None, 'dp')
- gains_newsq: float32 [2, 1536], P(None, 'dp')
- gains_update: float32 [2, 1536], P(None, 'dp')
- upgate_grad: float32 [2, 64, 1536, 512], P(None, 'dp', None, 'tensor')
- upgate_newmean: float32 [2, 64, 1536, 512], P(None, 'dp', None, 'tensor')
- upgate_newsq: float32 [2, 64, 1536, 512], P(None, 'dp', None, 'tensor')
- upgate_update: float32 [2, 64, 1536, 512], P(None, 'dp', None, 'tensor')
- downproj_grad: float32 [64, 512, 1536], P('dp', 'tensor')
- downproj_newmean: float32 [64, 512, 1536], P('dp', 'tensor')
- downproj_newsq: float32 [64, 512, 1536], P('dp', 'tensor')
- downproj_update: float32 [64, 512, 1536], P('dp', 'tensor')
The draws below stay inside these ranges and needn't reach their ends.
Inputs may be any that keep to these rules, and one draw needn't show every extreme that they name: `lengths`: positions of a sequence at or past its length are padding; some sequence has length 1024 and some has 256. `routes`: the 8 entries of a token are distinct experts. `pair_order`: each row is a permutation of the 2048 pairs of one block; lower values take slots first.
All inputs are finite; a program needn't handle non-finite values.
Results may differ from the reference program's by a relative error of at most 0.023.
Values may be sent and summed in bfloat16 or wider, within the bound.
No kernel may reach another device: no remote copies, remote signals or barrier semaphores. Data moves between devices by JAX's collectives and lax.ppermute only.
A program may use at most 576 MiB of HBM per device.

```python
import math
from functools import partial
import jax
import jax.numpy as jnp
from jax import lax

MODEL_DIMENSION = 1536
QUERY_HEADS = 24
KEYVALUE_HEADS = 8
HEAD_SIZE = 64
FF = 512
TOP = 8
SEQUENCE_SLOTS = 1024
EXPERTS = 64
ADAM_STEP = 5
TOK_DEV = 256
TOKEN_TOTAL = 8192
SEQUENCE_TOTAL = 8
CAP = 40
MINLEN = 256
N_DP = 8
N_TENSOR = 4


def draw_lengths(key, part):
    drawn = jax.random.randint(key, (SEQUENCE_TOTAL,), MINLEN, SEQUENCE_SLOTS + 1)
    chosen = jax.random.randint(jax.random.fold_in(key, 7), (), 0, SEQUENCE_TOTAL)
    position = jnp.arange(SEQUENCE_TOTAL)
    drawn = jnp.where(position == chosen, SEQUENCE_SLOTS, drawn)
    drawn = jnp.where(position == (chosen + 1) % SEQUENCE_TOTAL, MINLEN, drawn)
    return drawn.astype(jnp.int32)


def levels(key, shape, shards, least, largest):
    def one(dim, shards_of):
        heights = jax.random.uniform(jax.random.fold_in(jax.random.fold_in(key, 6), dim), (shards_of,), jnp.float32, least / len(shards), largest / len(shards))
        return jnp.repeat(jnp.exp(heights), shape[dim] // shards_of).reshape((-1,) + (1,) * (len(shape) - dim - 1))

    loudness = one(*shards[0])
    for cut in shards[1:]:
        loudness = loudness * one(*cut)
    return loudness


def distinct(own_key, rows, amount, top, lift):
    sequence = jax.random.permutation(jax.random.fold_in(own_key, 1), amount)
    boost = sequence
    for power in range(3):
        boost = boost * boost // amount
    boost = boost * lift // amount
    lots = jax.random.randint(jax.random.fold_in(own_key, 2), (rows, amount), 0, 4096) + boost
    holders = jax.random.permutation(jax.random.fold_in(own_key, 3), rows)[jnp.arange(amount) % rows]
    lots = jnp.where(jnp.arange(rows)[:, None] == holders[None, :], 1 << 14, lots)
    score = lots * amount + jnp.arange(amount)
    return lax.top_k(score.astype(jnp.int32), top)[1].astype(jnp.int32)


def scatter_about(own_key, extent, width, most, cuts=(), kind=jnp.bfloat16):
    values = width * jax.random.normal(own_key, extent, jnp.float32)
    if cuts:
        values = values * levels(own_key, extent, cuts, -0.22, 0.18)
    return jnp.clip(values, -most, most).astype(kind)


def setup_inputs(seed: int = 0) -> dict:
    key_list = jax.random.split(jax.random.key(seed), 25)
    return {
        "hidden_in": scatter_about(key_list[0], (TOKEN_TOTAL, MODEL_DIMENSION), 1.0, 6.0, ((0, 32),)),
        "cotangent": scatter_about(key_list[1], (TOKEN_TOTAL, MODEL_DIMENSION), 1.0, 6.0, ((0, 32),)),
        "lengths": draw_lengths(jax.random.fold_in(key_list[24], 71), 0),
        "routes": distinct(key_list[3], TOKEN_TOTAL, EXPERTS, TOP, 1024),
        "gate_values": jnp.clip(0.05 + 0.2 * jax.random.uniform(key_list[4], (TOKEN_TOTAL, TOP), jnp.float32) ** levels(key_list[4], (TOKEN_TOTAL, TOP), ((0, 32),), -0.2, 0.2), 0.05, 0.25),
        "pair_order": jax.vmap(lambda own: jax.random.permutation(own, TOK_DEV * TOP))(jax.random.split(key_list[5], (N_DP * N_TENSOR))).reshape((N_DP * N_TENSOR, TOK_DEV * TOP)).astype(jnp.int32),
        "query_weight": scatter_about(key_list[6], (MODEL_DIMENSION, QUERY_HEADS * HEAD_SIZE), MODEL_DIMENSION ** -0.5, 0.15625, ((0, 8), (1, 4)), jnp.float32),
        "keyvalue_matrix": scatter_about(key_list[7], (2, MODEL_DIMENSION, KEYVALUE_HEADS * HEAD_SIZE), MODEL_DIMENSION ** -0.5, 0.15625, ((1, 8), (2, 4)), jnp.float32),
        "outproj_weight": scatter_about(key_list[8], (QUERY_HEADS * HEAD_SIZE, MODEL_DIMENSION), (QUERY_HEADS * HEAD_SIZE * 8 // SEQUENCE_SLOTS) ** -0.5, 1.75, ((0, 4), (1, 8)), jnp.float32),
        "norm_gains": jnp.clip(1.0 + 0.1 * jax.random.normal(key_list[9], (2, MODEL_DIMENSION), jnp.float32), 0.5, 1.5),
        "upgate_weight": scatter_about(key_list[10], (2, EXPERTS, MODEL_DIMENSION, FF), MODEL_DIMENSION ** -0.5, 0.15625, ((1, 8), (3, 4)), jnp.float32),
        "downproj_weight": scatter_about(key_list[11], (EXPERTS, FF, MODEL_DIMENSION), FF ** -0.5, 0.25, ((0, 8), (1, 4)), jnp.float32),
        "query_mean": scatter_about(key_list[12], (MODEL_DIMENSION, QUERY_HEADS * HEAD_SIZE), (0.055 * TOKEN_TOTAL ** 0.5), 32.0, ((0, 8), (1, 4)), jnp.float32),
        "query_sqmean": jnp.clip(jnp.exp(math.log(229.376) - 1.5404451 * jax.random.uniform(key_list[13], (MODEL_DIMENSION, QUERY_HEADS * HEAD_SIZE), jnp.float32) ** levels(key_list[13], (MODEL_DIMENSION, QUERY_HEADS * HEAD_SIZE), ((0, 8), (1, 4)), -0.2, 0.2)), 49.152, 229.376),
        "keyvalue_first_moment": scatter_about(key_list[14], (2, MODEL_DIMENSION, KEYVALUE_HEADS * HEAD_SIZE), (0.055 * TOKEN_TOTAL ** 0.5), 32.0, ((1, 8), (2, 4)), jnp.float32),
        "keyvalue_second_moment": jnp.clip(jnp.exp(math.log(229.376) - 1.5404451 * jax.random.uniform(key_list[15], (2, MODEL_DIMENSION, KEYVALUE_HEADS * HEAD_SIZE), jnp.float32) ** levels(key_list[15], (2, MODEL_DIMENSION, KEYVALUE_HEADS * HEAD_SIZE), ((1, 8), (2, 4)), -0.2, 0.2)), 49.152, 229.376),
        "outproj_mean": scatter_about(key_list[16], (QUERY_HEADS * HEAD_SIZE, MODEL_DIMENSION), (0.0055 * TOKEN_TOTAL ** 0.5), 3.0, ((0, 4), (1, 8)), jnp.float32),
        "outproj_sqmean": jnp.clip(jnp.exp(math.log(2.29376) - 1.5404451 * jax.random.uniform(key_list[17], (QUERY_HEADS * HEAD_SIZE, MODEL_DIMENSION), jnp.float32) ** levels(key_list[17], (QUERY_HEADS * HEAD_SIZE, MODEL_DIMENSION), ((0, 4), (1, 8)), -0.2, 0.2)), 0.49152, 2.29376),
        "gains_mean": scatter_about(key_list[18], (2, MODEL_DIMENSION), (0.055 * TOKEN_TOTAL ** 0.5), 32.0, ((1, 8),), jnp.float32),
        "gains_sqmean": jnp.clip(jnp.exp(math.log(229.376) - 1.5404451 * jax.random.uniform(key_list[19], (2, MODEL_DIMENSION), jnp.float32) ** levels(key_list[19], (2, MODEL_DIMENSION), ((1, 8),), -0.2, 0.2)), 49.152, 229.376),
        "upgate_mean": scatter_about(key_list[20], (2, EXPERTS, MODEL_DIMENSION, FF), (0.011 * (TOKEN_TOTAL * TOP // EXPERTS) ** 0.5), 2.0, ((1, 8), (3, 4)), jnp.float32),
        "upgate_sqmean": jnp.clip(jnp.exp(math.log(1.1264) - 1.4816045 * jax.random.uniform(key_list[21], (2, EXPERTS, MODEL_DIMENSION, FF), jnp.float32) ** levels(key_list[21], (2, EXPERTS, MODEL_DIMENSION, FF), ((1, 8), (3, 4)), -0.2, 0.2)), 0.256, 1.1264),
        "downproj_mean": scatter_about(key_list[22], (EXPERTS, FF, MODEL_DIMENSION), (0.0077 * (TOKEN_TOTAL * TOP // EXPERTS) ** 0.5), 1.5, ((0, 8), (1, 4)), jnp.float32),
        "downproj_sqmean": jnp.clip(jnp.exp(math.log(0.55296) - 1.5040774 * jax.random.uniform(key_list[23], (EXPERTS, FF, MODEL_DIMENSION), jnp.float32) ** levels(key_list[23], (EXPERTS, FF, MODEL_DIMENSION), ((0, 8), (1, 4)), -0.2, 0.2)), 0.12288, 0.55296),
    }


NORM_EPS = 1e-05
ROPE_THETA = 10000.0
MASKED = -1e+30
BETA_ONE = 0.9
BETA_TWO = 0.95
LEARN_RATE = 0.03
WEIGHT_DECAY = 0.1
ADAM_EPS = 1e-08
FULL_PRECISION = lax.Precision.HIGHEST

@jax.custom_vjp
def low(v):
    return lax.optimization_barrier(v.astype(jnp.bfloat16)).astype(jnp.float32)

@jax.custom_vjp
def low_back(v):
    return v

def low_keep(v):
    return (low(v), None)

def low_pass(kept, grad):
    return (grad,)

def back_keep(v):
    return (v, None)

def back_low(kept, grad):
    return (low(grad),)
low.defvjp(low_keep, low_pass)
low_back.defvjp(back_keep, back_low)

def rope_tables(row_count):
    positions = (jnp.arange(row_count) % SEQUENCE_SLOTS).astype(jnp.float32)
    freqs = ROPE_THETA ** (-(2.0 * jnp.arange(HEAD_SIZE // 2).astype(jnp.float32)) / HEAD_SIZE)
    angles = positions[:, None] * freqs[None, :]
    return (jnp.cos(angles)[:, None, :], jnp.sin(angles)[:, None, :])

def rotate(values, cosine, sine_tab):
    half_dim = values.shape[-1] // 2
    first_half = values[..., :half_dim]
    second_half = values[..., half_dim:]
    return jnp.concatenate([first_half * cosine - second_half * sine_tab, second_half * cosine + first_half * sine_tab], axis=-1)

def slot_ranks(experts_flat, live_pairs, priority, expert_count):
    pair_count = experts_flat.shape[0]
    inverse = jnp.zeros((pair_count,), jnp.int32).at[priority].set(jnp.arange(pair_count, dtype=jnp.int32))
    sorted_expert = experts_flat[inverse]
    sorted_live = live_pairs[inverse]
    onehot_hits = ((sorted_expert[:, None] == jnp.arange(expert_count, dtype=jnp.int32)[None, :]) & sorted_live[:, None]).astype(jnp.int32)
    running = jnp.cumsum(onehot_hits, axis=0)
    rank_seq = lax.optimization_barrier(jnp.sum(running * onehot_hits, axis=1)) - 1
    return rank_seq[priority]

def adam_step(weight, gradient, first_old, second_old, decay_rate):
    first_new = BETA_ONE * first_old + (1.0 - BETA_ONE) * gradient
    second_new = BETA_TWO * second_old + (1.0 - BETA_TWO) * gradient * gradient
    first_hat = first_new / (1.0 - BETA_ONE ** ADAM_STEP)
    second_hat = second_new / (1.0 - BETA_TWO ** ADAM_STEP)
    update = -LEARN_RATE * (first_hat / (jnp.sqrt(second_hat) + ADAM_EPS) + decay_rate * weight)
    return (gradient, first_new, second_new, update)

def reference(hidden_in, cotangent, lengths, routes, gate_values, pair_order, query_weight, keyvalue_matrix, outproj_weight, norm_gains, upgate_weight, downproj_weight, query_mean, query_sqmean, keyvalue_first_moment, keyvalue_second_moment, outproj_mean, outproj_sqmean, gains_mean, gains_sqmean, upgate_mean, upgate_sqmean, downproj_mean, downproj_sqmean):
    device_count = N_DP * N_TENSOR
    pair_count = TOK_DEV * TOP
    slot_count = device_count * CAP
    token_ids = jnp.arange(TOKEN_TOTAL, dtype=jnp.int32)
    live_rows = token_ids % SEQUENCE_SLOTS < lengths[token_ids // SEQUENCE_SLOTS]
    live_pairs = jnp.repeat(live_rows, TOP).reshape(device_count, pair_count)
    expert_ids = routes.reshape(device_count, pair_count)
    slot_rank = jax.vmap(partial(slot_ranks, expert_count=EXPERTS))(expert_ids, live_pairs, pair_order)
    kept_pairs = live_pairs & (slot_rank < CAP)
    source_ids = jnp.arange(device_count, dtype=jnp.int32)[:, None]
    flat_slot = jnp.where(kept_pairs, expert_ids * slot_count + source_ids * CAP + slot_rank, EXPERTS * slot_count).reshape(-1)
    pair_ids = jnp.arange(TOKEN_TOTAL * TOP, dtype=jnp.int32)
    slot_token = jnp.full((EXPERTS * slot_count,), TOKEN_TOTAL, jnp.int32).at[flat_slot].set(pair_ids // TOP, mode='drop')
    slot_pair = jnp.full((EXPERTS * slot_count,), TOKEN_TOTAL * TOP, jnp.int32).at[flat_slot].set(pair_ids, mode='drop')
    cosine, sine_tab = rope_tables(TOKEN_TOTAL)
    proportion = QUERY_HEADS // KEYVALUE_HEADS

    def single_sequence(packed):
        seq_query, seq_key, seq_value, length = packed
        raw_scores = jnp.einsum('qhgd,khd->hgqk', seq_query, seq_key, precision=FULL_PRECISION)
        scores = low_back(raw_scores * HEAD_SIZE ** (-0.5))
        positions = jnp.arange(SEQUENCE_SLOTS)
        allowed = (positions[None, :] <= positions[:, None]) & (positions[None, :] < length)
        masked = jnp.where(allowed, scores, MASKED)
        shifted = jnp.exp(masked - lax.optimization_barrier(jnp.max(masked, axis=-1, keepdims=True)))
        attn_probs = shifted / lax.optimization_barrier(jnp.sum(shifted, axis=-1, keepdims=True))
        mixed_heads = jnp.einsum('hgqk,khd->qhgd', low(attn_probs), seq_value, precision=FULL_PRECISION)
        return low(low_back(mixed_heads)).reshape(SEQUENCE_SLOTS, QUERY_HEADS * HEAD_SIZE)

    def forward(inputs_f, query_w, keyval_w, outproj_w, gains_w, upgate_w, downproj_w, gates):
        query_low = low(query_w)
        keyvalue_reduced = low(keyval_w)
        outproj_low = low(outproj_w)
        gains_low = low(gains_w)
        upgate_low = low(upgate_w)
        downproj_low = low(downproj_w)
        rms_attn = lax.rsqrt(lax.optimization_barrier(jnp.mean(inputs_f * inputs_f, axis=-1, keepdims=True)) + NORM_EPS)
        normed_attn = inputs_f * rms_attn
        attention_input = low(normed_attn * gains_low[0])
        queries = low_back(jnp.dot(attention_input, query_low, precision=FULL_PRECISION)).reshape(TOKEN_TOTAL, QUERY_HEADS, HEAD_SIZE)
        unrotated_keys = low_back(jnp.dot(attention_input, keyvalue_reduced[0], precision=FULL_PRECISION)).reshape(TOKEN_TOTAL, KEYVALUE_HEADS, HEAD_SIZE)
        value_reduced = low(low_back(jnp.dot(attention_input, keyvalue_reduced[1], precision=FULL_PRECISION))).reshape(TOKEN_TOTAL, KEYVALUE_HEADS, HEAD_SIZE)
        rotated_queries = low(rotate(queries, cosine, sine_tab))
        rotated_keys = low(rotate(unrotated_keys, cosine, sine_tab))
        head_outputs = lax.map(jax.checkpoint(single_sequence), (rotated_queries.reshape(SEQUENCE_TOTAL, SEQUENCE_SLOTS, KEYVALUE_HEADS, proportion, HEAD_SIZE), rotated_keys.reshape(SEQUENCE_TOTAL, SEQUENCE_SLOTS, KEYVALUE_HEADS, HEAD_SIZE), value_reduced.reshape(SEQUENCE_TOTAL, SEQUENCE_SLOTS, KEYVALUE_HEADS, HEAD_SIZE), lengths))
        head_outputs = head_outputs.reshape(TOKEN_TOTAL, QUERY_HEADS * HEAD_SIZE)
        attn_out = low_back(jnp.dot(head_outputs, outproj_low, precision=FULL_PRECISION))
        middle = inputs_f + attn_out
        rms_moe = lax.rsqrt(lax.optimization_barrier(jnp.mean(middle * middle, axis=-1, keepdims=True)) + NORM_EPS)
        normed_moe = middle * rms_moe
        moe_in = low(normed_moe * gains_low[1])
        padded_in = jnp.concatenate([moe_in, jnp.zeros((1, MODEL_DIMENSION), jnp.float32)], axis=0)

        def one_expert(packed):
            gate_w, up_w, down_w, row_index = packed
            rows_in = low_back(padded_in[row_index])
            gate_pre = low_back(jnp.dot(rows_in, gate_w, precision=FULL_PRECISION))
            up_pre = low_back(jnp.dot(rows_in, up_w, precision=FULL_PRECISION))
            inner_act = low(jax.nn.silu(gate_pre) * up_pre)
            return low(low_back(jnp.dot(inner_act, down_w, precision=FULL_PRECISION)))
        expert_out = lax.map(jax.checkpoint(one_expert), (upgate_low[0], upgate_low[1], downproj_low, slot_token.reshape(EXPERTS, slot_count)))
        padded_gates = jnp.concatenate([gates.reshape(-1), jnp.zeros((1,), jnp.float32)])
        slot_weight = padded_gates[slot_pair]
        mixed = jnp.zeros((TOKEN_TOTAL, MODEL_DIMENSION), jnp.float32).at[slot_token].add(expert_out.reshape(-1, MODEL_DIMENSION) * slot_weight[:, None], mode='drop')
        return middle + mixed
    inputs_f = hidden_in.astype(jnp.float32)
    block_pre, backward = jax.vjp(forward, inputs_f, query_weight, keyvalue_matrix, outproj_weight, norm_gains, upgate_weight, downproj_weight, gate_values)
    seed_grad = cotangent.astype(jnp.float32) * live_rows[:, None].astype(jnp.float32)
    grads = backward(seed_grad)
    block_out = block_pre.astype(jnp.bfloat16)
    input_grad = grads[0]
    gate_grad = grads[7]
    query_grad, query_newmean, query_newsq, query_update = adam_step(query_weight, grads[1], query_mean, query_sqmean, WEIGHT_DECAY)
    keyval_grad, keyval_newmean, keyval_newsq, keyval_update = adam_step(keyvalue_matrix, grads[2], keyvalue_first_moment, keyvalue_second_moment, WEIGHT_DECAY)
    outproj_grad, outproj_newmean, outproj_newsq, outproj_update = adam_step(outproj_weight, grads[3], outproj_mean, outproj_sqmean, WEIGHT_DECAY)
    gains_grad, gains_newmean, gains_newsq, gains_update = adam_step(norm_gains, grads[4], gains_mean, gains_sqmean, 0.0)
    upgate_grad, upgate_newmean, upgate_newsq, upgate_update = adam_step(upgate_weight, grads[5], upgate_mean, upgate_sqmean, WEIGHT_DECAY)
    downproj_grad, downproj_newmean, downproj_newsq, downproj_update = adam_step(downproj_weight, grads[6], downproj_mean, downproj_sqmean, WEIGHT_DECAY)
    return (block_out, input_grad, gate_grad, query_grad, query_newmean, query_newsq, query_update, keyval_grad, keyval_newmean, keyval_newsq, keyval_update, outproj_grad, outproj_newmean, outproj_newsq, outproj_update, gains_grad, gains_newmean, gains_newsq, gains_update, upgate_grad, upgate_newmean, upgate_newsq, upgate_update, downproj_grad, downproj_newmean, downproj_newsq, downproj_update)
```

```python
import functools
import jax
import jax.numpy as jnp
from jax import lax
from jax.experimental import pallas as pl
from jax.experimental.pallas import tpu as pltpu
from jax.sharding import PartitionSpec as P

HEAD_SIZE = 64
TOP = 8
SEQUENCE_SLOTS = 1024
ADAM_STEP = 5
NORM_EPS = 1e-05
ROPE_THETA = 10000.0
MASKED = -1e30
BETA_ONE = 0.9
BETA_TWO = 0.95
LEARN_RATE = 0.03
WEIGHT_DECAY = 0.1
ADAM_EPS = 1e-08
BF = jnp.bfloat16
F32 = jnp.float32
BLOCK = 256
NN = (((1,), (0,)), ((), ()))
NT = (((1,), (1,)), ((), ()))
TN = (((0,), (0,)), ((), ()))


def mm(a, b, dims=NN):
    return lax.dot_general(a, b, dims, preferred_element_type=F32)


def params(mib=58):
    return pltpu.CompilerParams(vmem_limit_bytes=mib << 20)


def adam_step(weight, gradient, first_old, second_old, decay_rate):
    first_new = BETA_ONE * first_old + (1.0 - BETA_ONE) * gradient
    second_new = BETA_TWO * second_old + (1.0 - BETA_TWO) * gradient * gradient
    first_hat = first_new / (1.0 - BETA_ONE**ADAM_STEP)
    second_hat = second_new / (1.0 - BETA_TWO**ADAM_STEP)
    update = -LEARN_RATE * (first_hat / (jnp.sqrt(second_hat) + ADAM_EPS) + decay_rate * weight)
    return (gradient, first_new, second_new, update)


def rank_body(cap, ecol, ocol, erow, orow, out):
    pairs = erow.shape[1]
    step = 64
    er, orr = erow[...], orow[...]

    def chunk(i, acc):
        rows = pl.ds(i * step, step)
        hit = (ecol[rows, :] == er) & (ocol[rows, :] < orr)
        return acc + jnp.sum(hit.astype(jnp.int32), axis=0, keepdims=True)

    rank = lax.fori_loop(0, pairs // step, chunk, jnp.zeros((1, pairs), jnp.int32))
    kept = (orr < pairs) & (rank < cap)
    out[...] = jnp.where(kept, er * cap + rank, -1)


def slot_targets(experts, order, live_pairs, cap):
    pairs = experts.shape[0]
    order = jnp.where(live_pairs, order, pairs)
    return pl.pallas_call(
        functools.partial(rank_body, cap),
        out_shape=jax.ShapeDtypeStruct((1, pairs), jnp.int32),
        compiler_params=params(16),
        name="slot_targets",
    )(experts[:, None], order[:, None], experts[None, :], order[None, :])[0]


def swap_halves(u):
    width = u.shape[1]
    lane = lax.broadcasted_iota(jnp.int32, u.shape, 1) % HEAD_SIZE
    half = HEAD_SIZE // 2
    return jnp.where(lane < half, pltpu.roll(u, width - half, 1), pltpu.roll(u, half, 1))


def rope(u, cos, sin):
    reps = u.shape[1] // cos.shape[1]
    if reps > 1:
        cos = jnp.concatenate([cos] * reps, axis=1)
        sin = jnp.concatenate([sin] * reps, axis=1)
    return u * cos + swap_halves(u) * sin


def rope_lanes(rows):
    lane = jnp.arange(128) % HEAD_SIZE
    half = HEAD_SIZE // 2
    positions = (jnp.arange(rows) % SEQUENCE_SLOTS).astype(F32)
    freqs = ROPE_THETA ** (-(2.0 * (lane % half).astype(F32)) / HEAD_SIZE)
    angles = positions[:, None] * freqs[None, :]
    return jnp.cos(angles), jnp.where(lane < half, -1.0, 1.0) * jnp.sin(angles)


ANY = pl.BlockSpec(memory_space=pltpu.HBM)


def cost(flops, nbytes):
    return pl.CostEstimate(flops=int(flops), bytes_accessed=int(nbytes), transcendentals=0)


def qkv_body(qw, kw, xn, wn, at, *refs):
    xs, ws, refs = refs[:xn], refs[xn : xn + wn], refs[xn + wn :]
    cos, sin, a_out, q_out, k_out, v_out, gains, w_out, x_scr, sem = refs
    step = ws[0].shape[0]
    copies = []
    for i, ref in enumerate(ws):
        rows = pl.ds(pl.multiple_of(at[xn + i] * step, 16), step)
        copies.append(pltpu.make_async_copy(ref, w_out.at[rows, :], sem.at[xn + i]))
    for i, ref in enumerate(xs):
        rows = pl.ds(pl.multiple_of(at[i] * BLOCK, BLOCK), BLOCK)
        copies.append(pltpu.make_async_copy(ref, x_scr.at[rows, :], sem.at[i]))
    for c in copies:
        c.start()
    for c in copies:
        c.wait()
    wide = qw + 2 * kw
    gains[...] = w_out[:, wide + qw :].astype(F32).T[0:8, :]

    def block(i, _):
        rows = pl.ds(pl.multiple_of(i * BLOCK, BLOCK), BLOCK)
        v = x_scr[rows, :].astype(F32)
        r = lax.rsqrt(jnp.mean(v * v, axis=-1, keepdims=True) + NORM_EPS)
        a = (v * r * gains[0:1, :]).astype(BF)
        a_out[rows, :] = a
        y = mm(a, w_out[:, :wide])
        c, s = cos[rows, :], sin[rows, :]
        q_out[rows, :] = rope(y[:, :qw], c, s).astype(BF)
        k_out[rows, :] = rope(y[:, qw : qw + kw], c, s).astype(BF)
        v_out[rows, :] = y[:, qw + kw :].astype(BF)
        return 0

    lax.fori_loop(0, len(xs), block, 0)


def qkv(at, xs, ws, qw, kw, cos, sin):
    rows, width = BLOCK * len(xs), xs[0].shape[1]
    cols = ws[0].shape[1]
    depth = ws[0].shape[0] * len(ws)
    vm = pl.BlockSpec(memory_space=pltpu.VMEM)
    return pl.pallas_call(
        functools.partial(qkv_body, qw, kw, len(xs), len(ws)),
        in_specs=[pl.BlockSpec(memory_space=pltpu.SMEM)]
        + [ANY] * (len(xs) + len(ws))
        + [vm, vm],
        out_specs=[vm] * 6,
        out_shape=[
            jax.ShapeDtypeStruct((rows, width), BF),
            jax.ShapeDtypeStruct((rows, qw), BF),
            jax.ShapeDtypeStruct((rows, kw), BF),
            jax.ShapeDtypeStruct((rows, kw), BF),
            jax.ShapeDtypeStruct((8, width), F32),
            jax.ShapeDtypeStruct((depth, cols), BF),
        ],
        scratch_shapes=[
            pltpu.VMEM((rows, width), BF),
            pltpu.SemaphoreType.DMA((len(xs) + len(ws),)),
        ],
        compiler_params=params(32),
        cost_estimate=cost(2 * rows * width * cols, 2e7),
        name="qkv",
    )(at, *xs, *ws, cos, sin)


def project_body(cols, at, v, w, far, near):
    def block(i, _):
        for j, out in ((2, far), (0, near)):
            rows = pl.ds(pl.multiple_of(at[j + i] * BLOCK, BLOCK), BLOCK)
            out[i] = mm(v[rows, :], w[:, cols[0] : cols[1]], NT).astype(BF)
        return 0

    lax.fori_loop(0, 2, block, 0)


def project(at, v, w, cols):
    rows, depth = v.shape
    width = w.shape[0]
    vm = pl.BlockSpec(memory_space=pltpu.VMEM)
    return pl.pallas_call(
        functools.partial(project_body, cols),
        in_specs=[pl.BlockSpec(memory_space=pltpu.SMEM), vm, vm],
        out_specs=[vm] * 2,
        out_shape=[jax.ShapeDtypeStruct((2, BLOCK, width), BF)] * 2,
        compiler_params=params(32),
        cost_estimate=cost(2 * rows * depth * width, 1e7),
        name="project",
    )(at, v, w)


def heads_back_body(cols, at, m0, m1, m2, m3, w, h_out, m_out, sem):
    copies = []
    for i, ref in enumerate((m0, m1, m2, m3)):
        rows = pl.ds(pl.multiple_of(at[i] * BLOCK, BLOCK), BLOCK)
        copies.append(pltpu.make_async_copy(ref, m_out.at[rows, :], sem.at[i]))
    for c in copies:
        c.start()
    for c in copies:
        c.wait()

    def block(i, _):
        rows = pl.ds(pl.multiple_of(i * BLOCK, BLOCK), BLOCK)
        h_out[rows, :] = mm(m_out[rows, :], w[:, cols[0] : cols[1]]).astype(BF)
        return 0

    lax.fori_loop(0, 4, block, 0)


def heads_back(at, ms, w, cols):
    width, qw = w.shape[0], cols[1] - cols[0]
    rows = 4 * BLOCK
    vm = pl.BlockSpec(memory_space=pltpu.VMEM)
    return pl.pallas_call(
        functools.partial(heads_back_body, cols),
        in_specs=[pl.BlockSpec(memory_space=pltpu.SMEM)] + [ANY] * 4 + [vm],
        out_specs=[vm, vm],
        out_shape=[
            jax.ShapeDtypeStruct((rows, qw), BF),
            jax.ShapeDtypeStruct((rows, width), BF),
        ],
        scratch_shapes=[pltpu.SemaphoreType.DMA((4,))],
        compiler_params=params(32),
        cost_estimate=cost(2 * rows * qw * width, 1e7),
        name="heads_back",
    )(at, *ms, w)


def spread(pair_lanes, out):
    lane = lax.broadcasted_iota(jnp.int32, pair_lanes.shape, 1)
    full = pair_lanes.astype(F32)
    first = jnp.where(lane < HEAD_SIZE, full, 0.0)
    second = jnp.where(lane < HEAD_SIZE, 0.0, full)
    out[0] = first.astype(BF)
    out[1] = pltpu.roll(first, HEAD_SIZE, 1).astype(BF)
    out[2] = pltpu.roll(second, HEAD_SIZE, 1).astype(BF)
    out[3] = second.astype(BF)


def attend_body(share, length, q, k, v, o, lse, ks, vs):
    pair, qb = pl.program_id(0), pl.program_id(1)

    @pl.when((pair == 0) & (qb == 0))
    def _():
        spread(k[...], ks)
        spread(v[...], vs)

    scale = HEAD_SIZE**-0.5
    for j in range(SEQUENCE_SLOTS // BLOCK):

        @pl.when(qb == j)
        def _():
            keys = (j + 1) * BLOCK
            kpos = lax.broadcasted_iota(jnp.int32, (BLOCK, keys), 1)
            qpos = lax.broadcasted_iota(jnp.int32, (BLOCK, keys), 0) + j * BLOCK
            allowed = (kpos <= qpos) & (kpos < length[0])
            total = jnp.zeros((BLOCK, 128), F32)
            for u in range(2):
                which = 2 * ((2 * pair + u) // share) + u
                s = mm(q[...], ks[which, :keys, :], NT) * scale
                s = jnp.where(allowed, s, MASKED)
                top = jnp.max(s, axis=-1, keepdims=True)
                e = jnp.exp(s - top)
                den = jnp.sum(e, axis=-1, keepdims=True)
                total += mm(e.astype(BF), vs[which, :keys, :]) / den
                full = jnp.broadcast_to(top + jnp.log(den), (BLOCK, 128))
                lse[0, u : u + 1, :] = full.T[0:1, :]
            o[...] = total.astype(BF)


def attend(length, q, k, v, share):
    rows, qw = q.shape
    kw = k.shape[1]
    assert kw == 128 and rows == SEQUENCE_SLOTS
    pairs = qw // 128
    blocks = rows // BLOCK
    fix = lambda p, b, n: (0, 0)
    return pl.pallas_call(
        functools.partial(attend_body, share),
        grid_spec=pltpu.PrefetchScalarGridSpec(
            num_scalar_prefetch=1,
            grid=(pairs, blocks),
            in_specs=[
                pl.BlockSpec((BLOCK, 128), lambda p, b, n: (b, p)),
                pl.BlockSpec((rows, kw), fix),
                pl.BlockSpec((rows, kw), fix),
            ],
            out_specs=[
                pl.BlockSpec((BLOCK, 128), lambda p, b, n: (b, p)),
                pl.BlockSpec((1, 8, BLOCK), lambda p, b, n: (p, 0, b)),
            ],
            scratch_shapes=[pltpu.VMEM((4, rows, 128), BF), pltpu.VMEM((4, rows, 128), BF)],
        ),
        out_shape=[
            jax.ShapeDtypeStruct((rows, qw), BF),
            jax.ShapeDtypeStruct((pairs, 8, rows), F32),
        ],
        compiler_params=params(32),
        name="attend",
    )(length, q, k, v)


def attend_back_body(
    share, length, q, k, v, o, do, lse, cos, sin, coskv, sinkv, dq, dk, dv, ks, vs, kt, dka, dva
):
    pair, qb = pl.program_id(0), pl.program_id(1)
    scale = HEAD_SIZE**-0.5

    @pl.when((pair == 0) & (qb == 0))
    def _():
        spread(k[...], ks)
        spread(v[...], vs)
        for i in range(4):
            kt[i] = ks[i].astype(F32).T.astype(BF)
        dka[...] = jnp.zeros_like(dka)
        dva[...] = jnp.zeros_like(dva)

    live = length[0]

    @pl.when(qb * BLOCK >= live)
    def _():
        dq[...] = jnp.zeros_like(dq)

    @pl.when(qb * BLOCK < live)
    def _():
        qt, dot_ = q[...], do[...]
        lane = lax.broadcasted_iota(jnp.int32, (BLOCK, 128), 1)
        both = (dot_.astype(F32) * o[...].astype(F32)).T
        zero = jnp.zeros((), BF)
        mine = [lane < HEAD_SIZE, lane >= HEAD_SIZE]
        qm = [jnp.where(m, qt, zero) for m in mine]
        dm = [jnp.where(m, dot_, zero) for m in mine]
        delta = [
            jnp.sum(both[:HEAD_SIZE], axis=0, keepdims=True),
            jnp.sum(both[HEAD_SIZE:], axis=0, keepdims=True),
        ]

        def step(kb, acc):
            rows = pl.ds(pl.multiple_of(kb * BLOCK, BLOCK), BLOCK)
            kpos = lax.broadcasted_iota(jnp.int32, (BLOCK, BLOCK), 0) + kb * BLOCK
            qpos = lax.broadcasted_iota(jnp.int32, (BLOCK, BLOCK), 1) + qb * BLOCK
            allowed = (kpos <= qpos) & (kpos < live)
            for u in range(2):
                g = (2 * pair + u) // share
                which = 2 * g + u
                st = mm(ks[which, rows, :], qt, NT) * scale
                pt = jnp.where(allowed, jnp.exp(st - lse[0, u : u + 1, :]), 0.0)
                dpt = mm(vs[which, rows, :], dot_, NT)
                dst = (pt * (dpt - delta[u])).astype(BF)
                dka[g, rows, :] += mm(dst, qm[u])
                dva[g, rows, :] += mm(pt.astype(BF), dm[u])
                acc += mm(kt[which, :, rows], dst)
            return acc

        last = jnp.minimum(qb + 1, (live + BLOCK - 1) // BLOCK)
        acc = lax.fori_loop(0, last, step, jnp.zeros((128, BLOCK), F32))
        dq[...] = rope(acc.T * scale, cos[...], -sin[...]).astype(BF)

    @pl.when((pair == pl.num_programs(0) - 1) & (qb == pl.num_programs(1) - 1))
    def _():
        lane = lax.broadcasted_iota(jnp.int32, (SEQUENCE_SLOTS, 128), 1)

        def joined(acc):
            both = [acc[g] + pltpu.roll(acc[g], HEAD_SIZE, 1) for g in range(2)]
            return jnp.where(lane < HEAD_SIZE, both[0], both[1])

        dk[...] = rope(joined(dka) * scale, coskv[...], -sinkv[...]).astype(BF)
        dv[...] = joined(dva).astype(BF)


def attend_back(length, q, k, v, o, do, lse, cos, sin, share):
    rows, qw = q.shape
    kw = k.shape[1]
    pairs, blocks = qw // 128, rows // BLOCK
    fix = lambda p, b, n: (0, 0)
    tile = pl.BlockSpec((BLOCK, 128), lambda p, b, n: (b, p))
    whole = pl.BlockSpec((rows, kw), fix)
    part = pl.BlockSpec((BLOCK, 128), lambda p, b, n: (b, 0))
    return pl.pallas_call(
        functools.partial(attend_back_body, share),
        grid_spec=pltpu.PrefetchScalarGridSpec(
            num_scalar_prefetch=1,
            grid=(pairs, blocks),
            in_specs=[
                tile,
                whole,
                whole,
                tile,
                tile,
                pl.BlockSpec((1, 8, BLOCK), lambda p, b, n: (p, 0, b)),
                part,
                part,
                whole,
                whole,
            ],
            out_specs=[tile, whole, whole],
            scratch_shapes=[
                pltpu.VMEM((4, rows, 128), BF),
                pltpu.VMEM((4, rows, 128), BF),
                pltpu.VMEM((4, 128, rows), BF),
                pltpu.VMEM((2, rows, 128), F32),
                pltpu.VMEM((2, rows, 128), F32),
            ],
        ),
        out_shape=[
            jax.ShapeDtypeStruct((rows, qw), BF),
            jax.ShapeDtypeStruct((rows, kw), BF),
            jax.ShapeDtypeStruct((rows, kw), BF),
        ],
        compiler_params=params(32),
        name="attend_back",
    )(length, q, k, v, o, do, lse, cos, sin, cos, sin)


NB = 8


def local_slots(table, first, local):
    at = (lax.broadcasted_iota(jnp.int32, (local, BLOCK), 0) + first).astype(F32)
    slot = jnp.full((local, BLOCK), -1.0, F32)
    gate = jnp.zeros((local, BLOCK), F32)
    for k in range(TOP):
        row = table[k : k + 1, :]
        here = row[:, :BLOCK] == at
        slot = jnp.where(here, row[:, BLOCK : 2 * BLOCK], slot)
        gate = jnp.where(here, row[:, 2 * BLOCK : 3 * BLOCK] + row[:, 3 * BLOCK :], gate)
    return slot, gate


def one_hot(slot, cap):
    at = lax.broadcasted_iota(jnp.int32, (cap, BLOCK), 0).astype(F32)
    return jnp.concatenate(
        [jnp.where(at == slot[e : e + 1, :], 1.0, 0.0) for e in range(slot.shape[0])], axis=0
    )


def load_plane(own, sib, buf, sem):
    return [
        pltpu.make_async_copy(
            ref.at[n % 4, pl.ds(0, BLOCK), :], buf.at[n], sem.at[n]
        )
        for n in range(NB)
        for ref in (own if n < 4 else sib,)
    ]


def gather_pair(i, buf, hots, out, local, cap):
    width = buf.shape[2]
    cut = width // 3
    rows = pl.ds(pl.multiple_of(i * 2 * cap, 16), 2 * cap)
    for c in range(3):
        cols = slice(c * cut, (c + 1) * cut)
        got = [mm(hots[j], buf[2 * i + j, :, cols]) for j in range(2)]
        for e in range(local):
            mine = [g[e * cap : (e + 1) * cap, :] for g in got]
            out[e, rows, cols] = jnp.concatenate(mine, axis=0).astype(BF)


def seed_body(cap, plane, fresh, first, own, sib, *refs):
    down = refs[0]
    s_out, u_out, tab, buf, s_scr, d_scr, t_scr, sem, t_sem = refs[1 if fresh else 2 :]
    local = d_scr.shape[0]
    copies = load_plane(own, sib, buf, sem)
    for n in range(NB):
        ref = (own if n < 4 else sib).at[n % 4, pl.ds(BLOCK, TOP), :]
        copies.append(pltpu.make_async_copy(ref, t_scr.at[n], t_sem.at[n]))
    weights = pltpu.make_async_copy(down, d_scr, sem.at[NB + 2])
    for c in copies:
        c.start()
    weights.start()
    for c in copies:
        c.wait()
    for n in range(NB):
        tab[n] = t_scr[n, :, : 4 * BLOCK].astype(F32)

    def gather(i, _):
        hots = []
        for j in range(2):
            slot, _g = local_slots(tab[2 * i + j], first[0], local)
            hots.append(one_hot(slot, cap).astype(BF))
        gather_pair(i, buf, hots, s_scr, local, cap)
        return 0

    lax.fori_loop(0, NB // 2, gather, 0, unroll=2)
    rows = NB * cap
    keep = pltpu.make_async_copy(s_scr, s_out.at[:, pl.ds(plane * rows, rows), :], sem.at[NB + 3])
    keep.start()
    weights.wait()

    def expert(e, _):
        u_out[e] = mm(s_scr[e], d_scr[e], NT)
        return 0

    lax.fori_loop(0, local, expert, 0, unroll=4 if local % 4 == 0 else 1)
    keep.wait()


def seed_rows(plane, planes, first, own, sib, down, kept, cap):
    local, hidden, width = down.shape
    rows = NB * cap
    vm = pl.BlockSpec(memory_space=pltpu.VMEM)
    smem = pl.BlockSpec(memory_space=pltpu.SMEM)
    fresh = kept is None
    more = () if fresh else (kept,)
    return pl.pallas_call(
        functools.partial(seed_body, cap, plane, fresh),
        in_specs=[smem] + [ANY] * (3 + len(more)),
        out_specs=[ANY, vm, vm],
        out_shape=[
            jax.ShapeDtypeStruct((local, planes * rows, width), BF),
            jax.ShapeDtypeStruct((local, rows, hidden), F32),
            jax.ShapeDtypeStruct((NB, TOP, 4 * BLOCK), F32),
        ],
        scratch_shapes=[
            pltpu.VMEM((NB, BLOCK, width), BF),
            pltpu.VMEM((local, rows, width), BF),
            pltpu.VMEM((local, hidden, width), BF),
            pltpu.VMEM((NB, TOP, width), BF),
            pltpu.SemaphoreType.DMA((NB + 4,)),
            pltpu.SemaphoreType.DMA((NB,)),
        ],
        input_output_aliases={} if fresh else {4: 0},
        compiler_params=params(50),
        cost_estimate=cost(2 * rows * local * (BLOCK + hidden) * width, 2e7),
        name="seed_rows",
    )(first, own, sib, down, *more)


def main_body(cap, plane, fresh, first, tab, u, own_in, sib_in, *refs):
    wgu = refs[0]
    refs = refs[1 if fresh else 4 :]
    x_out, d_out, a_out, own, sib = refs[:5]
    buf, x_scr, w_scr, z_scr, p_scr, g_scr, r_scr, d_scr, a_scr, m_scr, sem, out_sem = refs[5:]
    local, hidden = a_scr.shape[0], a_scr.shape[2]
    rows = NB * cap
    slots = local * cap
    copies = load_plane(own_in, sib_in, buf, sem)
    weights = pltpu.make_async_copy(wgu, w_scr, sem.at[NB + 2])
    for c in copies:
        c.start()
    weights.start()
    for c in copies:
        c.wait()

    def gather(i, _):
        hots = []
        for j in range(2):
            b = 2 * i + j
            slot, gate = local_slots(tab[b], first[0], local)
            hot = one_hot(slot, cap)
            spread_gate = jnp.concatenate(
                [jnp.broadcast_to(gate[e : e + 1, :], (cap, BLOCK)) for e in range(local)], axis=0
            )
            weight = jnp.sum(hot * spread_gate, axis=1, keepdims=True)
            weight = jnp.broadcast_to(weight, (slots, hidden))
            for e in range(local):
                g_scr[e, pl.ds(b * cap, cap), :] = weight[e * cap : (e + 1) * cap, :]
            hots.append(hot.astype(BF))
            p_scr[b] = hots[-1]
        gather_pair(i, buf, hots, x_scr, local, cap)
        return 0

    lax.fori_loop(0, NB // 2, gather, 0, unroll=2)
    here = pl.ds(plane * rows, rows)
    keep_x = pltpu.make_async_copy(x_scr, x_out.at[:, here, :], sem.at[NB + 3])
    keep_x.start()
    weights.wait()

    def expert(e, _):
        gu = mm(x_scr[e], w_scr[e])
        gate, up = gu[:, :hidden], gu[:, hidden:]
        sig = 1.0 / (1.0 + jnp.exp(-gate))
        silu = gate * sig
        act = (silu * up).astype(BF).astype(F32)
        ue = u[e]
        w = g_scr[e]
        inner = w * ue
        dg = inner * up * sig * (1.0 + gate * (1.0 - sig))
        d = jnp.concatenate([dg, inner * silu], axis=1).astype(BF)
        d_scr[e] = d
        a_scr[e] = (act * w).astype(BF)
        r_scr[e] = act * ue
        z_scr[e] = mm(d, w_scr[e], NT)
        return 0

    lax.fori_loop(0, local, expert, 0, unroll=4 if local % 4 == 0 else 1)
    keep_d = pltpu.make_async_copy(d_scr, d_out.at[:, here, :], sem.at[NB + 4])
    keep_a = pltpu.make_async_copy(a_scr, a_out.at[:, here, :], sem.at[NB + 5])
    keep_d.start()
    keep_a.start()

    for half, out in ((1, sib), (0, own)):

        def combine(i, _):
            b = 4 * half + i
            at = pl.ds(b * cap, cap)
            zb = z_scr[:, at, :].reshape(slots, -1).astype(BF)
            m_scr[b, :BLOCK, :] = mm(p_scr[b], zb, TN).astype(BF)
            pair = jnp.sum(r_scr[:, at, :].reshape(slots, hidden), axis=1, keepdims=True)
            hot = p_scr[b].astype(F32) * pair
            per = jnp.concatenate(
                [
                    jnp.sum(hot[e * cap : (e + 1) * cap, :], axis=0, keepdims=True)
                    for e in range(local)
                ],
                axis=0,
            )
            ids = (lax.broadcasted_iota(jnp.int32, (local, BLOCK), 0) + first[0]).astype(F32)
            pairs = []
            for k in range(TOP):
                mine = tab[b, k : k + 1, :BLOCK] == ids
                pairs.append(jnp.sum(jnp.where(mine, per, 0.0), axis=0, keepdims=True))
            tail = jnp.zeros((TOP, m_scr.shape[2] - BLOCK), F32)
            pairs = jnp.concatenate([jnp.concatenate(pairs, axis=0), tail], axis=1)
            m_scr[b, BLOCK:, :] = pairs.astype(BF)
            pltpu.make_async_copy(m_scr.at[b], out.at[i], out_sem.at[b]).start()
            return 0

        lax.fori_loop(0, 4, combine, 0, unroll=2)
    for half, out in ((1, sib), (0, own)):
        for i in range(4):
            b = 4 * half + i
            pltpu.make_async_copy(m_scr.at[b], out.at[i], out_sem.at[b]).wait()
    keep_x.wait()
    keep_d.wait()
    keep_a.wait()


def expert_rows(plane, planes, first, tab, u, own, sib, wgu, kept, cap):
    local, width, two = wgu.shape
    hidden = two // 2
    rows = NB * cap
    vm = pl.BlockSpec(memory_space=pltpu.VMEM)
    smem = pl.BlockSpec(memory_space=pltpu.SMEM)
    fresh = kept is None
    more = () if fresh else tuple(kept)
    total = planes * rows
    return pl.pallas_call(
        functools.partial(main_body, cap, plane, fresh),
        in_specs=[smem, vm, vm] + [ANY] * (3 + len(more)),
        out_specs=[ANY] * 5,
        out_shape=[
            jax.ShapeDtypeStruct((local, total, width), BF),
            jax.ShapeDtypeStruct((local, total, two), BF),
            jax.ShapeDtypeStruct((local, total, hidden), BF),
            jax.ShapeDtypeStruct((4, BLOCK + TOP, width), BF),
            jax.ShapeDtypeStruct((4, BLOCK + TOP, width), BF),
        ],
        scratch_shapes=[
            pltpu.VMEM((NB, BLOCK, width), BF),
            pltpu.VMEM((local, rows, width), BF),
            pltpu.VMEM((local, width, two), BF),
            pltpu.VMEM((local, rows, width), F32),
            pltpu.VMEM((NB, local * cap, BLOCK), BF),
            pltpu.VMEM((local, rows, hidden), F32),
            pltpu.VMEM((local, rows, hidden), F32),
            pltpu.VMEM((local, rows, two), BF),
            pltpu.VMEM((local, rows, hidden), BF),
            pltpu.VMEM((NB, BLOCK + TOP, width), BF),
            pltpu.SemaphoreType.DMA((NB + 6,)),
            pltpu.SemaphoreType.DMA((NB,)),
        ],
        input_output_aliases={} if fresh else {6: 0, 7: 1, 8: 2},
        compiler_params=params(60),
        cost_estimate=cost(2 * rows * local * (2 * BLOCK + 2 * two) * width, 3e7),
        name="expert_rows",
    )(first, tab, u, own, sib, wgu, *more)


def mix_body(cap, plane, first, tab, a, down, own, sib, y_scr, m_scr, a_scr, sem, out_sem):
    local = down.shape[0]
    slots = local * cap
    rows = NB * cap
    load = pltpu.make_async_copy(a.at[:, pl.ds(plane * rows, rows), :], a_scr, sem)
    load.start()
    load.wait()

    def expert(e, _):
        y_scr[e] = mm(a_scr[e], down[e])
        return 0

    lax.fori_loop(0, local, expert, 0, unroll=4 if local % 4 == 0 else 1)
    for half, out in ((1, sib), (0, own)):

        def combine(i, _):
            b = 4 * half + i
            slot, _g = local_slots(tab[b], first[0], local)
            hot = one_hot(slot, cap).astype(BF)
            yb = y_scr[:, pl.ds(b * cap, cap), :].reshape(slots, -1).astype(BF)
            m_scr[b] = mm(hot, yb, TN).astype(BF)
            pltpu.make_async_copy(m_scr.at[b], out.at[i], out_sem.at[b]).start()
            return 0

        lax.fori_loop(0, 4, combine, 0, unroll=2)
    for half, out in ((1, sib), (0, own)):
        for i in range(4):
            b = 4 * half + i
            pltpu.make_async_copy(m_scr.at[b], out.at[i], out_sem.at[b]).wait()


def mix_rows(plane, first, tab, a, down, cap):
    local, hidden, width = down.shape
    rows = NB * cap
    vm = pl.BlockSpec(memory_space=pltpu.VMEM)
    return pl.pallas_call(
        functools.partial(mix_body, cap, plane),
        in_specs=[pl.BlockSpec(memory_space=pltpu.SMEM), vm, ANY, vm],
        out_specs=[ANY, ANY],
        out_shape=[jax.ShapeDtypeStruct((4, BLOCK, width), BF)] * 2,
        scratch_shapes=[
            pltpu.VMEM((local, rows, width), F32),
            pltpu.VMEM((NB, BLOCK, width), BF),
            pltpu.VMEM((local, rows, hidden), BF),
            pltpu.SemaphoreType.DMA(()),
            pltpu.SemaphoreType.DMA((NB,)),
        ],
        compiler_params=params(50),
        cost_estimate=cost(2 * rows * local * (BLOCK + hidden) * width, 2e7),
        name="mix_rows",
    )(first, tab, a, down)


def weights_body(older, turn, x, s, d, a, *refs):
    hidden = a.shape[2]
    ins, outs = refs[:6], refs[6 + older :]
    done = outs[-1]
    done[0] = turn[0]
    dgu = mm(d[0], x[0], TN).T
    for part in range(2):
        grad = dgu[:, part * hidden : (part + 1) * hidden]
        w, mean, sq = (r[part, 0] for r in ins[:3])
        for ref, val in zip(outs[:4], adam_step(w, grad, mean, sq, WEIGHT_DECAY)):
            ref[part, 0] = val
    ddown = mm(a[0], s[0], TN)
    w, mean, sq = (r[0] for r in ins[3:6])
    for ref, val in zip(outs[4:8], adam_step(w, ddown, mean, sq, WEIGHT_DECAY)):
        ref[0] = val


def weights_step(turn, begin, count, x, s, d, a, up, down, older, cuts=2):
    local, rows, width = x.shape
    hidden = a.shape[2]
    part = width // cuts
    wide = pl.BlockSpec((1, rows, part), lambda e, j: (e + begin, 0, j))
    slim = lambda n: pl.BlockSpec((1, rows, n), lambda e, j: (e + begin, 0, 0))
    ups = pl.BlockSpec((2, 1, part, hidden), lambda e, j: (0, e + begin, j, 0))
    downs = pl.BlockSpec((1, hidden, part), lambda e, j: (e + begin, 0, j))
    smem = pl.BlockSpec(memory_space=pltpu.SMEM)
    out = pl.pallas_call(
        functools.partial(weights_body, len(older)),
        grid=(count, cuts),
        in_specs=[smem, wide, wide, slim(2 * hidden), slim(hidden)]
        + [ups] * 3
        + [downs] * 3
        + [ANY] * len(older),
        out_specs=[ups] * 4 + [downs] * 4 + [smem],
        out_shape=[jax.ShapeDtypeStruct(up[0].shape, F32)] * 4
        + [jax.ShapeDtypeStruct(down[0].shape, F32)] * 4
        + [jax.ShapeDtypeStruct((1,), jnp.int32)],
        input_output_aliases={11 + i: i for i in range(len(older))},
        compiler_params=params(),
        cost_estimate=cost(2 * count * rows * width * 3 * hidden, 26e6 * count),
        name="weights_step",
    )(turn, x, s, d, a, *up, *down, *older)
    return list(out[:8]), out[8]


def experts_by_slot(
    moe_in, cotangent, live_rows, target, gate_values, lengths, up, down, capacity, data_size
):
    tensor_size = lax.axis_size("tensor")
    own_rows, model_width = moe_in.shape
    upgate_low, downproj_low = up[0].astype(BF), down[0].astype(BF)
    local_blocks = upgate_low.shape[1]
    expert_total = local_blocks * data_size
    slots = local_blocks * capacity
    kept = target >= 0
    put_at = jnp.where(kept, target, expert_total * capacity)
    fetch_at = jnp.where(kept, target, 0)
    pair_weight = jnp.where(kept, gate_values.reshape(-1), 0.0)

    def send(pair_rows):
        empty = jnp.zeros((expert_total * capacity, model_width), BF)
        filled = empty.at[put_at].set(pair_rows, mode="drop")
        filled = filled.reshape(1, data_size, slots, model_width)
        wide = lax.all_gather(filled, "tensor", axis=0, tiled=True)
        wide = lax.all_to_all(wide, "dp", split_axis=1, concat_axis=1, tiled=True)
        return wide.reshape(tensor_size, data_size, local_blocks, capacity, model_width)

    def bring(parts):
        parts = parts.reshape(tensor_size, data_size, slots, model_width)
        wide = lax.all_to_all(parts.astype(BF), "dp", split_axis=1, concat_axis=1, tiled=True)
        wide = lax.all_to_all(wide, "tensor", split_axis=0, concat_axis=0, tiled=True)
        summed = jnp.sum(wide.astype(F32), axis=0).astype(BF)
        return summed.reshape(expert_total * capacity, model_width)

    def dot(spec, a, b):
        return jnp.einsum(spec, a, b, preferred_element_type=F32)

    rows_in = send(jnp.repeat(moe_in, TOP, axis=0))
    gate_pre = dot("abecd,edf->abecf", rows_in, upgate_low[0])
    up_pre = dot("abecd,edf->abecf", rows_in, upgate_low[1])
    inner_act = (jax.nn.silu(gate_pre) * up_pre).astype(BF)
    pair_out = bring(dot("abecf,efd->abecd", inner_act, downproj_low))[fetch_at].astype(F32)
    mixed = jnp.sum((pair_weight[:, None] * pair_out).reshape(own_rows, TOP, model_width), axis=1)
    seed_grad = cotangent.astype(F32) * live_rows[:, None].astype(F32)
    seed_pairs = jnp.repeat(seed_grad, TOP, axis=0)
    gate_grad = jnp.where(kept, jnp.sum(pair_out * seed_pairs, axis=1), 0.0)
    out_seed = send((pair_weight[:, None] * seed_pairs).astype(BF))
    inner_grad = dot("abecd,efd->abecf", out_seed, downproj_low)
    down_grad = dot("abecf,abecd->efd", inner_act, out_seed)
    sig = jax.nn.sigmoid(gate_pre)
    gate_back = (inner_grad * up_pre * sig * (1.0 + gate_pre * (1.0 - sig))).astype(BF)
    up_back = (inner_grad * gate_pre * sig).astype(BF)
    up_grad = jnp.stack(
        [
            dot("abecd,abecf->edf", rows_in, gate_back),
            dot("abecd,abecf->edf", rows_in, up_back),
        ]
    )
    rows_grad = dot("abecf,edf->abecd", gate_back, upgate_low[0])
    rows_grad = rows_grad + dot("abecf,edf->abecd", up_back, upgate_low[1])
    back = bring(rows_grad)[fetch_at].astype(F32)
    back = jnp.where(kept[:, None], back, 0.0)
    moe_grad = jnp.sum(back.reshape(own_rows, TOP, model_width), axis=1)
    return (
        mixed,
        gate_grad.reshape(own_rows, TOP),
        moe_grad,
        adam_step(up[0], up_grad, *up[1:], WEIGHT_DECAY),
        adam_step(down[0], down_grad, *down[1:], WEIGHT_DECAY),
    )


def flip(v, axis, bit):
    return lax.ppermute(v, axis, [(i, i ^ bit) for i in range(lax.axis_size(axis))])


def core(v):
    return flip(v, "tensor", 1)


def across(v):
    return flip(v, "tensor", 2)


def side(v):
    return flip(v, "dp", 1)


def onward(v, planes=1):
    n = lax.axis_size("dp")
    return lax.ppermute(v, "dp", [(i, (i + 2 * planes) % n) for i in range(n)])


def plus(*vs):
    return functools.reduce(lambda a, b: a + b, [v.astype(F32) for v in vs]).astype(BF)


def meet(*vs):
    return lax.optimization_barrier(vs)


def group_sum(far, near):
    sent = across(plus(far[0], core(far[1])))
    return plus(near[0], core(near[1])).astype(F32) + sent.astype(F32)


HALF = BLOCK // 2


class Spread:
    def __init__(self, own):
        self.z, self.x, self.y, self.top, self.low, self.own, self.sib = (
            {0: own}, {}, {}, {}, {}, {}, {},
        )

    def on(self, r):
        self.z[r] = onward(self.z[r - 1])

    def x_(self, r):
        self.x[r] = across(self.z[r])

    def y_(self, r):
        self.y[r] = side(self.z[r])

    def wide(self, r):
        self.x_(r), self.y_(r)

    def corner(self, r):
        self.top[r], self.low[r] = side(self.x[r][:HALF]), across(self.y[r][HALF:])

    def cores(self, r):
        z = self.z[r]
        last = jnp.concatenate([self.top.pop(r), self.low.pop(r)], axis=0)
        self.own[r] = jnp.stack([z, self.x.pop(r), self.y.pop(r), last])
        self.sib[r] = core(self.own[r])

    def state(self):
        return [self.z, self.x, self.y, self.top, self.low, self.own, self.sib]

    def put(self, state):
        self.z, self.x, self.y, self.top, self.low, self.own, self.sib = state


class Reduce:
    def __init__(self):
        self.own, self.sib, self.came, self.here, self.x, self.y, self.top, self.low = (
            {} for _ in range(8)
        )
        self.wx, self.wy, self.total = {}, {}, {}

    def cores(self, r):
        self.came[r] = core(self.sib.pop(r))

    def corner(self, r):
        part = plus(self.own.pop(r), self.came.pop(r))
        self.here[r], self.x[r], self.y[r] = part[0], part[1], part[2]
        self.top[r], self.low[r] = side(part[3][:HALF]), across(part[3][HALF:])

    def x_(self, r):
        x = self.x.pop(r)
        self.wx[r] = across(jnp.concatenate([plus(x[:HALF], self.top.pop(r)), x[HALF:]], axis=0))

    def y_(self, r):
        y = self.y.pop(r)
        self.wy[r] = side(jnp.concatenate([y[:HALF], plus(y[HALF:], self.low.pop(r))], axis=0))

    def wide(self, r):
        self.x_(r), self.y_(r)

    def plane(self, r):
        vs = (self.here.pop(r), self.wx.pop(r), self.wy.pop(r))
        if r in self.total:
            vs = vs + (self.total.pop(r),)
        return functools.reduce(lambda a, b: a + b, [v.astype(F32) for v in vs])

    def on(self, r, count):
        self.total[(r + 1) % count] = onward(self.plane(r).astype(BF))

    def state(self):
        return [
            self.own, self.sib, self.came, self.here, self.x, self.y, self.top, self.low,
            self.wx, self.wy, self.total,
        ]

    def put(self, state):
        (
            self.own, self.sib, self.came, self.here, self.x, self.y, self.top, self.low,
            self.wx, self.wy, self.total,
        ) = state


def data_parts(part):
    n = lax.axis_size("dp")
    me = lax.axis_index("dp")
    planes = n // 2
    pairs = part.reshape((planes, 2, part.shape[0] // n) + part.shape[1:])
    mine = lax.dynamic_index_in_dim(pairs, me % 2, 1, keepdims=False)
    other = lax.dynamic_index_in_dim(pairs, 1 - me % 2, 1, keepdims=False)
    order = [((me // 2) + planes - r) % planes for r in range(planes)]
    at = lambda a, r: lax.dynamic_index_in_dim(a, order[r], 0, keepdims=False)
    return tuple(jnp.stack([at(a, r) for r in range(planes)]) for a in (mine, other))


def sum_all(v):
    for axis in ("tensor", "dp"):
        bit = 1
        while bit < lax.axis_size(axis):
            v = v + flip(v, axis, bit)
            bit *= 2
    return v


def pack_weights(query_weight, keyvalue_matrix, outproj_weight, norm_gains):
    return jnp.concatenate(
        [
            query_weight.astype(BF),
            keyvalue_matrix[0].astype(BF),
            keyvalue_matrix[1].astype(BF),
            outproj_weight.astype(BF).T,
            jnp.pad(norm_gains.astype(BF).T, ((0, 0), (0, 126))),
        ],
        axis=1,
    )


def normed(v):
    rms = lax.rsqrt(jnp.mean(v * v, axis=-1, keepdims=True) + NORM_EPS)
    return rms, v * rms


def norm_back(grad, gain, rms, norm):
    scaled = grad * gain
    return rms * (scaled - norm * jnp.mean(scaled * norm, axis=-1, keepdims=True))


def few_groups(
    hidden_in, cotangent, lengths, routes, gate_values, target, live_rows, capacity,
    query_weight, keyvalue_matrix, outproj_weight, norm_gains, up, down,
):
    tensor_index, me = lax.axis_index("tensor"), lax.axis_index("dp")
    count = lax.axis_size("dp") // 2
    qw, kw = query_weight.shape[1], keyvalue_matrix.shape[2]
    share = qw // kw
    local = up[0].shape[1]
    width = hidden_in.shape[1]

    wide = qw + 2 * kw
    out_cols, in_cols = (wide, wide + qw), (0, wide)

    w = [pack_weights(query_weight, keyvalue_matrix, outproj_weight, norm_gains)]
    hx, hc = across(hidden_in), core(hidden_in)
    sides = []
    for r in range(count - 1):
        sides.append(side(w[r]))
        w.append(onward(w[r]))
        w[r + 1], sides[r] = meet(w[r + 1], sides[r])
    sides.append(side(w[-1]))
    hxc = core(hx)
    upgate_low, down_low = up[0].astype(BF), down[0].astype(BF)
    wgu = jnp.concatenate([upgate_low[0], upgate_low[1]], axis=-1)
    places = [(me + 2 * (count - r)) % (2 * count) for r in range(count)]
    weight_places = [p for r in range(count) for p in (places[r], places[r] ^ 1)]
    at = [tensor_index ^ j for j in range(4)] + weight_places
    at = jnp.stack([jnp.asarray(p, jnp.int32) for p in at])
    cos, sin = rope_lanes(4 * BLOCK)

    seeds = jnp.where(live_rows[:, None], cotangent, jnp.zeros((), BF))
    slot = jnp.where(target >= 0, target - routes.reshape(-1) * capacity, -1).reshape(-1, TOP)
    high = gate_values.astype(BF)
    low = (gate_values - high.astype(F32)).astype(BF)
    table = jnp.concatenate([routes.astype(BF).T, slot.astype(BF).T, high.T, low.T], axis=1)
    table = jnp.pad(table, ((0, 0), (0, width - table.shape[1])))
    first = (me * local).astype(jnp.int32).reshape(1)
    c = Spread(jnp.concatenate([seeds, table], axis=0))
    c.z[0], w[-1] = meet(c.z[0], w[-1])
    c.x_(0), c.on(1)

    (rows_of, w, sides, wgu, down_low, cos, sin, st) = meet(
        [hidden_in, hc, hx, hxc], w, sides, wgu, down_low, cos, sin, c.state()
    )
    c.put(st)
    weight_blocks = [b for r in range(count) for b in (w[r], sides[r])]
    attn_in, q, k, v, gains, packed = qkv(at, rows_of, weight_blocks, qw, kw, cos, sin)
    c.y_(0), c.x_(1), c.on(2)
    q, k, v, gains, st = meet(q, k, v, gains, c.state())
    c.put(st)
    gain_attn, gain_moe = gains[0:1], gains[1:2]
    heads, lse = attend(lengths, q, k, v, share)
    c.corner(0), c.y_(1), c.on(3), c.x_(2)
    heads, st = meet(heads, c.state())
    c.put(st)
    far, near = project(at, heads, packed, out_cols)
    far1 = core(far[1])
    c.cores(0)
    far, near, far1, st, first = meet(far, near, far1, c.state(), first)
    c.put(st)
    sent, near1 = across(plus(far[0], far1)), core(near[1])
    us, tabs, kept_s = {}, {}, None

    def seed(r):
        nonlocal kept_s
        kept_s, us[r], tabs[r] = seed_rows(
            r, count, first, c.own.pop(r), c.sib.pop(r), down_low, kept_s, capacity
        )

    seed(0)
    c.y_(2)
    sent, near, near1, us[0], tabs[0], st = meet(sent, near, near1, us[0], tabs[0], c.state())
    c.put(st)
    attn_own = plus(near[0], near1).astype(F32) + sent.astype(F32)
    hidden = hidden_in.astype(F32)
    middle = hidden + attn_own
    rms_moe, normed_moe = normed(middle)
    m = Spread((normed_moe * gain_moe).astype(BF))
    back, mix = Reduce(), Reduce()
    kept, news, turn = None, [], first

    def expert(r):
        nonlocal kept
        x, dgu, act, back.own[r], back.sib[r] = expert_rows(
            r, count, first, tabs[r], us[r], m.own.pop(r), m.sib.pop(r), wgu, kept, capacity
        )
        kept = (x, dgu, act)

    def mixes(r):
        mix.own[r], mix.sib[r] = mix_rows(r, first, tabs[r], kept[2], down_low, capacity)

    def weights(begin, size):
        nonlocal news, turn
        news, turn = weights_step(
            turn, begin, size, kept[0], kept_s, kept[1], kept[2], up, down, news
        )

    def step():
        nonlocal first, us, tabs, turn
        first, turn, us, tabs, sc, sm, sb, sx = meet(
            first, turn, us, tabs, c.state(), m.state(), back.state(), mix.state()
        )
        c.put(sc), m.put(sm), back.put(sb), mix.put(sx)

    m.z[0], st = meet(m.z[0], c.state())
    c.put(st)
    m.wide(0), m.on(1), c.corner(1)
    step()
    m.corner(0), c.wide(3), c.cores(1), m.on(2)
    step()
    m.wide(1), c.corner(2), m.cores(0)
    seed(1)
    step()
    m.corner(1), m.wide(2), c.cores(2), m.on(3)
    expert(0)
    step()
    c.corner(3), m.wide(3), m.cores(1)
    seed(2)
    mixes(0)
    step()
    m.corner(2), c.cores(3), back.cores(0), mix.cores(0)
    expert(1)
    step()
    m.corner(3), m.cores(2), back.corner(0), back.cores(1)
    seed(3)
    mixes(1)
    step()
    back.corner(1), m.cores(3), mix.corner(0), mix.cores(1)
    expert(2)
    step()
    back.wide(1), back.cores(2), mix.corner(1)
    expert(3)
    step()
    back.on(1, count), back.wide(0), back.corner(2), back.cores(3)
    mixes(2)
    mixes(3)
    step()
    back.wide(2), back.corner(3), mix.cores(2)
    weights(0, 2)
    step()
    back.on(2, count), back.wide(3), mix.cores(3)
    weights(2, 2)
    step()
    back.on(3, count), mix.wide(1)
    step()
    whole = back.plane(0)
    gate_grad, moe_grad = whole[BLOCK:, :BLOCK].T, whole[:BLOCK]

    seed_grad = cotangent.astype(F32) * live_rows[:, None].astype(F32)
    gain_moe_part = jnp.sum(moe_grad * normed_moe, axis=0)
    middle_grad = seed_grad + norm_back(moe_grad, gain_moe, rms_moe, normed_moe)
    mid, turn, st = meet(middle_grad.astype(BF), turn, mix.state())
    mix.put(st)
    mx, mc = across(mid), core(mid)
    mix.on(1, count), mix.y_(0)
    weights(4, 2)
    mx, mc, turn, st, gain_moe_part = meet(mx, mc, turn, mix.state(), gain_moe_part)
    mix.put(st)
    mxc = core(mx)
    mix.corner(2)
    heads_grad, middle_low = heads_back(at, [mid, mc, mx, mxc], packed, out_cols)
    omine, oother = data_parts(mm(middle_low, heads, TN).astype(BF))
    heads_grad, omine, oother, st = meet(heads_grad, omine, oother, mix.state())
    mix.put(st)
    dq, dk, dv = attend_back(lengths, q, k, v, heads, heads_grad, lse, cos, sin, share)
    ocame = side(oother)
    mix.x_(0), mix.corner(3)
    dq, dk, dv, ocame, omine, st = meet(dq, dk, dv, ocame, omine, mix.state())
    mix.put(st)
    dqkv = jnp.concatenate([dq, dk, dv], axis=1)
    far, near = project(at, dqkv, packed, in_cols)
    far1 = core(far[1])
    osums = plus(omine, ocame)
    oring = onward(osums[1])
    qmine, qother = data_parts(mm(attn_in, dqkv, TN).astype(BF))
    far, near, far1, oring, osums, qmine, qother, st = meet(
        far, near, far1, oring, osums, qmine, qother, mix.state()
    )
    mix.put(st)
    sent, near1 = across(plus(far[0], far1)), core(near[1])
    qcame = side(qother)
    oring = onward(plus(osums[2], oring))
    weights(6, 2)
    sent, near, near1, qcame, qmine, oring, turn, st = meet(
        sent, near, near1, qcame, qmine, oring, turn, mix.state()
    )
    mix.put(st)
    attn_grad = plus(near[0], near1).astype(F32) + sent.astype(F32)
    rms_attn, normed_attn = normed(hidden)
    gain_attn_part = jnp.sum(attn_grad * normed_attn, axis=0)
    input_grad = middle_grad + norm_back(attn_grad, gain_attn, rms_attn, normed_attn)
    gains_sum = sum_all(jnp.stack([gain_attn_part, gain_moe_part]))
    qsums = plus(qmine, qcame)
    mix.wide(2)
    oring = onward(plus(osums[3], oring))
    qring = onward(qsums[1])
    oring, qring, st = meet(oring, qring, mix.state())
    mix.put(st)
    mix.wide(3), mix.on(2, count)
    qring = onward(plus(qsums[2], qring))
    qring, st = meet(qring, mix.state())
    mix.put(st)
    mix.on(3, count)
    qring = onward(plus(qsums[3], qring))
    outproj_sum = (osums[0].astype(F32) + oring.astype(F32)).T
    qkv_sum = qsums[0].astype(F32) + qring.astype(F32)
    block_out = (middle + mix.plane(0)).astype(BF)
    return (
        block_out, input_grad, gate_grad, qkv_sum, outproj_sum, gains_sum,
        tuple(news[:4]), tuple(news[4:]),
    )


def many_groups(
    hidden_in, cotangent, lengths, routes, gate_values, target, live_rows, capacity,
    query_weight, keyvalue_matrix, outproj_weight, norm_gains, up, down,
):
    qw, kw = query_weight.shape[1], keyvalue_matrix.shape[2]
    share = qw // kw
    packed = pack_weights(query_weight, keyvalue_matrix, outproj_weight, norm_gains)
    packed = lax.all_gather(packed, "dp", axis=0, tiled=True)
    group = lax.all_gather(hidden_in, "tensor", axis=0, tiled=True)
    rows_of = [group[i * BLOCK : (i + 1) * BLOCK] for i in range(4)]
    at = jnp.concatenate([jnp.arange(4, dtype=jnp.int32), jnp.zeros((1,), jnp.int32)])
    cos, sin = rope_lanes(4 * BLOCK)
    attn_in, q, k, v, gains, packed = qkv(at, rows_of, [packed], qw, kw, cos, sin)
    wide = qw + 2 * kw
    qkv_low, outproj_low = packed[:, :wide], packed[:, wide : wide + qw]
    gain_attn, gain_moe = gains[0:1], gains[1:2]
    heads, lse = attend(lengths, q, k, v, share)

    def scattered(part):
        part = lax.psum_scatter(part.astype(BF), "tensor", scatter_dimension=0, tiled=True)
        return part.astype(F32)

    hidden = hidden_in.astype(F32)
    middle = hidden + scattered(mm(heads, outproj_low, NT))
    rms_moe, normed_moe = normed(middle)
    moe_in = (normed_moe * gain_moe).astype(BF)
    mixed, gate_grad, moe_grad, up_new, down_new = experts_by_slot(
        moe_in, cotangent, live_rows, target, gate_values, lengths, up, down, capacity,
        lax.axis_size("dp"),
    )
    block_out = (middle + mixed).astype(BF)
    seed_grad = cotangent.astype(F32) * live_rows[:, None].astype(F32)
    gain_moe_part = jnp.sum(moe_grad * normed_moe, axis=0)
    middle_grad = seed_grad + norm_back(moe_grad, gain_moe, rms_moe, normed_moe)
    middle_low = lax.all_gather(middle_grad.astype(BF), "tensor", axis=0, tiled=True)
    heads_grad = mm(middle_low, outproj_low).astype(BF)
    dq, dk, dv = attend_back(lengths, q, k, v, heads, heads_grad, lse, cos, sin, share)
    dqkv = jnp.concatenate([dq, dk, dv], axis=1)
    attn_grad = scattered(mm(dqkv, qkv_low, NT))
    rms_attn, normed_attn = normed(hidden)
    gain_attn_part = jnp.sum(attn_grad * normed_attn, axis=0)
    input_grad = middle_grad + norm_back(attn_grad, gain_attn, rms_attn, normed_attn)
    gains_sum = lax.psum(jnp.stack([gain_attn_part, gain_moe_part]), ("dp", "tensor"))
    part = jnp.concatenate([mm(attn_in, dqkv, TN), mm(middle_low, heads, TN)], axis=1)
    summed = lax.psum_scatter(part, "dp", scatter_dimension=0, tiled=True)
    return (
        block_out, input_grad, gate_grad, summed[:, :wide], summed[:, wide:].T, gains_sum,
        up_new, down_new,
    )


def on_device(
    hidden_in,
    cotangent,
    lengths,
    routes,
    gate_values,
    pair_order,
    query_weight,
    keyvalue_matrix,
    outproj_weight,
    norm_gains,
    upgate_weight,
    downproj_weight,
    query_mean,
    query_sqmean,
    keyvalue_first_moment,
    keyvalue_second_moment,
    outproj_mean,
    outproj_sqmean,
    gains_mean,
    gains_sqmean,
    upgate_mean,
    upgate_sqmean,
    downproj_mean,
    downproj_sqmean,
):
    tensor_size = lax.axis_size("tensor")
    data_size = lax.axis_size("dp")
    own_rows, model_width = hidden_in.shape
    group_rows = own_rows * tensor_size
    qw = query_weight.shape[1]
    kw = keyvalue_matrix.shape[2]
    assert lengths.shape[0] == 1 and group_rows == SEQUENCE_SLOTS and own_rows == BLOCK

    tensor_index = lax.axis_index("tensor")
    row_ids = tensor_index * own_rows + jnp.arange(own_rows, dtype=jnp.int32)
    live_rows = row_ids < lengths[0]
    capacity = max(2, own_rows * TOP * 5 // (4 * upgate_weight.shape[1] * data_size))
    target = slot_targets(routes.reshape(-1), pair_order[0], jnp.repeat(live_rows, TOP), capacity)
    few = data_size * group_rows * model_width <= 1 << 24
    block_out, input_grad, gate_grad, qkv_sum, outproj_sum, gains_sum, up_new, down_new = (
        few_groups if few else many_groups
    )(
        hidden_in, cotangent, lengths, routes, gate_values, target, live_rows, capacity,
        query_weight, keyvalue_matrix, outproj_weight, norm_gains,
        (upgate_weight, upgate_mean, upgate_sqmean),
        (downproj_weight, downproj_mean, downproj_sqmean),
    )
    own_cols = norm_gains.shape[1]
    gains_sum = lax.dynamic_slice_in_dim(gains_sum, lax.axis_index("dp") * own_cols, own_cols, 1)
    query_sum = qkv_sum[:, :qw]
    keyval_sum = jnp.stack([qkv_sum[:, qw : qw + kw], qkv_sum[:, qw + kw :]])
    return (
        (block_out, input_grad, gate_grad)
        + adam_step(query_weight, query_sum, query_mean, query_sqmean, WEIGHT_DECAY)
        + adam_step(
            keyvalue_matrix, keyval_sum, keyvalue_first_moment, keyvalue_second_moment, WEIGHT_DECAY
        )
        + adam_step(outproj_weight, outproj_sum, outproj_mean, outproj_sqmean, WEIGHT_DECAY)
        + adam_step(norm_gains, gains_sum, gains_mean, gains_sqmean, 0.0)
        + up_new
        + down_new
    )


def solution(mesh):
    placed = (
        P(("dp", "tensor"), None),
        P(("dp", "tensor"), None),
        P("dp"),
        P(("dp", "tensor"), None),
        P(("dp", "tensor"), None),
        P(("dp", "tensor"), None),
        P("dp", "tensor"),
        P(None, "dp", "tensor"),
        P("tensor", "dp"),
        P(None, "dp"),
        P(None, "dp", None, "tensor"),
        P("dp", "tensor", None),
        P("dp", "tensor"),
        P("dp", "tensor"),
        P(None, "dp", "tensor"),
        P(None, "dp", "tensor"),
        P("tensor", "dp"),
        P("tensor", "dp"),
        P(None, "dp"),
        P(None, "dp"),
        P(None, "dp", None, "tensor"),
        P(None, "dp", None, "tensor"),
        P("dp", "tensor", None),
        P("dp", "tensor", None),
    )
    return jax.shard_map(
        on_device,
        mesh=mesh,
        in_specs=placed,
        out_specs=(
            P(("dp", "tensor"), None),
            P(("dp", "tensor"), None),
            P(("dp", "tensor"), None),
            P("dp", "tensor"),
            P("dp", "tensor"),
            P("dp", "tensor"),
            P("dp", "tensor"),
            P(None, "dp", "tensor"),
            P(None, "dp", "tensor"),
            P(None, "dp", "tensor"),
            P(None, "dp", "tensor"),
            P("tensor", "dp"),
            P("tensor", "dp"),
            P("tensor", "dp"),
            P("tensor", "dp"),
            P(None, "dp"),
            P(None, "dp"),
            P(None, "dp"),
            P(None, "dp"),
            P(None, "dp", None, "tensor"),
            P(None, "dp", None, "tensor"),
            P(None, "dp", None, "tensor"),
            P(None, "dp", None, "tensor"),
            P("dp", "tensor", None),
            P("dp", "tensor", None),
            P("dp", "tensor", None),
            P("dp", "tensor", None),
        ),
        check_vma=False,
    )
```

```python
import functools
import jax
import jax.numpy as jnp
from jax import lax
from jax.experimental import pallas as pl
from jax.experimental.pallas import tpu as pltpu
from jax.sharding import PartitionSpec as P

HEAD_SIZE = 64
TOP = 8
SEQUENCE_SLOTS = 1024
ADAM_STEP = 5
NORM_EPS = 1e-05
ROPE_THETA = 10000.0
MASKED = -1e30
BETA_ONE = 0.9
BETA_TWO = 0.95
LEARN_RATE = 0.03
WEIGHT_DECAY = 0.1
ADAM_EPS = 1e-08
BF = jnp.bfloat16
F32 = jnp.float32
BLOCK = 256
NN = (((1,), (0,)), ((), ()))
NT = (((1,), (1,)), ((), ()))
TN = (((0,), (0,)), ((), ()))


def mm(a, b, dims=NN):
    return lax.dot_general(a, b, dims, preferred_element_type=F32)


def params(mib=58):
    return pltpu.CompilerParams(vmem_limit_bytes=mib << 20)


def adam_step(weight, gradient, first_old, second_old, decay_rate):
    first_new = BETA_ONE * first_old + (1.0 - BETA_ONE) * gradient
    second_new = BETA_TWO * second_old + (1.0 - BETA_TWO) * gradient * gradient
    first_hat = first_new / (1.0 - BETA_ONE**ADAM_STEP)
    second_hat = second_new / (1.0 - BETA_TWO**ADAM_STEP)
    update = -LEARN_RATE * (first_hat / (jnp.sqrt(second_hat) + ADAM_EPS) + decay_rate * weight)
    return (gradient, first_new, second_new, update)


def rank_body(cap, ecol, ocol, erow, orow, out):
    pairs = erow.shape[1]
    step = 64
    er, orr = erow[...], orow[...]

    def chunk(i, acc):
        rows = pl.ds(i * step, step)
        hit = (ecol[rows, :] == er) & (ocol[rows, :] < orr)
        return acc + jnp.sum(hit.astype(jnp.int32), axis=0, keepdims=True)

    rank = lax.fori_loop(0, pairs // step, chunk, jnp.zeros((1, pairs), jnp.int32))
    kept = (orr < pairs) & (rank < cap)
    out[...] = jnp.where(kept, er * cap + rank, -1)


def slot_targets(experts, order, live_pairs, cap):
    pairs = experts.shape[0]
    order = jnp.where(live_pairs, order, pairs)
    return pl.pallas_call(
        functools.partial(rank_body, cap),
        out_shape=jax.ShapeDtypeStruct((1, pairs), jnp.int32),
        compiler_params=params(16),
        name="slot_targets",
    )(experts[:, None], order[:, None], experts[None, :], order[None, :])[0]


def swap_halves(u):
    width = u.shape[1]
    lane = lax.broadcasted_iota(jnp.int32, u.shape, 1) % HEAD_SIZE
    half = HEAD_SIZE // 2
    return jnp.where(lane < half, pltpu.roll(u, width - half, 1), pltpu.roll(u, half, 1))


def rope(u, cos, sin):
    reps = u.shape[1] // cos.shape[1]
    if reps > 1:
        cos = jnp.concatenate([cos] * reps, axis=1)
        sin = jnp.concatenate([sin] * reps, axis=1)
    return u * cos + swap_halves(u) * sin


def rope_lanes(rows):
    lane = jnp.arange(128) % HEAD_SIZE
    half = HEAD_SIZE // 2
    positions = (jnp.arange(rows) % SEQUENCE_SLOTS).astype(F32)
    freqs = ROPE_THETA ** (-(2.0 * (lane % half).astype(F32)) / HEAD_SIZE)
    angles = positions[:, None] * freqs[None, :]
    return jnp.cos(angles), jnp.where(lane < half, -1.0, 1.0) * jnp.sin(angles)


ANY = pl.BlockSpec(memory_space=pltpu.HBM)


def cost(flops, nbytes):
    return pl.CostEstimate(flops=int(flops), bytes_accessed=int(nbytes), transcendentals=0)


def qkv_body(qw, kw, xn, wn, at, *refs):
    xs, ws, refs = refs[:xn], refs[xn : xn + wn], refs[xn + wn :]
    cos, sin, a_out, q_out, k_out, v_out, gains, w_out, x_scr, sem = refs
    step = ws[0].shape[0]
    copies = []
    for i, ref in enumerate(ws):
        rows = pl.ds(pl.multiple_of(at[xn + i] * step, 16), step)
        copies.append(pltpu.make_async_copy(ref, w_out.at[rows, :], sem.at[xn + i]))
    for i, ref in enumerate(xs):
        rows = pl.ds(pl.multiple_of(at[i] * BLOCK, BLOCK), BLOCK)
        copies.append(pltpu.make_async_copy(ref, x_scr.at[rows, :], sem.at[i]))
    for c in copies:
        c.start()
    for c in copies:
        c.wait()
    wide = qw + 2 * kw
    gains[...] = w_out[:, wide + qw :].astype(F32).T[0:8, :]

    def block(i, _):
        rows = pl.ds(pl.multiple_of(i * BLOCK, BLOCK), BLOCK)
        v = x_scr[rows, :].astype(F32)
        r = lax.rsqrt(jnp.mean(v * v, axis=-1, keepdims=True) + NORM_EPS)
        a = (v * r * gains[0:1, :]).astype(BF)
        a_out[rows, :] = a
        y = mm(a, w_out[:, :wide])
        c, s = cos[rows, :], sin[rows, :]
        q_out[rows, :] = rope(y[:, :qw], c, s).astype(BF)
        k_out[rows, :] = rope(y[:, qw : qw + kw], c, s).astype(BF)
        v_out[rows, :] = y[:, qw + kw :].astype(BF)
        return 0

    lax.fori_loop(0, len(xs), block, 0)


def qkv(at, xs, ws, qw, kw, cos, sin):
    rows, width = BLOCK * len(xs), xs[0].shape[1]
    cols = ws[0].shape[1]
    depth = ws[0].shape[0] * len(ws)
    vm = pl.BlockSpec(memory_space=pltpu.VMEM)
    return pl.pallas_call(
        functools.partial(qkv_body, qw, kw, len(xs), len(ws)),
        in_specs=[pl.BlockSpec(memory_space=pltpu.SMEM)]
        + [ANY] * (len(xs) + len(ws))
        + [vm, vm],
        out_specs=[vm] * 6,
        out_shape=[
            jax.ShapeDtypeStruct((rows, width), BF),
            jax.ShapeDtypeStruct((rows, qw), BF),
            jax.ShapeDtypeStruct((rows, kw), BF),
            jax.ShapeDtypeStruct((rows, kw), BF),
            jax.ShapeDtypeStruct((8, width), F32),
            jax.ShapeDtypeStruct((depth, cols), BF),
        ],
        scratch_shapes=[
            pltpu.VMEM((rows, width), BF),
            pltpu.SemaphoreType.DMA((len(xs) + len(ws),)),
        ],
        compiler_params=params(60),
        cost_estimate=cost(2 * rows * width * cols, 2e7),
        name="qkv",
    )(at, *xs, *ws, cos, sin)


def project_body(cols, at, v, w, *outs):
    for i, out in enumerate(outs):
        rows = pl.ds(pl.multiple_of(at[i] * BLOCK, BLOCK), BLOCK)
        out[...] = mm(v[rows, :], w[:, cols[0] : cols[1]], NT).astype(BF)


def project(at, v, w, cols):
    rows, depth = v.shape
    width = w.shape[0]
    vm = pl.BlockSpec(memory_space=pltpu.VMEM)
    return pl.pallas_call(
        functools.partial(project_body, cols),
        in_specs=[pl.BlockSpec(memory_space=pltpu.SMEM), vm, vm],
        out_specs=[vm] * 4,
        out_shape=[jax.ShapeDtypeStruct((BLOCK, width), BF)] * 4,
        compiler_params=params(32),
        cost_estimate=cost(2 * rows * depth * width, 1e7),
        name="project",
    )(at, v, w)


def heads_back_body(cols, at, m0, m1, m2, m3, w, h_out, m_out, sem):
    copies = []
    for i, ref in enumerate((m0, m1, m2, m3)):
        rows = pl.ds(pl.multiple_of(at[i] * BLOCK, BLOCK), BLOCK)
        copies.append(pltpu.make_async_copy(ref, m_out.at[rows, :], sem.at[i]))
    for c in copies:
        c.start()
    for c in copies:
        c.wait()

    def block(i, _):
        rows = pl.ds(pl.multiple_of(i * BLOCK, BLOCK), BLOCK)
        h_out[rows, :] = mm(m_out[rows, :], w[:, cols[0] : cols[1]]).astype(BF)
        return 0

    lax.fori_loop(0, 4, block, 0)


def heads_back(at, ms, w, cols):
    width, qw = w.shape[0], cols[1] - cols[0]
    rows = 4 * BLOCK
    vm = pl.BlockSpec(memory_space=pltpu.VMEM)
    return pl.pallas_call(
        functools.partial(heads_back_body, cols),
        in_specs=[pl.BlockSpec(memory_space=pltpu.SMEM)] + [ANY] * 4 + [vm],
        out_specs=[vm, vm],
        out_shape=[
            jax.ShapeDtypeStruct((rows, qw), BF),
            jax.ShapeDtypeStruct((rows, width), BF),
        ],
        scratch_shapes=[pltpu.SemaphoreType.DMA((4,))],
        compiler_params=params(32),
        cost_estimate=cost(2 * rows * qw * width, 1e7),
        name="heads_back",
    )(at, *ms, w)


def spread(pair_lanes, out):
    lane = lax.broadcasted_iota(jnp.int32, pair_lanes.shape, 1)
    full = pair_lanes.astype(F32)
    first = jnp.where(lane < HEAD_SIZE, full, 0.0)
    second = jnp.where(lane < HEAD_SIZE, 0.0, full)
    out[0] = first.astype(BF)
    out[1] = pltpu.roll(first, HEAD_SIZE, 1).astype(BF)
    out[2] = pltpu.roll(second, HEAD_SIZE, 1).astype(BF)
    out[3] = second.astype(BF)


def attend_body(share, length, q, k, v, o, lse, ks, vs):
    pair, qb = pl.program_id(0), pl.program_id(1)

    @pl.when((pair == 0) & (qb == 0))
    def _():
        spread(k[...], ks)
        spread(v[...], vs)

    scale = HEAD_SIZE**-0.5
    for j in range(SEQUENCE_SLOTS // BLOCK):

        @pl.when(qb == j)
        def _():
            keys = (j + 1) * BLOCK
            kpos = lax.broadcasted_iota(jnp.int32, (BLOCK, keys), 1)
            qpos = lax.broadcasted_iota(jnp.int32, (BLOCK, keys), 0) + j * BLOCK
            allowed = (kpos <= qpos) & (kpos < length[0])
            total = jnp.zeros((BLOCK, 128), F32)
            for u in range(2):
                which = 2 * ((2 * pair + u) // share) + u
                s = mm(q[...], ks[which, :keys, :], NT) * scale
                s = jnp.where(allowed, s, MASKED)
                top = jnp.max(s, axis=-1, keepdims=True)
                e = jnp.exp(s - top)
                den = jnp.sum(e, axis=-1, keepdims=True)
                total += mm(e.astype(BF), vs[which, :keys, :]) / den
                full = jnp.broadcast_to(top + jnp.log(den), (BLOCK, 128))
                lse[0, u : u + 1, :] = full.T[0:1, :]
            o[...] = total.astype(BF)


def attend(length, q, k, v, share):
    rows, qw = q.shape
    kw = k.shape[1]
    assert kw == 128 and rows == SEQUENCE_SLOTS
    pairs = qw // 128
    blocks = rows // BLOCK
    fix = lambda p, b, n: (0, 0)
    return pl.pallas_call(
        functools.partial(attend_body, share),
        grid_spec=pltpu.PrefetchScalarGridSpec(
            num_scalar_prefetch=1,
            grid=(pairs, blocks),
            in_specs=[
                pl.BlockSpec((BLOCK, 128), lambda p, b, n: (b, p)),
                pl.BlockSpec((rows, kw), fix),
                pl.BlockSpec((rows, kw), fix),
            ],
            out_specs=[
                pl.BlockSpec((BLOCK, 128), lambda p, b, n: (b, p)),
                pl.BlockSpec((1, 8, BLOCK), lambda p, b, n: (p, 0, b)),
            ],
            scratch_shapes=[pltpu.VMEM((4, rows, 128), BF), pltpu.VMEM((4, rows, 128), BF)],
        ),
        out_shape=[
            jax.ShapeDtypeStruct((rows, qw), BF),
            jax.ShapeDtypeStruct((pairs, 8, rows), F32),
        ],
        compiler_params=params(32),
        name="attend",
    )(length, q, k, v)


def attend_back_body(
    share, length, q, k, v, o, do, lse, cos, sin, coskv, sinkv, dq, dk, dv, ks, vs, kt, dka, dva
):
    pair, qb = pl.program_id(0), pl.program_id(1)
    scale = HEAD_SIZE**-0.5

    @pl.when((pair == 0) & (qb == 0))
    def _():
        spread(k[...], ks)
        spread(v[...], vs)
        for i in range(4):
            kt[i] = ks[i].astype(F32).T.astype(BF)
        dka[...] = jnp.zeros_like(dka)
        dva[...] = jnp.zeros_like(dva)

    live = length[0]

    @pl.when(qb * BLOCK >= live)
    def _():
        dq[...] = jnp.zeros_like(dq)

    @pl.when(qb * BLOCK < live)
    def _():
        qt, dot_ = q[...], do[...]
        lane = lax.broadcasted_iota(jnp.int32, (BLOCK, 128), 1)
        both = (dot_.astype(F32) * o[...].astype(F32)).T
        zero = jnp.zeros((), BF)
        mine = [lane < HEAD_SIZE, lane >= HEAD_SIZE]
        qm = [jnp.where(m, qt, zero) for m in mine]
        dm = [jnp.where(m, dot_, zero) for m in mine]
        delta = [
            jnp.sum(both[:HEAD_SIZE], axis=0, keepdims=True),
            jnp.sum(both[HEAD_SIZE:], axis=0, keepdims=True),
        ]

        def step(kb, acc):
            rows = pl.ds(pl.multiple_of(kb * BLOCK, BLOCK), BLOCK)
            kpos = lax.broadcasted_iota(jnp.int32, (BLOCK, BLOCK), 0) + kb * BLOCK
            qpos = lax.broadcasted_iota(jnp.int32, (BLOCK, BLOCK), 1) + qb * BLOCK
            allowed = (kpos <= qpos) & (kpos < live)
            for u in range(2):
                g = (2 * pair + u) // share
                which = 2 * g + u
                st = mm(ks[which, rows, :], qt, NT) * scale
                pt = jnp.where(allowed, jnp.exp(st - lse[0, u : u + 1, :]), 0.0)
                dpt = mm(vs[which, rows, :], dot_, NT)
                dst = (pt * (dpt - delta[u])).astype(BF)
                dka[g, rows, :] += mm(dst, qm[u])
                dva[g, rows, :] += mm(pt.astype(BF), dm[u])
                acc += mm(kt[which, :, rows], dst)
            return acc

        last = jnp.minimum(qb + 1, (live + BLOCK - 1) // BLOCK)
        acc = lax.fori_loop(0, last, step, jnp.zeros((128, BLOCK), F32))
        dq[...] = rope(acc.T * scale, cos[...], -sin[...]).astype(BF)

    @pl.when((pair == pl.num_programs(0) - 1) & (qb == pl.num_programs(1) - 1))
    def _():
        lane = lax.broadcasted_iota(jnp.int32, (SEQUENCE_SLOTS, 128), 1)

        def joined(acc):
            both = [acc[g] + pltpu.roll(acc[g], HEAD_SIZE, 1) for g in range(2)]
            return jnp.where(lane < HEAD_SIZE, both[0], both[1])

        dk[...] = rope(joined(dka) * scale, coskv[...], -sinkv[...]).astype(BF)
        dv[...] = joined(dva).astype(BF)


def attend_back(length, q, k, v, o, do, lse, cos, sin, share):
    rows, qw = q.shape
    kw = k.shape[1]
    pairs, blocks = qw // 128, rows // BLOCK
    fix = lambda p, b, n: (0, 0)
    tile = pl.BlockSpec((BLOCK, 128), lambda p, b, n: (b, p))
    whole = pl.BlockSpec((rows, kw), fix)
    part = pl.BlockSpec((BLOCK, 128), lambda p, b, n: (b, 0))
    return pl.pallas_call(
        functools.partial(attend_back_body, share),
        grid_spec=pltpu.PrefetchScalarGridSpec(
            num_scalar_prefetch=1,
            grid=(pairs, blocks),
            in_specs=[
                tile,
                whole,
                whole,
                tile,
                tile,
                pl.BlockSpec((1, 8, BLOCK), lambda p, b, n: (p, 0, b)),
                part,
                part,
                whole,
                whole,
            ],
            out_specs=[tile, whole, whole],
            scratch_shapes=[
                pltpu.VMEM((4, rows, 128), BF),
                pltpu.VMEM((4, rows, 128), BF),
                pltpu.VMEM((4, 128, rows), BF),
                pltpu.VMEM((2, rows, 128), F32),
                pltpu.VMEM((2, rows, 128), F32),
            ],
        ),
        out_shape=[
            jax.ShapeDtypeStruct((rows, qw), BF),
            jax.ShapeDtypeStruct((rows, kw), BF),
            jax.ShapeDtypeStruct((rows, kw), BF),
        ],
        compiler_params=params(32),
        name="attend_back",
    )(length, q, k, v, o, do, lse, cos, sin, cos, sin)


NB = 8


def local_slots(table, first, local):
    at = (lax.broadcasted_iota(jnp.int32, (local, BLOCK), 0) + first).astype(F32)
    slot = jnp.full((local, BLOCK), -1.0, F32)
    gate = jnp.zeros((local, BLOCK), F32)
    for k in range(TOP):
        row = table[k : k + 1, :]
        here = row[:, :BLOCK] == at
        slot = jnp.where(here, row[:, BLOCK : 2 * BLOCK], slot)
        gate = jnp.where(here, row[:, 2 * BLOCK : 3 * BLOCK] + row[:, 3 * BLOCK :], gate)
    return slot, gate


def one_hot(slot, cap):
    at = lax.broadcasted_iota(jnp.int32, (cap, BLOCK), 0).astype(F32)
    return jnp.concatenate(
        [jnp.where(at == slot[e : e + 1, :], 1.0, 0.0) for e in range(slot.shape[0])], axis=0
    )


def load_plane(own, sib, buf, sem):
    return [
        pltpu.make_async_copy(
            ref.at[n % 4, pl.ds(0, BLOCK), :], buf.at[n], sem.at[n]
        )
        for n in range(NB)
        for ref in (own if n < 4 else sib,)
    ]


def gather_pair(i, buf, hots, out, local, cap):
    width = buf.shape[2]
    cut = width // 3
    rows = pl.ds(pl.multiple_of(i * 2 * cap, 16), 2 * cap)
    for c in range(3):
        cols = slice(c * cut, (c + 1) * cut)
        got = [mm(hots[j], buf[2 * i + j, :, cols]) for j in range(2)]
        for e in range(local):
            mine = [g[e * cap : (e + 1) * cap, :] for g in got]
            out[e, rows, cols] = jnp.concatenate(mine, axis=0).astype(BF)


def seed_body(cap, plane, fresh, first, own, sib, *refs):
    down = refs[0]
    s_out, u_out, tab, buf, s_scr, d_scr, t_scr, sem, t_sem = refs[1 if fresh else 2 :]
    local = d_scr.shape[0]
    copies = load_plane(own, sib, buf, sem)
    for n in range(NB):
        ref = (own if n < 4 else sib).at[n % 4, pl.ds(BLOCK, TOP), :]
        copies.append(pltpu.make_async_copy(ref, t_scr.at[n], t_sem.at[n]))
    weights = pltpu.make_async_copy(down, d_scr, sem.at[NB + 2])
    for c in copies:
        c.start()
    weights.start()
    for c in copies:
        c.wait()
    for n in range(NB):
        tab[n] = t_scr[n, :, : 4 * BLOCK].astype(F32)

    def gather(i, _):
        hots = []
        for j in range(2):
            slot, _g = local_slots(tab[2 * i + j], first[0], local)
            hots.append(one_hot(slot, cap).astype(BF))
        gather_pair(i, buf, hots, s_scr, local, cap)
        return 0

    lax.fori_loop(0, NB // 2, gather, 0, unroll=2)
    rows = NB * cap
    keep = pltpu.make_async_copy(s_scr, s_out.at[:, pl.ds(plane * rows, rows), :], sem.at[NB + 3])
    keep.start()
    weights.wait()

    def expert(e, _):
        u_out[e] = mm(s_scr[e], d_scr[e], NT)
        return 0

    lax.fori_loop(0, local, expert, 0, unroll=4 if local % 4 == 0 else 1)
    keep.wait()


def seed_rows(plane, planes, first, own, sib, down, kept, cap):
    local, hidden, width = down.shape
    rows = NB * cap
    vm = pl.BlockSpec(memory_space=pltpu.VMEM)
    smem = pl.BlockSpec(memory_space=pltpu.SMEM)
    fresh = kept is None
    more = () if fresh else (kept,)
    return pl.pallas_call(
        functools.partial(seed_body, cap, plane, fresh),
        in_specs=[smem] + [ANY] * (3 + len(more)),
        out_specs=[ANY, vm, vm],
        out_shape=[
            jax.ShapeDtypeStruct((local, planes * rows, width), BF),
            jax.ShapeDtypeStruct((local, rows, hidden), F32),
            jax.ShapeDtypeStruct((NB, TOP, 4 * BLOCK), F32),
        ],
        scratch_shapes=[
            pltpu.VMEM((NB, BLOCK, width), BF),
            pltpu.VMEM((local, rows, width), BF),
            pltpu.VMEM((local, hidden, width), BF),
            pltpu.VMEM((NB, TOP, width), BF),
            pltpu.SemaphoreType.DMA((NB + 4,)),
            pltpu.SemaphoreType.DMA((NB,)),
        ],
        input_output_aliases={} if fresh else {4: 0},
        compiler_params=params(50),
        cost_estimate=cost(2 * rows * local * (BLOCK + hidden) * width, 2e7),
        name="seed_rows",
    )(first, own, sib, down, *more)


def main_body(cap, plane, fresh, first, tab, u, own_in, sib_in, *refs):
    wgu = refs[0]
    refs = refs[1 if fresh else 4 :]
    x_out, d_out, a_out, own, sib = refs[:5]
    buf, x_scr, w_scr, z_scr, p_scr, g_scr, r_scr, d_scr, a_scr, m_scr, sem, out_sem = refs[5:]
    local, hidden = a_scr.shape[0], a_scr.shape[2]
    rows = NB * cap
    slots = local * cap
    copies = load_plane(own_in, sib_in, buf, sem)
    weights = pltpu.make_async_copy(wgu, w_scr, sem.at[NB + 2])
    for c in copies:
        c.start()
    weights.start()
    for c in copies:
        c.wait()

    def gather(i, _):
        hots = []
        for j in range(2):
            b = 2 * i + j
            slot, gate = local_slots(tab[b], first[0], local)
            hot = one_hot(slot, cap)
            spread_gate = jnp.concatenate(
                [jnp.broadcast_to(gate[e : e + 1, :], (cap, BLOCK)) for e in range(local)], axis=0
            )
            weight = jnp.sum(hot * spread_gate, axis=1, keepdims=True)
            weight = jnp.broadcast_to(weight, (slots, hidden))
            for e in range(local):
                g_scr[e, pl.ds(b * cap, cap), :] = weight[e * cap : (e + 1) * cap, :]
            hots.append(hot.astype(BF))
            p_scr[b] = hots[-1]
        gather_pair(i, buf, hots, x_scr, local, cap)
        return 0

    lax.fori_loop(0, NB // 2, gather, 0, unroll=2)
    here = pl.ds(plane * rows, rows)
    keep_x = pltpu.make_async_copy(x_scr, x_out.at[:, here, :], sem.at[NB + 3])
    keep_x.start()
    weights.wait()

    def expert(e, _):
        gu = mm(x_scr[e], w_scr[e])
        gate, up = gu[:, :hidden], gu[:, hidden:]
        sig = 1.0 / (1.0 + jnp.exp(-gate))
        silu = gate * sig
        act = (silu * up).astype(BF).astype(F32)
        ue = u[e]
        w = g_scr[e]
        inner = w * ue
        dg = inner * up * sig * (1.0 + gate * (1.0 - sig))
        d = jnp.concatenate([dg, inner * silu], axis=1).astype(BF)
        d_scr[e] = d
        a_scr[e] = (act * w).astype(BF)
        r_scr[e] = act * ue
        z_scr[e] = mm(d, w_scr[e], NT)
        return 0

    lax.fori_loop(0, local, expert, 0, unroll=4 if local % 4 == 0 else 1)
    keep_d = pltpu.make_async_copy(d_scr, d_out.at[:, here, :], sem.at[NB + 4])
    keep_a = pltpu.make_async_copy(a_scr, a_out.at[:, here, :], sem.at[NB + 5])
    keep_d.start()
    keep_a.start()

    for half, out in ((1, sib), (0, own)):

        def combine(i, _):
            b = 4 * half + i
            at = pl.ds(b * cap, cap)
            zb = z_scr[:, at, :].reshape(slots, -1).astype(BF)
            m_scr[b, :BLOCK, :] = mm(p_scr[b], zb, TN).astype(BF)
            pair = jnp.sum(r_scr[:, at, :].reshape(slots, hidden), axis=1, keepdims=True)
            hot = p_scr[b].astype(F32) * pair
            per = jnp.concatenate(
                [
                    jnp.sum(hot[e * cap : (e + 1) * cap, :], axis=0, keepdims=True)
                    for e in range(local)
                ],
                axis=0,
            )
            ids = (lax.broadcasted_iota(jnp.int32, (local, BLOCK), 0) + first[0]).astype(F32)
            pairs = []
            for k in range(TOP):
                mine = tab[b, k : k + 1, :BLOCK] == ids
                pairs.append(jnp.sum(jnp.where(mine, per, 0.0), axis=0, keepdims=True))
            tail = jnp.zeros((TOP, m_scr.shape[2] - BLOCK), F32)
            pairs = jnp.concatenate([jnp.concatenate(pairs, axis=0), tail], axis=1)
            m_scr[b, BLOCK:, :] = pairs.astype(BF)
            pltpu.make_async_copy(m_scr.at[b], out.at[i], out_sem.at[b]).start()
            return 0

        lax.fori_loop(0, 4, combine, 0, unroll=2)
    for half, out in ((1, sib), (0, own)):
        for i in range(4):
            b = 4 * half + i
            pltpu.make_async_copy(m_scr.at[b], out.at[i], out_sem.at[b]).wait()
    keep_x.wait()
    keep_d.wait()
    keep_a.wait()


def expert_rows(plane, planes, first, tab, u, own, sib, wgu, kept, cap):
    local, width, two = wgu.shape
    hidden = two // 2
    rows = NB * cap
    vm = pl.BlockSpec(memory_space=pltpu.VMEM)
    smem = pl.BlockSpec(memory_space=pltpu.SMEM)
    fresh = kept is None
    more = () if fresh else tuple(kept)
    total = planes * rows
    return pl.pallas_call(
        functools.partial(main_body, cap, plane, fresh),
        in_specs=[smem, vm, vm] + [ANY] * (3 + len(more)),
        out_specs=[ANY] * 5,
        out_shape=[
            jax.ShapeDtypeStruct((local, total, width), BF),
            jax.ShapeDtypeStruct((local, total, two), BF),
            jax.ShapeDtypeStruct((local, total, hidden), BF),
            jax.ShapeDtypeStruct((4, BLOCK + TOP, width), BF),
            jax.ShapeDtypeStruct((4, BLOCK + TOP, width), BF),
        ],
        scratch_shapes=[
            pltpu.VMEM((NB, BLOCK, width), BF),
            pltpu.VMEM((local, rows, width), BF),
            pltpu.VMEM((local, width, two), BF),
            pltpu.VMEM((local, rows, width), F32),
            pltpu.VMEM((NB, local * cap, BLOCK), BF),
            pltpu.VMEM((local, rows, hidden), F32),
            pltpu.VMEM((local, rows, hidden), F32),
            pltpu.VMEM((local, rows, two), BF),
            pltpu.VMEM((local, rows, hidden), BF),
            pltpu.VMEM((NB, BLOCK + TOP, width), BF),
            pltpu.SemaphoreType.DMA((NB + 6,)),
            pltpu.SemaphoreType.DMA((NB,)),
        ],
        input_output_aliases={} if fresh else {6: 0, 7: 1, 8: 2},
        compiler_params=params(60),
        cost_estimate=cost(2 * rows * local * (2 * BLOCK + 2 * two) * width, 3e7),
        name="expert_rows",
    )(first, tab, u, own, sib, wgu, *more)


def mix_body(cap, plane, first, tab, a, down, own, sib, y_scr, m_scr, a_scr, sem, out_sem):
    local = down.shape[0]
    slots = local * cap
    rows = NB * cap
    load = pltpu.make_async_copy(a.at[:, pl.ds(plane * rows, rows), :], a_scr, sem)
    load.start()
    load.wait()

    def expert(e, _):
        y_scr[e] = mm(a_scr[e], down[e])
        return 0

    lax.fori_loop(0, local, expert, 0, unroll=4 if local % 4 == 0 else 1)
    for half, out in ((1, sib), (0, own)):

        def combine(i, _):
            b = 4 * half + i
            slot, _g = local_slots(tab[b], first[0], local)
            hot = one_hot(slot, cap).astype(BF)
            yb = y_scr[:, pl.ds(b * cap, cap), :].reshape(slots, -1).astype(BF)
            m_scr[b] = mm(hot, yb, TN).astype(BF)
            pltpu.make_async_copy(m_scr.at[b], out.at[i], out_sem.at[b]).start()
            return 0

        lax.fori_loop(0, 4, combine, 0, unroll=2)
    for half, out in ((1, sib), (0, own)):
        for i in range(4):
            b = 4 * half + i
            pltpu.make_async_copy(m_scr.at[b], out.at[i], out_sem.at[b]).wait()


def mix_rows(plane, first, tab, a, down, cap):
    local, hidden, width = down.shape
    rows = NB * cap
    vm = pl.BlockSpec(memory_space=pltpu.VMEM)
    return pl.pallas_call(
        functools.partial(mix_body, cap, plane),
        in_specs=[pl.BlockSpec(memory_space=pltpu.SMEM), vm, ANY, vm],
        out_specs=[ANY, ANY],
        out_shape=[jax.ShapeDtypeStruct((4, BLOCK, width), BF)] * 2,
        scratch_shapes=[
            pltpu.VMEM((local, rows, width), F32),
            pltpu.VMEM((NB, BLOCK, width), BF),
            pltpu.VMEM((local, rows, hidden), BF),
            pltpu.SemaphoreType.DMA(()),
            pltpu.SemaphoreType.DMA((NB,)),
        ],
        compiler_params=params(50),
        cost_estimate=cost(2 * rows * local * (BLOCK + hidden) * width, 2e7),
        name="mix_rows",
    )(first, tab, a, down)


def round_body(turn, up, down, wgu, low):
    hidden = low.shape[1]
    for part in range(2):
        wgu[0, :, part * hidden : (part + 1) * hidden] = up[part, 0].astype(BF)
    low[0] = down[0].astype(BF)


def round_weights(turn, up, down):
    local, hidden, width = down.shape
    return pl.pallas_call(
        round_body,
        grid=(local,),
        in_specs=[
            pl.BlockSpec(memory_space=pltpu.SMEM),
            pl.BlockSpec((2, 1, width, hidden), lambda e: (0, e, 0, 0)),
            pl.BlockSpec((1, hidden, width), lambda e: (e, 0, 0)),
        ],
        out_specs=[
            pl.BlockSpec((1, width, 2 * hidden), lambda e: (e, 0, 0)),
            pl.BlockSpec((1, hidden, width), lambda e: (e, 0, 0)),
        ],
        out_shape=[
            jax.ShapeDtypeStruct((local, width, 2 * hidden), BF),
            jax.ShapeDtypeStruct((local, hidden, width), BF),
        ],
        compiler_params=params(32),
        cost_estimate=cost(0, 28e6),
        name="round_weights",
    )(turn, up, down)


def weights_body(older, turn, x, s, d, a, *refs):
    hidden = a.shape[2]
    ins, outs = refs[:6], refs[6 + older :]
    done = outs[-1]
    done[0] = turn[0]
    dgu = mm(d[0], x[0], TN).T
    for part in range(2):
        grad = dgu[:, part * hidden : (part + 1) * hidden]
        w, mean, sq = (r[part, 0] for r in ins[:3])
        for ref, val in zip(outs[:4], adam_step(w, grad, mean, sq, WEIGHT_DECAY)):
            ref[part, 0] = val
    ddown = mm(a[0], s[0], TN)
    w, mean, sq = (r[0] for r in ins[3:6])
    for ref, val in zip(outs[4:8], adam_step(w, ddown, mean, sq, WEIGHT_DECAY)):
        ref[0] = val


def weights_step(turn, begin, count, x, s, d, a, up, down, older, cuts=2):
    local, rows, width = x.shape
    hidden = a.shape[2]
    part = width // cuts
    wide = pl.BlockSpec((1, rows, part), lambda e, j: (e + begin, 0, j))
    slim = lambda n: pl.BlockSpec((1, rows, n), lambda e, j: (e + begin, 0, 0))
    ups = pl.BlockSpec((2, 1, part, hidden), lambda e, j: (0, e + begin, j, 0))
    downs = pl.BlockSpec((1, hidden, part), lambda e, j: (e + begin, 0, j))
    smem = pl.BlockSpec(memory_space=pltpu.SMEM)
    out = pl.pallas_call(
        functools.partial(weights_body, len(older)),
        grid=(count, cuts),
        in_specs=[smem, wide, wide, slim(2 * hidden), slim(hidden)]
        + [ups] * 3
        + [downs] * 3
        + [ANY] * len(older),
        out_specs=[ups] * 4 + [downs] * 4 + [smem],
        out_shape=[jax.ShapeDtypeStruct(up[0].shape, F32)] * 4
        + [jax.ShapeDtypeStruct(down[0].shape, F32)] * 4
        + [jax.ShapeDtypeStruct((1,), jnp.int32)],
        input_output_aliases={11 + i: i for i in range(len(older))},
        compiler_params=params(),
        cost_estimate=cost(2 * count * rows * width * 3 * hidden, 26e6 * count),
        name="weights_step",
    )(turn, x, s, d, a, *up, *down, *older)
    return list(out[:8]), out[8]


def experts_by_slot(
    moe_in, cotangent, live_rows, target, gate_values, lengths, up, down, capacity, data_size
):
    tensor_size = lax.axis_size("tensor")
    own_rows, model_width = moe_in.shape
    upgate_low, downproj_low = up[0].astype(BF), down[0].astype(BF)
    local_blocks = upgate_low.shape[1]
    expert_total = local_blocks * data_size
    slots = local_blocks * capacity
    kept = target >= 0
    put_at = jnp.where(kept, target, expert_total * capacity)
    fetch_at = jnp.where(kept, target, 0)
    pair_weight = jnp.where(kept, gate_values.reshape(-1), 0.0)

    def send(pair_rows):
        empty = jnp.zeros((expert_total * capacity, model_width), BF)
        filled = empty.at[put_at].set(pair_rows, mode="drop")
        filled = filled.reshape(1, data_size, slots, model_width)
        wide = lax.all_gather(filled, "tensor", axis=0, tiled=True)
        wide = lax.all_to_all(wide, "dp", split_axis=1, concat_axis=1, tiled=True)
        return wide.reshape(tensor_size, data_size, local_blocks, capacity, model_width)

    def bring(parts):
        parts = parts.reshape(tensor_size, data_size, slots, model_width)
        wide = lax.all_to_all(parts.astype(BF), "dp", split_axis=1, concat_axis=1, tiled=True)
        wide = lax.all_to_all(wide, "tensor", split_axis=0, concat_axis=0, tiled=True)
        summed = jnp.sum(wide.astype(F32), axis=0).astype(BF)
        return summed.reshape(expert_total * capacity, model_width)

    def dot(spec, a, b):
        return jnp.einsum(spec, a, b, preferred_element_type=F32)

    rows_in = send(jnp.repeat(moe_in, TOP, axis=0))
    gate_pre = dot("abecd,edf->abecf", rows_in, upgate_low[0])
    up_pre = dot("abecd,edf->abecf", rows_in, upgate_low[1])
    inner_act = (jax.nn.silu(gate_pre) * up_pre).astype(BF)
    pair_out = bring(dot("abecf,efd->abecd", inner_act, downproj_low))[fetch_at].astype(F32)
    mixed = jnp.sum((pair_weight[:, None] * pair_out).reshape(own_rows, TOP, model_width), axis=1)
    seed_grad = cotangent.astype(F32) * live_rows[:, None].astype(F32)
    seed_pairs = jnp.repeat(seed_grad, TOP, axis=0)
    gate_grad = jnp.where(kept, jnp.sum(pair_out * seed_pairs, axis=1), 0.0)
    out_seed = send((pair_weight[:, None] * seed_pairs).astype(BF))
    inner_grad = dot("abecd,efd->abecf", out_seed, downproj_low)
    down_grad = dot("abecf,abecd->efd", inner_act, out_seed)
    sig = jax.nn.sigmoid(gate_pre)
    gate_back = (inner_grad * up_pre * sig * (1.0 + gate_pre * (1.0 - sig))).astype(BF)
    up_back = (inner_grad * gate_pre * sig).astype(BF)
    up_grad = jnp.stack(
        [
            dot("abecd,abecf->edf", rows_in, gate_back),
            dot("abecd,abecf->edf", rows_in, up_back),
        ]
    )
    rows_grad = dot("abecf,edf->abecd", gate_back, upgate_low[0])
    rows_grad = rows_grad + dot("abecf,edf->abecd", up_back, upgate_low[1])
    back = bring(rows_grad)[fetch_at].astype(F32)
    back = jnp.where(kept[:, None], back, 0.0)
    moe_grad = jnp.sum(back.reshape(own_rows, TOP, model_width), axis=1)
    return (
        mixed,
        gate_grad.reshape(own_rows, TOP),
        moe_grad,
        adam_step(up[0], up_grad, *up[1:], WEIGHT_DECAY),
        adam_step(down[0], down_grad, *down[1:], WEIGHT_DECAY),
    )


def flip(v, axis, bit):
    return lax.ppermute(v, axis, [(i, i ^ bit) for i in range(lax.axis_size(axis))])


def core(v):
    return flip(v, "tensor", 1)


def across(v):
    return flip(v, "tensor", 2)


def side(v):
    return flip(v, "dp", 1)


def onward(v, planes=1):
    n = lax.axis_size("dp")
    return lax.ppermute(v, "dp", [(i, (i + 2 * planes) % n) for i in range(n)])


def plus(*vs):
    return functools.reduce(lambda a, b: a + b, [v.astype(F32) for v in vs]).astype(BF)


def meet(*vs):
    return lax.optimization_barrier(vs)


class Spread:
    def __init__(self, own):
        self.z, self.x, self.y, self.d, self.own, self.sib = {0: own}, {}, {}, {}, {}, {}

    def on(self, r):
        self.z[r] = onward(self.z[r - 1])

    def x_(self, r):
        self.x[r] = across(self.z[r])

    def y_(self, r):
        self.y[r] = side(self.z[r])

    def x_on(self, r):
        self.x[r] = onward(self.x[r - 1])

    def y_on(self, r):
        self.y[r] = onward(self.y[r - 1])

    def d_(self, r):
        self.d[r] = across(self.y[r]) if r % 2 else side(self.x[r])

    def cores(self, r):
        self.own[r] = jnp.stack([self.z[r], self.x[r], self.y[r], self.d.pop(r)])
        self.sib[r] = core(self.own[r])

    def state(self):
        return [self.z, self.x, self.y, self.d, self.own, self.sib]

    def put(self, state):
        self.z, self.x, self.y, self.d, self.own, self.sib = state


class Reduce:
    def __init__(self):
        self.own, self.sib, self.parts, self.d = {}, {}, {}, {}
        self.wx, self.wy, self.zx, self.zy, self.total = {}, {}, {}, {}, {}

    def cores(self, r):
        own, came = self.own.pop(r), core(self.sib.pop(r))
        self.parts[r] = [plus(own[i], came[i]) for i in range(4)]

    def part(self, r, i):
        vs = [self.parts[r][i]]
        if i == (2 if r % 2 else 1) and r in self.d:
            vs.append(self.d[r])
        if r == 0 and i == 1:
            vs.append(self.zx[1])
        if r == 0 and i == 2:
            vs.append(self.zy[1])
        return vs

    def d_(self, r):
        v = plus(*self.part(r, 3))
        self.d[r] = across(v) if r % 2 else side(v)

    def x_(self, r):
        self.wx[r] = across(plus(*self.part(r, 1)))

    def y_(self, r):
        self.wy[r] = side(plus(*self.part(r, 2)))

    def x_in(self, r):
        self.zx[r] = onward(plus(*self.part(r, 1)), -1)

    def y_in(self, r):
        self.zy[r] = onward(plus(*self.part(r, 2)), -1)

    def plane(self, r):
        vs = self.part(r, 0)
        vs = vs + [w.pop(r) for w in (self.wx, self.wy, self.total) if r in w]
        return functools.reduce(lambda a, b: a + b, [v.astype(F32) for v in vs])

    def on(self, r, count):
        self.total[(r + 1) % count] = onward(self.plane(r).astype(BF))

    def state(self):
        return [
            self.own, self.sib, self.parts, self.d,
            self.wx, self.wy, self.zx, self.zy, self.total,
        ]

    def put(self, state):
        (
            self.own, self.sib, self.parts, self.d,
            self.wx, self.wy, self.zx, self.zy, self.total,
        ) = state


def data_parts(part):
    n = lax.axis_size("dp")
    me = lax.axis_index("dp")
    planes = n // 2
    pairs = part.reshape((planes, 2, part.shape[0] // n) + part.shape[1:])
    mine = lax.dynamic_index_in_dim(pairs, me % 2, 1, keepdims=False)
    other = lax.dynamic_index_in_dim(pairs, 1 - me % 2, 1, keepdims=False)
    order = [((me // 2) + planes - r) % planes for r in range(planes)]
    at = lambda a, r: lax.dynamic_index_in_dim(a, order[r], 0, keepdims=False)
    return tuple(jnp.stack([at(a, r) for r in range(planes)]) for a in (mine, other))


def pack_weights(query_weight, keyvalue_matrix, outproj_weight, norm_gains):
    return jnp.concatenate(
        [
            query_weight.astype(BF),
            keyvalue_matrix[0].astype(BF),
            keyvalue_matrix[1].astype(BF),
            outproj_weight.astype(BF).T,
            jnp.pad(norm_gains.astype(BF).T, ((0, 0), (0, 126))),
        ],
        axis=1,
    )


def normed(v):
    rms = lax.rsqrt(jnp.mean(v * v, axis=-1, keepdims=True) + NORM_EPS)
    return rms, v * rms


def norm_back(grad, gain, rms, norm):
    scaled = grad * gain
    return rms * (scaled - norm * jnp.mean(scaled * norm, axis=-1, keepdims=True))


def few_groups(
    hidden_in, cotangent, lengths, routes, gate_values, target, live_rows, capacity,
    query_weight, keyvalue_matrix, outproj_weight, norm_gains, up, down,
):
    tensor_index, me = lax.axis_index("tensor"), lax.axis_index("dp")
    count = lax.axis_size("dp") // 2
    qw, kw = query_weight.shape[1], keyvalue_matrix.shape[2]
    share = qw // kw
    local = up[0].shape[1]
    width = hidden_in.shape[1]

    wide = qw + 2 * kw
    out_cols, in_cols = (wide, wide + qw), (0, wide)

    own_packed = pack_weights(query_weight, keyvalue_matrix, outproj_weight, norm_gains)
    w = [own_packed]
    hx, hc = across(hidden_in), core(hidden_in)
    sides = []
    for r in range(count - 1):
        sides.append(side(w[r]))
        w.append(onward(w[r]))
        w[r + 1], sides[r] = meet(w[r + 1], sides[r])
    sides.append(side(w[-1]))
    hxc = core(hx)
    places = [(me + 2 * (count - r)) % (2 * count) for r in range(count)]
    weight_places = [p for r in range(count) for p in (places[r], places[r] ^ 1)]
    at = [tensor_index ^ j for j in range(4)] + weight_places
    at = jnp.stack([jnp.asarray(p, jnp.int32) for p in at])
    cos, sin = rope_lanes(4 * BLOCK)

    seeds = jnp.where(live_rows[:, None], cotangent, jnp.zeros((), BF))
    slot = jnp.where(target >= 0, target - routes.reshape(-1) * capacity, -1).reshape(-1, TOP)
    high = gate_values.astype(BF)
    low = (gate_values - high.astype(F32)).astype(BF)
    table = jnp.concatenate([routes.astype(BF).T, slot.astype(BF).T, high.T, low.T], axis=1)
    table = jnp.pad(table, ((0, 0), (0, width - table.shape[1])))
    first = (me * local).astype(jnp.int32).reshape(1)
    c = Spread(jnp.concatenate([seeds, table], axis=0))
    c.z[0], w[2], hx = meet(c.z[0], w[2], hx)
    c.x_(0)
    c.z[0], w[3] = meet(c.z[0], w[3])
    c.on(1)

    (rows_of, w, sides, cos, sin, st) = meet(
        [hidden_in, hc, hx, hxc], w, sides, cos, sin, c.state()
    )
    c.put(st)
    weight_blocks = [b for r in range(count) for b in (w[r], sides[r])]
    attn_in, q, k, v, gains, packed = qkv(at, rows_of, weight_blocks, qw, kw, cos, sin)
    c.x_(1), c.y_(0), c.on(2)
    q, k, v, gains, st = meet(q, k, v, gains, c.state())
    c.put(st)
    gain_attn, gain_moe = gains[0:1], gains[1:2]
    heads, lse = attend(lengths, q, k, v, share)
    c.x_(2), c.d_(0), c.on(3)
    heads, st = meet(heads, c.state())
    c.put(st)
    near0, near1, far0, far1 = project(at, heads, packed, out_cols)
    far1 = core(far1)
    c.y_(1), c.cores(0)
    near0, near1, far0, far1, st, first = meet(near0, near1, far0, far1, c.state(), first)
    c.put(st)
    sent, near1 = across(plus(far0, far1)), core(near1)
    us, tabs, kept_s = {}, {}, None

    def seed(r):
        nonlocal kept_s
        kept_s, us[r], tabs[r] = seed_rows(
            r, count, first, c.own.pop(r), c.sib.pop(r), down_low, kept_s, capacity
        )

    c.y_(2)
    wgu, down_low = round_weights(first, up[0], down[0])
    sent, near0, near1, wgu, down_low, st = meet(sent, near0, near1, wgu, down_low, c.state())
    c.put(st)
    attn_own = plus(near0, near1).astype(F32) + sent.astype(F32)
    hidden = hidden_in.astype(F32)
    middle = hidden + attn_own
    rms_moe, normed_moe = normed(middle)
    m = Spread((normed_moe * gain_moe).astype(BF))
    back, mix = Reduce(), Reduce()
    kept, news, turn = None, [], first

    def expert(r):
        nonlocal kept
        x, dgu, act, back.own[r], back.sib[r] = expert_rows(
            r, count, first, tabs[r], us[r], m.own.pop(r), m.sib.pop(r), wgu, kept, capacity
        )
        kept = (x, dgu, act)

    def mixes(r):
        mix.own[r], mix.sib[r] = mix_rows(r, first, tabs[r], kept[2], down_low, capacity)

    def weights(begin, size):
        nonlocal news, turn
        news, turn = weights_step(
            turn, begin, size, kept[0], kept_s, kept[1], kept[2], up, down, news
        )

    def step():
        nonlocal first, us, tabs, turn
        first, turn, us, tabs, sc, sm, sb, sx = meet(
            first, turn, us, tabs, c.state(), m.state(), back.state(), mix.state()
        )
        c.put(sc), m.put(sm), back.put(sb), mix.put(sx)

    m.z[0], st = meet(m.z[0], c.state())
    c.put(st)
    m.x_(0), m.y_(0), m.on(1)
    seed(0)
    step()
    c.d_(1), m.d_(0), m.y_on(1)
    step()
    m.d_(1), c.d_(2), m.on(2), c.cores(1), m.cores(0)
    step()
    m.x_(2), m.y_(2), m.x_on(1), c.cores(2)
    expert(0)
    step()
    c.x_(3), m.d_(2), m.on(3), m.cores(1), back.cores(0)
    seed(1)
    seed(2)
    step()
    m.x_(3), c.y_(3), m.cores(2)
    expert(1)
    step()
    c.d_(3), m.y_(3), back.cores(1)
    expert(2)
    step()
    m.d_(3), back.d_(0), back.x_in(1), c.cores(3), back.cores(2)
    mixes(0)
    step()
    back.d_(1), back.d_(2), back.on(1, count), m.cores(3), mix.cores(0)
    seed(3)
    mixes(1)
    step()
    back.x_(2), back.y_(2), back.y_in(1), mix.cores(1)
    expert(3)
    step()
    mix.d_(1), mix.d_(0), back.on(2, count), back.cores(3)
    mixes(2)
    step()
    back.d_(3), mix.x_in(1), mix.cores(2)
    mixes(3)
    step()
    back.x_(3), back.y_(3), mix.y_in(1), mix.cores(3)
    weights(0, 2)
    step()
    back.x_(0), back.y_(0), back.on(3, count)
    weights(2, 2)
    step()
    whole = back.plane(0)
    gate_grad, moe_grad = whole[BLOCK:, :BLOCK].T, whole[:BLOCK]

    seed_grad = cotangent.astype(F32) * live_rows[:, None].astype(F32)
    gain_sum = jnp.sum(moe_grad * normed_moe, axis=0, keepdims=True)
    middle_grad = seed_grad + norm_back(moe_grad, gain_moe, rms_moe, normed_moe)
    mid, turn, st = meet(middle_grad.astype(BF), turn, mix.state())
    mix.put(st)
    mx, mc = across(mid), core(mid)
    mix.d_(2), mix.on(1, count)
    weights(4, 2)
    mx, mc, turn, st, gain_sum = meet(mx, mc, turn, mix.state(), gain_sum)
    mix.put(st)
    mxc = core(mx)
    mix.x_(0), mix.y_(0)
    gain_sum = gain_sum + flip(gain_sum, "tensor", 1)
    heads_grad, middle_low = heads_back(at, [mid, mc, mx, mxc], packed, out_cols)
    omine, oother = data_parts(mm(middle_low, heads, TN).astype(BF))
    heads_grad, omine, oother, gain_sum, st = meet(
        heads_grad, omine, oother, gain_sum, mix.state()
    )
    mix.put(st)
    dq, dk, dv = attend_back(lengths, q, k, v, heads, heads_grad, lse, cos, sin, share)
    ocame = side(oother)
    mix.d_(3), mix.x_(2), mix.y_(2)
    gain_sum = gain_sum + flip(gain_sum, "tensor", 2)
    dq, dk, dv, ocame, omine, gain_sum, st = meet(dq, dk, dv, ocame, omine, gain_sum, mix.state())
    mix.put(st)
    dqkv = jnp.concatenate([dq, dk, dv], axis=1)
    near0, near1, far0, far1 = project(at, dqkv, packed, in_cols)
    far1 = core(far1)
    osums = plus(omine, ocame)
    ohere = [osums[0]] + [onward(osums[r], -r) for r in range(1, count)]
    qmine, qother = data_parts(mm(attn_in, dqkv, TN).astype(BF))
    gain_sum = gain_sum + flip(gain_sum, "dp", 1)
    near0, near1, far0, far1, ohere, qmine, qother, gain_sum, st = meet(
        near0, near1, far0, far1, ohere, qmine, qother, gain_sum, mix.state()
    )
    mix.put(st)
    sent, near1 = across(plus(far0, far1)), core(near1)
    qcame = side(qother)
    mix.on(2, count)
    weights(6, 2)
    sent, near0, near1, qcame, qmine, turn, gain_sum, st = meet(
        sent, near0, near1, qcame, qmine, turn, gain_sum, mix.state()
    )
    mix.put(st)
    attn_grad = plus(near0, near1).astype(F32) + sent.astype(F32)
    rms_attn, normed_attn = normed(hidden)
    input_grad = middle_grad + norm_back(attn_grad, gain_attn, rms_attn, normed_attn)
    qsums = plus(qmine, qcame)
    qhere = [qsums[0]] + [onward(qsums[r], -r) for r in range(1, count)]
    mix.x_(3), mix.y_(3)
    qhere, gain_sum, st = meet(qhere, gain_sum, mix.state())
    mix.put(st)
    mix.on(3, count)
    gain_sum = gain_sum + flip(gain_sum, "dp", 2)
    gain_sum = gain_sum + flip(gain_sum, "dp", 4)
    outproj_sum = functools.reduce(lambda a, b: a + b, [o.astype(F32) for o in ohere]).T
    qkv_sum = functools.reduce(lambda a, b: a + b, [q.astype(F32) for q in qhere])
    own_gains = norm_gains.astype(BF).astype(F32)
    gain_part = jnp.sum(own_packed[:, :wide].astype(F32) * qkv_sum, axis=1)[None, :]
    gain_part = gain_part + flip(gain_part, "tensor", 1)
    gain_part = gain_part + flip(gain_part, "tensor", 2)
    own_cols = norm_gains.shape[1]
    gain_moe_own = lax.dynamic_slice_in_dim(gain_sum, me * own_cols, own_cols, 1)
    gains_sum = jnp.concatenate([gain_part / own_gains[0:1], gain_moe_own], axis=0)
    block_out = (middle + mix.plane(0)).astype(BF)
    return (
        block_out, input_grad, gate_grad, qkv_sum, outproj_sum, gains_sum,
        tuple(news[:4]), tuple(news[4:]),
    )


def many_groups(
    hidden_in, cotangent, lengths, routes, gate_values, target, live_rows, capacity,
    query_weight, keyvalue_matrix, outproj_weight, norm_gains, up, down,
):
    qw, kw = query_weight.shape[1], keyvalue_matrix.shape[2]
    share = qw // kw
    packed = pack_weights(query_weight, keyvalue_matrix, outproj_weight, norm_gains)
    packed = lax.all_gather(packed, "dp", axis=0, tiled=True)
    group = lax.all_gather(hidden_in, "tensor", axis=0, tiled=True)
    rows_of = [group[i * BLOCK : (i + 1) * BLOCK] for i in range(4)]
    at = jnp.concatenate([jnp.arange(4, dtype=jnp.int32), jnp.zeros((1,), jnp.int32)])
    cos, sin = rope_lanes(4 * BLOCK)
    attn_in, q, k, v, gains, packed = qkv(at, rows_of, [packed], qw, kw, cos, sin)
    wide = qw + 2 * kw
    qkv_low, outproj_low = packed[:, :wide], packed[:, wide : wide + qw]
    gain_attn, gain_moe = gains[0:1], gains[1:2]
    heads, lse = attend(lengths, q, k, v, share)

    def scattered(part):
        part = lax.psum_scatter(part.astype(BF), "tensor", scatter_dimension=0, tiled=True)
        return part.astype(F32)

    hidden = hidden_in.astype(F32)
    middle = hidden + scattered(mm(heads, outproj_low, NT))
    rms_moe, normed_moe = normed(middle)
    moe_in = (normed_moe * gain_moe).astype(BF)
    mixed, gate_grad, moe_grad, up_new, down_new = experts_by_slot(
        moe_in, cotangent, live_rows, target, gate_values, lengths, up, down, capacity,
        lax.axis_size("dp"),
    )
    block_out = (middle + mixed).astype(BF)
    seed_grad = cotangent.astype(F32) * live_rows[:, None].astype(F32)
    gain_moe_part = jnp.sum(moe_grad * normed_moe, axis=0)
    middle_grad = seed_grad + norm_back(moe_grad, gain_moe, rms_moe, normed_moe)
    middle_low = lax.all_gather(middle_grad.astype(BF), "tensor", axis=0, tiled=True)
    heads_grad = mm(middle_low, outproj_low).astype(BF)
    dq, dk, dv = attend_back(lengths, q, k, v, heads, heads_grad, lse, cos, sin, share)
    dqkv = jnp.concatenate([dq, dk, dv], axis=1)
    attn_grad = scattered(mm(dqkv, qkv_low, NT))
    rms_attn, normed_attn = normed(hidden)
    gain_attn_part = jnp.sum(attn_grad * normed_attn, axis=0)
    input_grad = middle_grad + norm_back(attn_grad, gain_attn, rms_attn, normed_attn)
    gains_sum = lax.psum(jnp.stack([gain_attn_part, gain_moe_part]), ("dp", "tensor"))
    own_cols = norm_gains.shape[1]
    gains_sum = lax.dynamic_slice_in_dim(gains_sum, lax.axis_index("dp") * own_cols, own_cols, 1)
    part = jnp.concatenate([mm(attn_in, dqkv, TN), mm(middle_low, heads, TN)], axis=1)
    summed = lax.psum_scatter(part, "dp", scatter_dimension=0, tiled=True)
    return (
        block_out, input_grad, gate_grad, summed[:, :wide], summed[:, wide:].T, gains_sum,
        up_new, down_new,
    )


def on_device(
    hidden_in,
    cotangent,
    lengths,
    routes,
    gate_values,
    pair_order,
    query_weight,
    keyvalue_matrix,
    outproj_weight,
    norm_gains,
    upgate_weight,
    downproj_weight,
    query_mean,
    query_sqmean,
    keyvalue_first_moment,
    keyvalue_second_moment,
    outproj_mean,
    outproj_sqmean,
    gains_mean,
    gains_sqmean,
    upgate_mean,
    upgate_sqmean,
    downproj_mean,
    downproj_sqmean,
):
    tensor_size = lax.axis_size("tensor")
    data_size = lax.axis_size("dp")
    own_rows, model_width = hidden_in.shape
    group_rows = own_rows * tensor_size
    qw = query_weight.shape[1]
    kw = keyvalue_matrix.shape[2]
    assert lengths.shape[0] == 1 and group_rows == SEQUENCE_SLOTS and own_rows == BLOCK

    tensor_index = lax.axis_index("tensor")
    row_ids = tensor_index * own_rows + jnp.arange(own_rows, dtype=jnp.int32)
    live_rows = row_ids < lengths[0]
    capacity = max(2, own_rows * TOP * 5 // (4 * upgate_weight.shape[1] * data_size))
    target = slot_targets(routes.reshape(-1), pair_order[0], jnp.repeat(live_rows, TOP), capacity)
    few = data_size * group_rows * model_width <= 1 << 24
    block_out, input_grad, gate_grad, qkv_sum, outproj_sum, gains_sum, up_new, down_new = (
        few_groups if few else many_groups
    )(
        hidden_in, cotangent, lengths, routes, gate_values, target, live_rows, capacity,
        query_weight, keyvalue_matrix, outproj_weight, norm_gains,
        (upgate_weight, upgate_mean, upgate_sqmean),
        (downproj_weight, downproj_mean, downproj_sqmean),
    )
    query_sum = qkv_sum[:, :qw]
    keyval_sum = jnp.stack([qkv_sum[:, qw : qw + kw], qkv_sum[:, qw + kw :]])
    return (
        (block_out, input_grad, gate_grad)
        + adam_step(query_weight, query_sum, query_mean, query_sqmean, WEIGHT_DECAY)
        + adam_step(
            keyvalue_matrix, keyval_sum, keyvalue_first_moment, keyvalue_second_moment, WEIGHT_DECAY
        )
        + adam_step(outproj_weight, outproj_sum, outproj_mean, outproj_sqmean, WEIGHT_DECAY)
        + adam_step(norm_gains, gains_sum, gains_mean, gains_sqmean, 0.0)
        + up_new
        + down_new
    )


def solution(mesh):
    placed = (
        P(("dp", "tensor"), None),
        P(("dp", "tensor"), None),
        P("dp"),
        P(("dp", "tensor"), None),
        P(("dp", "tensor"), None),
        P(("dp", "tensor"), None),
        P("dp", "tensor"),
        P(None, "dp", "tensor"),
        P("tensor", "dp"),
        P(None, "dp"),
        P(None, "dp", None, "tensor"),
        P("dp", "tensor", None),
        P("dp", "tensor"),
        P("dp", "tensor"),
        P(None, "dp", "tensor"),
        P(None, "dp", "tensor"),
        P("tensor", "dp"),
        P("tensor", "dp"),
        P(None, "dp"),
        P(None, "dp"),
        P(None, "dp", None, "tensor"),
        P(None, "dp", None, "tensor"),
        P("dp", "tensor", None),
        P("dp", "tensor", None),
    )
    return jax.shard_map(
        on_device,
        mesh=mesh,
        in_specs=placed,
        out_specs=(
            P(("dp", "tensor"), None),
            P(("dp", "tensor"), None),
            P(("dp", "tensor"), None),
            P("dp", "tensor"),
            P("dp", "tensor"),
            P("dp", "tensor"),
            P("dp", "tensor"),
            P(None, "dp", "tensor"),
            P(None, "dp", "tensor"),
            P(None, "dp", "tensor"),
            P(None, "dp", "tensor"),
            P("tensor", "dp"),
            P("tensor", "dp"),
            P("tensor", "dp"),
            P("tensor", "dp"),
            P(None, "dp"),
            P(None, "dp"),
            P(None, "dp"),
            P(None, "dp"),
            P(None, "dp", None, "tensor"),
            P(None, "dp", None, "tensor"),
            P(None, "dp", None, "tensor"),
            P(None, "dp", None, "tensor"),
            P("dp", "tensor", None),
            P("dp", "tensor", None),
            P("dp", "tensor", None),
            P("dp", "tensor", None),
        ),
        check_vma=False,
    )
```

```python
import functools
import jax
import jax.numpy as jnp
from jax import lax
from jax.experimental import pallas as pl
from jax.experimental.pallas import tpu as pltpu
from jax.sharding import PartitionSpec as P

HEAD_SIZE = 64
TOP = 8
SEQUENCE_SLOTS = 1024
ADAM_STEP = 5
NORM_EPS = 1e-05
ROPE_THETA = 10000.0
MASKED = -1e30
BETA_ONE = 0.9
BETA_TWO = 0.95
LEARN_RATE = 0.03
WEIGHT_DECAY = 0.1
ADAM_EPS = 1e-08
BF = jnp.bfloat16
F32 = jnp.float32
BLOCK = 256
NN = (((1,), (0,)), ((), ()))
NT = (((1,), (1,)), ((), ()))
TN = (((0,), (0,)), ((), ()))


def mm(a, b, dims=NN):
    return lax.dot_general(a, b, dims, preferred_element_type=F32)


def params(mib=58):
    return pltpu.CompilerParams(vmem_limit_bytes=mib << 20)


def adam_step(weight, gradient, first_old, second_old, decay_rate):
    first_new = BETA_ONE * first_old + (1.0 - BETA_ONE) * gradient
    second_new = BETA_TWO * second_old + (1.0 - BETA_TWO) * gradient * gradient
    first_hat = first_new / (1.0 - BETA_ONE**ADAM_STEP)
    second_hat = second_new / (1.0 - BETA_TWO**ADAM_STEP)
    update = -LEARN_RATE * (first_hat / (jnp.sqrt(second_hat) + ADAM_EPS) + decay_rate * weight)
    return (gradient, first_new, second_new, update)


def rank_body(cap, ecol, ocol, erow, orow, out):
    pairs = erow.shape[1]
    step = 64
    er, orr = erow[...], orow[...]

    def chunk(i, acc):
        rows = pl.ds(i * step, step)
        hit = (ecol[rows, :] == er) & (ocol[rows, :] < orr)
        return acc + jnp.sum(hit.astype(jnp.int32), axis=0, keepdims=True)

    rank = lax.fori_loop(0, pairs // step, chunk, jnp.zeros((1, pairs), jnp.int32))
    kept = (orr < pairs) & (rank < cap)
    out[...] = jnp.where(kept, er * cap + rank, -1)


def slot_targets(experts, order, live_pairs, cap):
    pairs = experts.shape[0]
    order = jnp.where(live_pairs, order, pairs)
    return pl.pallas_call(
        functools.partial(rank_body, cap),
        out_shape=jax.ShapeDtypeStruct((1, pairs), jnp.int32),
        compiler_params=params(16),
        name="slot_targets",
    )(experts[:, None], order[:, None], experts[None, :], order[None, :])[0]


def swap_halves(u):
    width = u.shape[1]
    lane = lax.broadcasted_iota(jnp.int32, u.shape, 1) % HEAD_SIZE
    half = HEAD_SIZE // 2
    return jnp.where(lane < half, pltpu.roll(u, width - half, 1), pltpu.roll(u, half, 1))


def rope(u, cos, sin):
    reps = u.shape[1] // cos.shape[1]
    if reps > 1:
        cos = jnp.concatenate([cos] * reps, axis=1)
        sin = jnp.concatenate([sin] * reps, axis=1)
    return u * cos + swap_halves(u) * sin


def rope_lanes(rows):
    lane = jnp.arange(128) % HEAD_SIZE
    half = HEAD_SIZE // 2
    positions = (jnp.arange(rows) % SEQUENCE_SLOTS).astype(F32)
    freqs = ROPE_THETA ** (-(2.0 * (lane % half).astype(F32)) / HEAD_SIZE)
    angles = positions[:, None] * freqs[None, :]
    return jnp.cos(angles), jnp.where(lane < half, -1.0, 1.0) * jnp.sin(angles)


ANY = pl.BlockSpec(memory_space=pltpu.HBM)


def cost(flops, nbytes):
    return pl.CostEstimate(flops=int(flops), bytes_accessed=int(nbytes), transcendentals=0)


def qkv_body(qw, kw, xn, wn, at, *refs):
    xs, ws, refs = refs[:xn], refs[xn : xn + wn], refs[xn + wn :]
    cos, sin, a_out, q_out, k_out, v_out, gains, w_out, x_scr, sem = refs
    step = ws[0].shape[0]
    copies = []
    for i, ref in enumerate(ws):
        rows = pl.ds(pl.multiple_of(at[xn + i] * step, 16), step)
        copies.append(pltpu.make_async_copy(ref, w_out.at[rows, :], sem.at[xn + i]))
    for i, ref in enumerate(xs):
        rows = pl.ds(pl.multiple_of(at[i] * BLOCK, BLOCK), BLOCK)
        copies.append(pltpu.make_async_copy(ref, x_scr.at[rows, :], sem.at[i]))
    for c in copies:
        c.start()
    for c in copies:
        c.wait()
    wide = qw + 2 * kw
    gains[...] = w_out[:, wide + qw :].astype(F32).T[0:8, :]

    def block(i, _):
        rows = pl.ds(pl.multiple_of(i * BLOCK, BLOCK), BLOCK)
        v = x_scr[rows, :].astype(F32)
        r = lax.rsqrt(jnp.mean(v * v, axis=-1, keepdims=True) + NORM_EPS)
        a = (v * r * gains[0:1, :]).astype(BF)
        a_out[rows, :] = a
        y = mm(a, w_out[:, :wide])
        c, s = cos[rows, :], sin[rows, :]
        q_out[rows, :] = rope(y[:, :qw], c, s).astype(BF)
        k_out[rows, :] = rope(y[:, qw : qw + kw], c, s).astype(BF)
        v_out[rows, :] = y[:, qw + kw :].astype(BF)
        return 0

    lax.fori_loop(0, len(xs), block, 0)


def qkv(at, xs, ws, qw, kw, cos, sin):
    rows, width = BLOCK * len(xs), xs[0].shape[1]
    cols = ws[0].shape[1]
    depth = ws[0].shape[0] * len(ws)
    vm = pl.BlockSpec(memory_space=pltpu.VMEM)
    return pl.pallas_call(
        functools.partial(qkv_body, qw, kw, len(xs), len(ws)),
        in_specs=[pl.BlockSpec(memory_space=pltpu.SMEM)]
        + [ANY] * (len(xs) + len(ws))
        + [vm, vm],
        out_specs=[vm] * 6,
        out_shape=[
            jax.ShapeDtypeStruct((rows, width), BF),
            jax.ShapeDtypeStruct((rows, qw), BF),
            jax.ShapeDtypeStruct((rows, kw), BF),
            jax.ShapeDtypeStruct((rows, kw), BF),
            jax.ShapeDtypeStruct((8, width), F32),
            jax.ShapeDtypeStruct((depth, cols), BF),
        ],
        scratch_shapes=[
            pltpu.VMEM((rows, width), BF),
            pltpu.SemaphoreType.DMA((len(xs) + len(ws),)),
        ],
        compiler_params=params(60),
        cost_estimate=cost(2 * rows * width * cols, 2e7),
        name="qkv",
    )(at, *xs, *ws, cos, sin)


def project_body(cols, at, v, w, *outs):
    for i, out in enumerate(outs):
        rows = pl.ds(pl.multiple_of(at[i] * BLOCK, BLOCK), BLOCK)
        out[...] = mm(v[rows, :], w[:, cols[0] : cols[1]], NT).astype(BF)


def project(at, v, w, cols):
    rows, depth = v.shape
    width = w.shape[0]
    vm = pl.BlockSpec(memory_space=pltpu.VMEM)
    return pl.pallas_call(
        functools.partial(project_body, cols),
        in_specs=[pl.BlockSpec(memory_space=pltpu.SMEM), vm, vm],
        out_specs=[vm] * 4,
        out_shape=[jax.ShapeDtypeStruct((BLOCK, width), BF)] * 4,
        compiler_params=params(32),
        cost_estimate=cost(2 * rows * depth * width, 1e7),
        name="project",
    )(at, v, w)


def heads_back_body(cols, at, m0, m1, m2, m3, w, h_out, m_out, sem):
    copies = []
    for i, ref in enumerate((m0, m1, m2, m3)):
        rows = pl.ds(pl.multiple_of(at[i] * BLOCK, BLOCK), BLOCK)
        copies.append(pltpu.make_async_copy(ref, m_out.at[rows, :], sem.at[i]))
    for c in copies:
        c.start()
    for c in copies:
        c.wait()

    def block(i, _):
        rows = pl.ds(pl.multiple_of(i * BLOCK, BLOCK), BLOCK)
        h_out[rows, :] = mm(m_out[rows, :], w[:, cols[0] : cols[1]]).astype(BF)
        return 0

    lax.fori_loop(0, 4, block, 0)


def heads_back(at, ms, w, cols):
    width, qw = w.shape[0], cols[1] - cols[0]
    rows = 4 * BLOCK
    vm = pl.BlockSpec(memory_space=pltpu.VMEM)
    return pl.pallas_call(
        functools.partial(heads_back_body, cols),
        in_specs=[pl.BlockSpec(memory_space=pltpu.SMEM)] + [ANY] * 4 + [vm],
        out_specs=[vm, vm],
        out_shape=[
            jax.ShapeDtypeStruct((rows, qw), BF),
            jax.ShapeDtypeStruct((rows, width), BF),
        ],
        scratch_shapes=[pltpu.SemaphoreType.DMA((4,))],
        compiler_params=params(32),
        cost_estimate=cost(2 * rows * qw * width, 1e7),
        name="heads_back",
    )(at, *ms, w)


def spread(pair_lanes, out):
    lane = lax.broadcasted_iota(jnp.int32, pair_lanes.shape, 1)
    full = pair_lanes.astype(F32)
    first = jnp.where(lane < HEAD_SIZE, full, 0.0)
    second = jnp.where(lane < HEAD_SIZE, 0.0, full)
    out[0] = first.astype(BF)
    out[1] = pltpu.roll(first, HEAD_SIZE, 1).astype(BF)
    out[2] = pltpu.roll(second, HEAD_SIZE, 1).astype(BF)
    out[3] = second.astype(BF)


def attend_body(share, length, q, k, v, o, lse, ks, vs):
    pair, qb = pl.program_id(0), pl.program_id(1)

    @pl.when((pair == 0) & (qb == 0))
    def _():
        spread(k[...], ks)
        spread(v[...], vs)

    scale = HEAD_SIZE**-0.5
    for j in range(SEQUENCE_SLOTS // BLOCK):

        @pl.when(qb == j)
        def _():
            keys = (j + 1) * BLOCK
            kpos = lax.broadcasted_iota(jnp.int32, (BLOCK, keys), 1)
            qpos = lax.broadcasted_iota(jnp.int32, (BLOCK, keys), 0) + j * BLOCK
            allowed = (kpos <= qpos) & (kpos < length[0])
            total = jnp.zeros((BLOCK, 128), F32)
            for u in range(2):
                which = 2 * ((2 * pair + u) // share) + u
                s = mm(q[...], ks[which, :keys, :], NT) * scale
                s = jnp.where(allowed, s, MASKED)
                top = jnp.max(s, axis=-1, keepdims=True)
                e = jnp.exp(s - top)
                den = jnp.sum(e, axis=-1, keepdims=True)
                total += mm(e.astype(BF), vs[which, :keys, :]) / den
                full = jnp.broadcast_to(top + jnp.log(den), (BLOCK, 128))
                lse[0, u : u + 1, :] = full.T[0:1, :]
            o[...] = total.astype(BF)


def attend(length, q, k, v, share):
    rows, qw = q.shape
    kw = k.shape[1]
    assert kw == 128 and rows == SEQUENCE_SLOTS
    pairs = qw // 128
    blocks = rows // BLOCK
    fix = lambda p, b, n: (0, 0)
    return pl.pallas_call(
        functools.partial(attend_body, share),
        grid_spec=pltpu.PrefetchScalarGridSpec(
            num_scalar_prefetch=1,
            grid=(pairs, blocks),
            in_specs=[
                pl.BlockSpec((BLOCK, 128), lambda p, b, n: (b, p)),
                pl.BlockSpec((rows, kw), fix),
                pl.BlockSpec((rows, kw), fix),
            ],
            out_specs=[
                pl.BlockSpec((BLOCK, 128), lambda p, b, n: (b, p)),
                pl.BlockSpec((1, 8, BLOCK), lambda p, b, n: (p, 0, b)),
            ],
            scratch_shapes=[pltpu.VMEM((4, rows, 128), BF), pltpu.VMEM((4, rows, 128), BF)],
        ),
        out_shape=[
            jax.ShapeDtypeStruct((rows, qw), BF),
            jax.ShapeDtypeStruct((pairs, 8, rows), F32),
        ],
        compiler_params=params(32),
        name="attend",
    )(length, q, k, v)


def attend_back_body(
    share, length, q, k, v, o, do, lse, cos, sin, coskv, sinkv, dq, dk, dv, ks, vs, kt, dka, dva
):
    pair, qb = pl.program_id(0), pl.program_id(1)
    scale = HEAD_SIZE**-0.5

    @pl.when((pair == 0) & (qb == 0))
    def _():
        spread(k[...], ks)
        spread(v[...], vs)
        for i in range(4):
            kt[i] = ks[i].astype(F32).T.astype(BF)
        dka[...] = jnp.zeros_like(dka)
        dva[...] = jnp.zeros_like(dva)

    live = length[0]

    @pl.when(qb * BLOCK >= live)
    def _():
        dq[...] = jnp.zeros_like(dq)

    @pl.when(qb * BLOCK < live)
    def _():
        qt, dot_ = q[...], do[...]
        lane = lax.broadcasted_iota(jnp.int32, (BLOCK, 128), 1)
        both = (dot_.astype(F32) * o[...].astype(F32)).T
        zero = jnp.zeros((), BF)
        mine = [lane < HEAD_SIZE, lane >= HEAD_SIZE]
        qm = [jnp.where(m, qt, zero) for m in mine]
        dm = [jnp.where(m, dot_, zero) for m in mine]
        delta = [
            jnp.sum(both[:HEAD_SIZE], axis=0, keepdims=True),
            jnp.sum(both[HEAD_SIZE:], axis=0, keepdims=True),
        ]

        def step(kb, acc):
            rows = pl.ds(pl.multiple_of(kb * BLOCK, BLOCK), BLOCK)
            kpos = lax.broadcasted_iota(jnp.int32, (BLOCK, BLOCK), 0) + kb * BLOCK
            qpos = lax.broadcasted_iota(jnp.int32, (BLOCK, BLOCK), 1) + qb * BLOCK
            allowed = (kpos <= qpos) & (kpos < live)
            for u in range(2):
                g = (2 * pair + u) // share
                which = 2 * g + u
                st = mm(ks[which, rows, :], qt, NT) * scale
                pt = jnp.where(allowed, jnp.exp(st - lse[0, u : u + 1, :]), 0.0)
                dpt = mm(vs[which, rows, :], dot_, NT)
                dst = (pt * (dpt - delta[u])).astype(BF)
                dka[g, rows, :] += mm(dst, qm[u])
                dva[g, rows, :] += mm(pt.astype(BF), dm[u])
                acc += mm(kt[which, :, rows], dst)
            return acc

        last = jnp.minimum(qb + 1, (live + BLOCK - 1) // BLOCK)
        acc = lax.fori_loop(0, last, step, jnp.zeros((128, BLOCK), F32))
        dq[...] = rope(acc.T * scale, cos[...], -sin[...]).astype(BF)

    @pl.when((pair == pl.num_programs(0) - 1) & (qb == pl.num_programs(1) - 1))
    def _():
        lane = lax.broadcasted_iota(jnp.int32, (SEQUENCE_SLOTS, 128), 1)

        def joined(acc):
            both = [acc[g] + pltpu.roll(acc[g], HEAD_SIZE, 1) for g in range(2)]
            return jnp.where(lane < HEAD_SIZE, both[0], both[1])

        dk[...] = rope(joined(dka) * scale, coskv[...], -sinkv[...]).astype(BF)
        dv[...] = joined(dva).astype(BF)


def attend_back(length, q, k, v, o, do, lse, cos, sin, share):
    rows, qw = q.shape
    kw = k.shape[1]
    pairs, blocks = qw // 128, rows // BLOCK
    fix = lambda p, b, n: (0, 0)
    tile = pl.BlockSpec((BLOCK, 128), lambda p, b, n: (b, p))
    whole = pl.BlockSpec((rows, kw), fix)
    part = pl.BlockSpec((BLOCK, 128), lambda p, b, n: (b, 0))
    return pl.pallas_call(
        functools.partial(attend_back_body, share),
        grid_spec=pltpu.PrefetchScalarGridSpec(
            num_scalar_prefetch=1,
            grid=(pairs, blocks),
            in_specs=[
                tile,
                whole,
                whole,
                tile,
                tile,
                pl.BlockSpec((1, 8, BLOCK), lambda p, b, n: (p, 0, b)),
                part,
                part,
                whole,
                whole,
            ],
            out_specs=[tile, whole, whole],
            scratch_shapes=[
                pltpu.VMEM((4, rows, 128), BF),
                pltpu.VMEM((4, rows, 128), BF),
                pltpu.VMEM((4, 128, rows), BF),
                pltpu.VMEM((2, rows, 128), F32),
                pltpu.VMEM((2, rows, 128), F32),
            ],
        ),
        out_shape=[
            jax.ShapeDtypeStruct((rows, qw), BF),
            jax.ShapeDtypeStruct((rows, kw), BF),
            jax.ShapeDtypeStruct((rows, kw), BF),
        ],
        compiler_params=params(32),
        name="attend_back",
    )(length, q, k, v, o, do, lse, cos, sin, cos, sin)


NB = 8


def local_slots(table, first, local):
    at = (lax.broadcasted_iota(jnp.int32, (local, BLOCK), 0) + first).astype(F32)
    slot = jnp.full((local, BLOCK), -1.0, F32)
    gate = jnp.zeros((local, BLOCK), F32)
    for k in range(TOP):
        row = table[k : k + 1, :]
        here = row[:, :BLOCK] == at
        slot = jnp.where(here, row[:, BLOCK : 2 * BLOCK], slot)
        gate = jnp.where(here, row[:, 2 * BLOCK : 3 * BLOCK] + row[:, 3 * BLOCK :], gate)
    return slot, gate


def one_hot(slot, cap):
    at = lax.broadcasted_iota(jnp.int32, (cap, BLOCK), 0).astype(F32)
    return jnp.concatenate(
        [jnp.where(at == slot[e : e + 1, :], 1.0, 0.0) for e in range(slot.shape[0])], axis=0
    )


def load_plane(own, sib, buf, sem):
    return [
        pltpu.make_async_copy(
            ref.at[n % 4, pl.ds(0, BLOCK), :], buf.at[n], sem.at[n]
        )
        for n in range(NB)
        for ref in (own if n < 4 else sib,)
    ]


def wait_pair(i, own, buf, sem):
    for n in (2 * i, 2 * i + 1):
        pltpu.make_async_copy(own.at[0, pl.ds(0, BLOCK), :], buf.at[n], sem.at[n]).wait()


def gather_pair(i, buf, hots, out, local, cap):
    width = buf.shape[2]
    cut = width // 3
    rows = pl.ds(pl.multiple_of(i * 2 * cap, 16), 2 * cap)
    for c in range(3):
        cols = slice(c * cut, (c + 1) * cut)
        got = [mm(hots[j], buf[2 * i + j, :, cols]) for j in range(2)]
        for e in range(local):
            mine = [g[e * cap : (e + 1) * cap, :] for g in got]
            out[e, rows, cols] = jnp.concatenate(mine, axis=0).astype(BF)


def seed_body(cap, plane, fresh, first, own, sib, *refs):
    down = refs[0]
    s_out, u_out, tab, buf, s_scr, d_scr, t_scr, sem, t_sem = refs[1 if fresh else 2 :]
    local = d_scr.shape[0]
    copies = load_plane(own, sib, buf, sem)
    tables = []
    for n in range(NB):
        ref = (own if n < 4 else sib).at[n % 4, pl.ds(BLOCK, TOP), :]
        tables.append(pltpu.make_async_copy(ref, t_scr.at[n], t_sem.at[n]))
    weights = pltpu.make_async_copy(down, d_scr, sem.at[NB + 2])
    for c in tables + copies:
        c.start()
    weights.start()
    for c in tables:
        c.wait()
    for n in range(NB):
        tab[n] = t_scr[n, :, : 4 * BLOCK].astype(F32)

    def gather(i, _):
        hots = []
        for j in range(2):
            slot, _g = local_slots(tab[2 * i + j], first[0], local)
            hots.append(one_hot(slot, cap).astype(BF))
        wait_pair(i, own, buf, sem)
        gather_pair(i, buf, hots, s_scr, local, cap)
        return 0

    lax.fori_loop(0, NB // 2, gather, 0, unroll=2)
    rows = NB * cap
    keep = pltpu.make_async_copy(s_scr, s_out.at[:, pl.ds(plane * rows, rows), :], sem.at[NB + 3])
    keep.start()
    weights.wait()

    def expert(e, _):
        u_out[e] = mm(s_scr[e], d_scr[e], NT)
        return 0

    lax.fori_loop(0, local, expert, 0, unroll=4 if local % 4 == 0 else 1)
    keep.wait()


def seed_rows(plane, planes, first, own, sib, down, kept, cap):
    local, hidden, width = down.shape
    rows = NB * cap
    vm = pl.BlockSpec(memory_space=pltpu.VMEM)
    smem = pl.BlockSpec(memory_space=pltpu.SMEM)
    fresh = kept is None
    more = () if fresh else (kept,)
    return pl.pallas_call(
        functools.partial(seed_body, cap, plane, fresh),
        in_specs=[smem] + [ANY] * (3 + len(more)),
        out_specs=[ANY, vm, vm],
        out_shape=[
            jax.ShapeDtypeStruct((local, planes * rows, width), BF),
            jax.ShapeDtypeStruct((local, rows, hidden), F32),
            jax.ShapeDtypeStruct((NB, TOP, 4 * BLOCK), F32),
        ],
        scratch_shapes=[
            pltpu.VMEM((NB, BLOCK, width), BF),
            pltpu.VMEM((local, rows, width), BF),
            pltpu.VMEM((local, hidden, width), BF),
            pltpu.VMEM((NB, TOP, width), BF),
            pltpu.SemaphoreType.DMA((NB + 4,)),
            pltpu.SemaphoreType.DMA((NB,)),
        ],
        input_output_aliases={} if fresh else {4: 0},
        compiler_params=params(50),
        cost_estimate=cost(2 * rows * local * (BLOCK + hidden) * width, 2e7),
        name="seed_rows",
    )(first, own, sib, down, *more)


def main_body(cap, plane, fresh, first, tab, u, own_in, sib_in, *refs):
    wgu = refs[0]
    refs = refs[1 if fresh else 4 :]
    x_out, d_out, a_out, own, sib = refs[:5]
    buf, x_scr, w_scr, z_scr, p_scr, g_scr, r_scr, d_scr, a_scr, m_scr, sem, out_sem = refs[5:]
    local, hidden = a_scr.shape[0], a_scr.shape[2]
    rows = NB * cap
    slots = local * cap
    copies = load_plane(own_in, sib_in, buf, sem)
    weights = pltpu.make_async_copy(wgu, w_scr, sem.at[NB + 2])
    for c in copies:
        c.start()
    weights.start()

    def gather(i, _):
        hots = []
        for j in range(2):
            b = 2 * i + j
            slot, gate = local_slots(tab[b], first[0], local)
            hot = one_hot(slot, cap)
            spread_gate = jnp.concatenate(
                [jnp.broadcast_to(gate[e : e + 1, :], (cap, BLOCK)) for e in range(local)], axis=0
            )
            weight = jnp.sum(hot * spread_gate, axis=1, keepdims=True)
            weight = jnp.broadcast_to(weight, (slots, hidden))
            for e in range(local):
                g_scr[e, pl.ds(b * cap, cap), :] = weight[e * cap : (e + 1) * cap, :]
            hots.append(hot.astype(BF))
            p_scr[b] = hots[-1]
        wait_pair(i, own_in, buf, sem)
        gather_pair(i, buf, hots, x_scr, local, cap)
        return 0

    lax.fori_loop(0, NB // 2, gather, 0, unroll=2)
    here = pl.ds(plane * rows, rows)
    keep_x = pltpu.make_async_copy(x_scr, x_out.at[:, here, :], sem.at[NB + 3])
    keep_x.start()
    weights.wait()

    def expert(e, _):
        gu = mm(x_scr[e], w_scr[e])
        gate, up = gu[:, :hidden], gu[:, hidden:]
        sig = 1.0 / (1.0 + jnp.exp(-gate))
        silu = gate * sig
        act = (silu * up).astype(BF).astype(F32)
        ue = u[e]
        w = g_scr[e]
        inner = w * ue
        dg = inner * up * sig * (1.0 + gate * (1.0 - sig))
        d = jnp.concatenate([dg, inner * silu], axis=1).astype(BF)
        d_scr[e] = d
        a_scr[e] = (act * w).astype(BF)
        r_scr[e] = act * ue
        z_scr[e] = mm(d, w_scr[e], NT)
        return 0

    lax.fori_loop(0, local, expert, 0, unroll=4 if local % 4 == 0 else 1)
    keep_d = pltpu.make_async_copy(d_scr, d_out.at[:, here, :], sem.at[NB + 4])
    keep_a = pltpu.make_async_copy(a_scr, a_out.at[:, here, :], sem.at[NB + 5])
    keep_d.start()
    keep_a.start()

    for half, out in ((1, sib), (0, own)):

        def combine(i, _):
            b = 4 * half + i
            at = pl.ds(b * cap, cap)
            zb = z_scr[:, at, :].reshape(slots, -1).astype(BF)
            m_scr[b, :BLOCK, :] = mm(p_scr[b], zb, TN).astype(BF)
            pair = jnp.sum(r_scr[:, at, :].reshape(slots, hidden), axis=1, keepdims=True)
            hot = p_scr[b].astype(F32) * pair
            per = jnp.concatenate(
                [
                    jnp.sum(hot[e * cap : (e + 1) * cap, :], axis=0, keepdims=True)
                    for e in range(local)
                ],
                axis=0,
            )
            ids = (lax.broadcasted_iota(jnp.int32, (local, BLOCK), 0) + first[0]).astype(F32)
            pairs = []
            for k in range(TOP):
                mine = tab[b, k : k + 1, :BLOCK] == ids
                pairs.append(jnp.sum(jnp.where(mine, per, 0.0), axis=0, keepdims=True))
            tail = jnp.zeros((TOP, m_scr.shape[2] - BLOCK), F32)
            pairs = jnp.concatenate([jnp.concatenate(pairs, axis=0), tail], axis=1)
            m_scr[b, BLOCK:, :] = pairs.astype(BF)
            pltpu.make_async_copy(m_scr.at[b], out.at[i], out_sem.at[b]).start()
            return 0

        lax.fori_loop(0, 4, combine, 0, unroll=2)
    for half, out in ((1, sib), (0, own)):
        for i in range(4):
            b = 4 * half + i
            pltpu.make_async_copy(m_scr.at[b], out.at[i], out_sem.at[b]).wait()
    keep_x.wait()
    keep_d.wait()
    keep_a.wait()


def expert_rows(plane, planes, first, tab, u, own, sib, wgu, kept, cap):
    local, width, two = wgu.shape
    hidden = two // 2
    rows = NB * cap
    vm = pl.BlockSpec(memory_space=pltpu.VMEM)
    smem = pl.BlockSpec(memory_space=pltpu.SMEM)
    fresh = kept is None
    more = () if fresh else tuple(kept)
    total = planes * rows
    return pl.pallas_call(
        functools.partial(main_body, cap, plane, fresh),
        in_specs=[smem, vm, vm] + [ANY] * (3 + len(more)),
        out_specs=[ANY] * 5,
        out_shape=[
            jax.ShapeDtypeStruct((local, total, width), BF),
            jax.ShapeDtypeStruct((local, total, two), BF),
            jax.ShapeDtypeStruct((local, total, hidden), BF),
            jax.ShapeDtypeStruct((4, BLOCK + TOP, width), BF),
            jax.ShapeDtypeStruct((4, BLOCK + TOP, width), BF),
        ],
        scratch_shapes=[
            pltpu.VMEM((NB, BLOCK, width), BF),
            pltpu.VMEM((local, rows, width), BF),
            pltpu.VMEM((local, width, two), BF),
            pltpu.VMEM((local, rows, width), F32),
            pltpu.VMEM((NB, local * cap, BLOCK), BF),
            pltpu.VMEM((local, rows, hidden), F32),
            pltpu.VMEM((local, rows, hidden), F32),
            pltpu.VMEM((local, rows, two), BF),
            pltpu.VMEM((local, rows, hidden), BF),
            pltpu.VMEM((NB, BLOCK + TOP, width), BF),
            pltpu.SemaphoreType.DMA((NB + 6,)),
            pltpu.SemaphoreType.DMA((NB,)),
        ],
        input_output_aliases={} if fresh else {6: 0, 7: 1, 8: 2},
        compiler_params=params(60),
        cost_estimate=cost(2 * rows * local * (2 * BLOCK + 2 * two) * width, 3e7),
        name="expert_rows",
    )(first, tab, u, own, sib, wgu, *more)


def mix_body(cap, plane, first, tab, a, down_in, own, sib, y_scr, a_scr, down, sem):
    local = down.shape[0]
    slots = local * cap
    rows = NB * cap
    load = pltpu.make_async_copy(a.at[:, pl.ds(plane * rows, rows), :], a_scr, sem.at[0])
    half = local // 2
    cuts = [pl.ds(0, half), pl.ds(half, local - half)] if half else [pl.ds(0, local)]
    weights = [
        pltpu.make_async_copy(down_in.at[c], down.at[c], sem.at[1 + i]) for i, c in enumerate(cuts)
    ]
    load.start()
    for w in weights:
        w.start()
    load.wait()
    for w in weights:
        w.wait()

    def expert(e, _):
        y_scr[e] = mm(a_scr[e], down[e])
        return 0

    lax.fori_loop(0, local, expert, 0, unroll=4 if local % 4 == 0 else 1)
    for half, out in ((1, sib), (0, own)):

        def combine(i, _):
            b = 4 * half + i
            slot, _g = local_slots(tab[b], first[0], local)
            hot = one_hot(slot, cap).astype(BF)
            yb = y_scr[:, pl.ds(b * cap, cap), :].reshape(slots, -1).astype(BF)
            out[i] = mm(hot, yb, TN).astype(BF)
            return 0

        lax.fori_loop(0, 4, combine, 0, unroll=2)


def mix_rows(plane, first, tab, a, down, cap):
    local, hidden, width = down.shape
    rows = NB * cap
    vm = pl.BlockSpec(memory_space=pltpu.VMEM)
    return pl.pallas_call(
        functools.partial(mix_body, cap, plane),
        in_specs=[pl.BlockSpec(memory_space=pltpu.SMEM), vm, ANY, ANY],
        out_specs=[vm, vm],
        out_shape=[jax.ShapeDtypeStruct((4, BLOCK, width), BF)] * 2,
        scratch_shapes=[
            pltpu.VMEM((local, rows, width), F32),
            pltpu.VMEM((local, rows, hidden), BF),
            pltpu.VMEM((local, hidden, width), BF),
            pltpu.SemaphoreType.DMA((3,)),
        ],
        compiler_params=params(34),
        cost_estimate=cost(2 * rows * local * (BLOCK + hidden) * width, 2e7),
        name="mix_rows",
    )(first, tab, a, down)


def round_body(turn, up, down, wgu, low):
    hidden = low.shape[1]
    for part in range(2):
        wgu[0, :, part * hidden : (part + 1) * hidden] = up[part, 0].astype(BF)
    low[0] = down[0].astype(BF)


def round_weights(turn, up, down):
    local, hidden, width = down.shape
    return pl.pallas_call(
        round_body,
        grid=(local,),
        in_specs=[
            pl.BlockSpec(memory_space=pltpu.SMEM),
            pl.BlockSpec((2, 1, width, hidden), lambda e: (0, e, 0, 0)),
            pl.BlockSpec((1, hidden, width), lambda e: (e, 0, 0)),
        ],
        out_specs=[
            pl.BlockSpec((1, width, 2 * hidden), lambda e: (e, 0, 0)),
            pl.BlockSpec((1, hidden, width), lambda e: (e, 0, 0)),
        ],
        out_shape=[
            jax.ShapeDtypeStruct((local, width, 2 * hidden), BF),
            jax.ShapeDtypeStruct((local, hidden, width), BF),
        ],
        compiler_params=params(32),
        cost_estimate=cost(0, 28e6),
        name="round_weights",
    )(turn, up, down)


def weights_body(older, turn, x, s, d, a, *refs):
    hidden = a.shape[2]
    ins, outs = refs[:6], refs[6 + older :]
    done = outs[-1]
    done[0] = turn[0]
    dgu = mm(d[0], x[0], TN).T
    for part in range(2):
        grad = dgu[:, part * hidden : (part + 1) * hidden]
        w, mean, sq = (r[part, 0] for r in ins[:3])
        for ref, val in zip(outs[:4], adam_step(w, grad, mean, sq, WEIGHT_DECAY)):
            ref[part, 0] = val
    ddown = mm(a[0], s[0], TN)
    w, mean, sq = (r[0] for r in ins[3:6])
    for ref, val in zip(outs[4:8], adam_step(w, ddown, mean, sq, WEIGHT_DECAY)):
        ref[0] = val


def weights_step(turn, begin, count, x, s, d, a, up, down, older, cuts=2):
    local, rows, width = x.shape
    hidden = a.shape[2]
    part = width // cuts
    wide = pl.BlockSpec((1, rows, part), lambda e, j: (e + begin, 0, j))
    slim = lambda n: pl.BlockSpec((1, rows, n), lambda e, j: (e + begin, 0, 0))
    ups = pl.BlockSpec((2, 1, part, hidden), lambda e, j: (0, e + begin, j, 0))
    downs = pl.BlockSpec((1, hidden, part), lambda e, j: (e + begin, 0, j))
    smem = pl.BlockSpec(memory_space=pltpu.SMEM)
    out = pl.pallas_call(
        functools.partial(weights_body, len(older)),
        grid=(count, cuts),
        in_specs=[smem, wide, wide, slim(2 * hidden), slim(hidden)]
        + [ups] * 3
        + [downs] * 3
        + [ANY] * len(older),
        out_specs=[ups] * 4 + [downs] * 4 + [smem],
        out_shape=[jax.ShapeDtypeStruct(up[0].shape, F32)] * 4
        + [jax.ShapeDtypeStruct(down[0].shape, F32)] * 4
        + [jax.ShapeDtypeStruct((1,), jnp.int32)],
        input_output_aliases={11 + i: i for i in range(len(older))},
        compiler_params=params(),
        cost_estimate=cost(2 * count * rows * width * 3 * hidden, 26e6 * count),
        name="weights_step",
    )(turn, x, s, d, a, *up, *down, *older)
    return list(out[:8]), out[8]


def experts_by_slot(
    moe_in, cotangent, live_rows, target, gate_values, lengths, up, down, capacity, data_size
):
    tensor_size = lax.axis_size("tensor")
    own_rows, model_width = moe_in.shape
    upgate_low, downproj_low = up[0].astype(BF), down[0].astype(BF)
    local_blocks = upgate_low.shape[1]
    expert_total = local_blocks * data_size
    slots = local_blocks * capacity
    kept = target >= 0
    put_at = jnp.where(kept, target, expert_total * capacity)
    fetch_at = jnp.where(kept, target, 0)
    pair_weight = jnp.where(kept, gate_values.reshape(-1), 0.0)

    def send(pair_rows):
        empty = jnp.zeros((expert_total * capacity, model_width), BF)
        filled = empty.at[put_at].set(pair_rows, mode="drop")
        filled = filled.reshape(1, data_size, slots, model_width)
        wide = lax.all_gather(filled, "tensor", axis=0, tiled=True)
        wide = lax.all_to_all(wide, "dp", split_axis=1, concat_axis=1, tiled=True)
        return wide.reshape(tensor_size, data_size, local_blocks, capacity, model_width)

    def bring(parts):
        parts = parts.reshape(tensor_size, data_size, slots, model_width)
        wide = lax.all_to_all(parts.astype(BF), "dp", split_axis=1, concat_axis=1, tiled=True)
        wide = lax.all_to_all(wide, "tensor", split_axis=0, concat_axis=0, tiled=True)
        summed = jnp.sum(wide.astype(F32), axis=0).astype(BF)
        return summed.reshape(expert_total * capacity, model_width)

    def dot(spec, a, b):
        return jnp.einsum(spec, a, b, preferred_element_type=F32)

    rows_in = send(jnp.repeat(moe_in, TOP, axis=0))
    gate_pre = dot("abecd,edf->abecf", rows_in, upgate_low[0])
    up_pre = dot("abecd,edf->abecf", rows_in, upgate_low[1])
    inner_act = (jax.nn.silu(gate_pre) * up_pre).astype(BF)
    pair_out = bring(dot("abecf,efd->abecd", inner_act, downproj_low))[fetch_at].astype(F32)
    mixed = jnp.sum((pair_weight[:, None] * pair_out).reshape(own_rows, TOP, model_width), axis=1)
    seed_grad = cotangent.astype(F32) * live_rows[:, None].astype(F32)
    seed_pairs = jnp.repeat(seed_grad, TOP, axis=0)
    gate_grad = jnp.where(kept, jnp.sum(pair_out * seed_pairs, axis=1), 0.0)
    out_seed = send((pair_weight[:, None] * seed_pairs).astype(BF))
    inner_grad = dot("abecd,efd->abecf", out_seed, downproj_low)
    down_grad = dot("abecf,abecd->efd", inner_act, out_seed)
    sig = jax.nn.sigmoid(gate_pre)
    gate_back = (inner_grad * up_pre * sig * (1.0 + gate_pre * (1.0 - sig))).astype(BF)
    up_back = (inner_grad * gate_pre * sig).astype(BF)
    up_grad = jnp.stack(
        [
            dot("abecd,abecf->edf", rows_in, gate_back),
            dot("abecd,abecf->edf", rows_in, up_back),
        ]
    )
    rows_grad = dot("abecf,edf->abecd", gate_back, upgate_low[0])
    rows_grad = rows_grad + dot("abecf,edf->abecd", up_back, upgate_low[1])
    back = bring(rows_grad)[fetch_at].astype(F32)
    back = jnp.where(kept[:, None], back, 0.0)
    moe_grad = jnp.sum(back.reshape(own_rows, TOP, model_width), axis=1)
    return (
        mixed,
        gate_grad.reshape(own_rows, TOP),
        moe_grad,
        adam_step(up[0], up_grad, *up[1:], WEIGHT_DECAY),
        adam_step(down[0], down_grad, *down[1:], WEIGHT_DECAY),
    )


def flip(v, axis, bit):
    return lax.ppermute(v, axis, [(i, i ^ bit) for i in range(lax.axis_size(axis))])


def core(v):
    return flip(v, "tensor", 1)


def across(v):
    return flip(v, "tensor", 2)


def side(v):
    return flip(v, "dp", 1)


def onward(v, planes=1):
    n = lax.axis_size("dp")
    return lax.ppermute(v, "dp", [(i, (i + 2 * planes) % n) for i in range(n)])


def plus(*vs):
    return functools.reduce(lambda a, b: a + b, [v.astype(F32) for v in vs]).astype(BF)


def meet(*vs):
    return lax.optimization_barrier(vs)


class Spread:
    def __init__(self, own):
        self.z, self.x, self.y, self.d, self.own, self.sib = {0: own}, {}, {}, {}, {}, {}

    def on(self, r):
        self.z[r] = onward(self.z[r - 1])

    def x_(self, r):
        self.x[r] = across(self.z[r])

    def y_(self, r):
        self.y[r] = side(self.z[r])

    def x_on(self, r):
        self.x[r] = onward(self.x[r - 1])

    def y_on(self, r):
        self.y[r] = onward(self.y[r - 1])

    def d_(self, r):
        self.d[r] = across(self.y[r]) if r % 2 else side(self.x[r])

    def cores(self, r):
        self.own[r] = jnp.stack([self.z[r], self.x[r], self.y[r], self.d.pop(r)])
        self.sib[r] = core(self.own[r])

    def state(self):
        return [self.z, self.x, self.y, self.d, self.own, self.sib]

    def put(self, state):
        self.z, self.x, self.y, self.d, self.own, self.sib = state


class Reduce:
    def __init__(self):
        self.own, self.sib, self.parts, self.d = {}, {}, {}, {}
        self.wx, self.wy, self.zx, self.zy, self.total = {}, {}, {}, {}, {}

    def cores(self, r):
        own, came = self.own.pop(r), core(self.sib.pop(r))
        self.parts[r] = [plus(own[i], came[i]) for i in range(4)]

    def part(self, r, i):
        vs = [self.parts[r][i]]
        if i == (2 if r % 2 else 1) and r in self.d:
            vs.append(self.d[r])
        if r == 0 and i == 1:
            vs.append(self.zx[1])
        if r == 0 and i == 2:
            vs.append(self.zy[1])
        return vs

    def d_(self, r):
        v = plus(*self.part(r, 3))
        self.d[r] = across(v) if r % 2 else side(v)

    def x_(self, r):
        self.wx[r] = across(plus(*self.part(r, 1)))

    def y_(self, r):
        self.wy[r] = side(plus(*self.part(r, 2)))

    def x_in(self, r):
        self.zx[r] = onward(plus(*self.part(r, 1)), -1)

    def y_in(self, r):
        self.zy[r] = onward(plus(*self.part(r, 2)), -1)

    def plane(self, r):
        vs = self.part(r, 0)
        vs = vs + [w.pop(r) for w in (self.wx, self.wy, self.total) if r in w]
        return functools.reduce(lambda a, b: a + b, [v.astype(F32) for v in vs])

    def on(self, r, count):
        self.total[(r + 1) % count] = onward(self.plane(r).astype(BF))

    def state(self):
        return [
            self.own, self.sib, self.parts, self.d,
            self.wx, self.wy, self.zx, self.zy, self.total,
        ]

    def put(self, state):
        (
            self.own, self.sib, self.parts, self.d,
            self.wx, self.wy, self.zx, self.zy, self.total,
        ) = state


def data_parts(part):
    n = lax.axis_size("dp")
    me = lax.axis_index("dp")
    planes = n // 2
    pairs = part.reshape((planes, 2, part.shape[0] // n) + part.shape[1:])
    mine = lax.dynamic_index_in_dim(pairs, me % 2, 1, keepdims=False)
    other = lax.dynamic_index_in_dim(pairs, 1 - me % 2, 1, keepdims=False)
    order = [((me // 2) + planes - r) % planes for r in range(planes)]
    at = lambda a, r: lax.dynamic_index_in_dim(a, order[r], 0, keepdims=False)
    return tuple(jnp.stack([at(a, r) for r in range(planes)]) for a in (mine, other))


def pack_weights(query_weight, keyvalue_matrix, outproj_weight, norm_gains):
    return jnp.concatenate(
        [
            query_weight.astype(BF),
            keyvalue_matrix[0].astype(BF),
            keyvalue_matrix[1].astype(BF),
            outproj_weight.astype(BF).T,
            jnp.pad(norm_gains.astype(BF).T, ((0, 0), (0, 126))),
        ],
        axis=1,
    )


def normed(v):
    rms = lax.rsqrt(jnp.mean(v * v, axis=-1, keepdims=True) + NORM_EPS)
    return rms, v * rms


def norm_back(grad, gain, rms, norm):
    scaled = grad * gain
    return rms * (scaled - norm * jnp.mean(scaled * norm, axis=-1, keepdims=True))


def few_groups(
    hidden_in, cotangent, lengths, routes, gate_values, target, live_rows, capacity,
    query_weight, keyvalue_matrix, outproj_weight, norm_gains, up, down,
):
    tensor_index, me = lax.axis_index("tensor"), lax.axis_index("dp")
    count = lax.axis_size("dp") // 2
    qw, kw = query_weight.shape[1], keyvalue_matrix.shape[2]
    share = qw // kw
    local = up[0].shape[1]
    width = hidden_in.shape[1]

    wide = qw + 2 * kw
    out_cols, in_cols = (wide, wide + qw), (0, wide)

    own_packed = pack_weights(query_weight, keyvalue_matrix, outproj_weight, norm_gains)
    w = [own_packed]
    hx, hc = across(hidden_in), core(hidden_in)
    sides = []
    for r in range(count - 1):
        sides.append(side(w[r]))
        w.append(onward(w[r]))
        w[r + 1], sides[r] = meet(w[r + 1], sides[r])
    sides.append(side(w[-1]))
    hxc = core(hx)
    places = [(me + 2 * (count - r)) % (2 * count) for r in range(count)]
    weight_places = [p for r in range(count) for p in (places[r], places[r] ^ 1)]
    at = [tensor_index ^ j for j in range(4)] + weight_places
    at = jnp.stack([jnp.asarray(p, jnp.int32) for p in at])
    cos, sin = rope_lanes(4 * BLOCK)

    seeds = jnp.where(live_rows[:, None], cotangent, jnp.zeros((), BF))
    slot = jnp.where(target >= 0, target - routes.reshape(-1) * capacity, -1).reshape(-1, TOP)
    high = gate_values.astype(BF)
    low = (gate_values - high.astype(F32)).astype(BF)
    table = jnp.concatenate([routes.astype(BF).T, slot.astype(BF).T, high.T, low.T], axis=1)
    table = jnp.pad(table, ((0, 0), (0, width - table.shape[1])))
    first = (me * local).astype(jnp.int32).reshape(1)
    c = Spread(jnp.concatenate([seeds, table], axis=0))
    c.z[0], w[2], hx = meet(c.z[0], w[2], hx)
    c.x_(0)
    c.z[0], w[3] = meet(c.z[0], w[3])
    c.on(1)

    (rows_of, w, sides, cos, sin, st) = meet(
        [hidden_in, hc, hx, hxc], w, sides, cos, sin, c.state()
    )
    c.put(st)
    weight_blocks = [b for r in range(count) for b in (w[r], sides[r])]
    attn_in, q, k, v, gains, packed = qkv(at, rows_of, weight_blocks, qw, kw, cos, sin)
    c.x_(1), c.y_(0), c.on(2)
    q, k, v, gains, st = meet(q, k, v, gains, c.state())
    c.put(st)
    gain_attn, gain_moe = gains[0:1], gains[1:2]
    heads, lse = attend(lengths, q, k, v, share)
    c.x_(2), c.d_(0), c.on(3)
    heads, st = meet(heads, c.state())
    c.put(st)
    near0, near1, far0, far1 = project(at, heads, packed, out_cols)
    far1 = core(far1)
    c.y_(1), c.cores(0)
    near0, near1, far0, far1, st, first = meet(near0, near1, far0, far1, c.state(), first)
    c.put(st)
    sent, near1 = across(plus(far0, far1)), core(near1)
    us, tabs, kept_s = {}, {}, None

    def seed(r):
        nonlocal kept_s
        kept_s, us[r], tabs[r] = seed_rows(
            r, count, first, c.own.pop(r), c.sib.pop(r), down_low, kept_s, capacity
        )

    c.d_(2), c.y_on(2)
    wgu, down_low = round_weights(first, up[0], down[0])
    sent, near0, near1, wgu, down_low, st = meet(sent, near0, near1, wgu, down_low, c.state())
    c.put(st)
    attn_own = plus(near0, near1).astype(F32) + sent.astype(F32)
    hidden = hidden_in.astype(F32)
    middle = hidden + attn_own
    rms_moe, normed_moe = normed(middle)
    m = Spread((normed_moe * gain_moe).astype(BF))
    back, mix = Reduce(), Reduce()
    kept, news, turn = None, [], first

    def expert(r):
        nonlocal kept
        x, dgu, act, back.own[r], back.sib[r] = expert_rows(
            r, count, first, tabs[r], us[r], m.own.pop(r), m.sib.pop(r), wgu, kept, capacity
        )
        kept = (x, dgu, act)

    def mixes(r):
        mix.own[r], mix.sib[r] = mix_rows(r, first, tabs[r], kept[2], down_low, capacity)

    def weights(begin, size):
        nonlocal news, turn
        news, turn = weights_step(
            turn, begin, size, kept[0], kept_s, kept[1], kept[2], up, down, news
        )

    def step():
        nonlocal first, us, tabs, turn
        first, turn, us, tabs, sc, sm, sb, sx = meet(
            first, turn, us, tabs, c.state(), m.state(), back.state(), mix.state()
        )
        c.put(sc), m.put(sm), back.put(sb), mix.put(sx)

    m.z[0], st = meet(m.z[0], c.state())
    c.put(st)
    m.x_(0), m.y_(0), m.on(1)
    seed(0)
    step()
    c.d_(1), m.d_(0), m.y_on(1)
    step()
    m.d_(1), c.y_(3), m.on(2), c.cores(1), m.cores(0)
    step()
    m.x_(2), m.y_(2), m.x_on(1), c.cores(2)
    expert(0)
    step()
    c.d_(3), m.d_(2), m.on(3), m.cores(1)
    seed(1)
    seed(2)
    step()
    m.x_(3), m.y_(3), c.x_on(3), m.cores(2), back.cores(0)
    expert(1)
    step()
    m.d_(3), back.d_(0), back.cores(1), c.cores(3)
    expert(2)
    step()
    back.d_(1), back.x_in(1), back.cores(2), m.cores(3)
    seed(3)
    mixes(0)
    step()
    back.d_(2), back.on(1, count), mix.cores(0)
    expert(3)
    step()
    back.x_(2), back.y_(2), back.y_in(1), back.cores(3)
    mixes(1)
    step()
    back.d_(3), mix.d_(0), back.on(2, count), mix.cores(1)
    mixes(2)
    step()
    back.x_(3), back.y_(3), mix.x_in(1), mix.cores(2)
    mixes(3)
    step()
    back.x_(0), back.y_(0), back.on(3, count), mix.cores(3)
    weights(0, 2)
    step()
    whole = back.plane(0)
    gate_grad, moe_grad = whole[BLOCK:, :BLOCK].T, whole[:BLOCK]

    seed_grad = cotangent.astype(F32) * live_rows[:, None].astype(F32)
    gain_part = jnp.sum(moe_grad * normed_moe, axis=0)
    middle_grad = seed_grad + norm_back(moe_grad, gain_moe, rms_moe, normed_moe)
    mid, turn, st = meet(middle_grad.astype(BF), turn, mix.state())
    mix.put(st)
    mx, mc = across(mid), core(mid)
    mix.d_(2), mix.on(1, count)
    weights(2, 2)
    mx, mc, turn, st, gain_part = meet(mx, mc, turn, mix.state(), gain_part)
    mix.put(st)
    mxc = core(mx)
    mix.d_(1)
    heads_grad, middle_low = heads_back(at, [mid, mc, mx, mxc], packed, out_cols)
    outproj_part = mm(middle_low, heads, TN).astype(BF)
    heads_grad, outproj_part, st = meet(heads_grad, outproj_part, mix.state())
    mix.put(st)
    dq, dk, dv = attend_back(lengths, q, k, v, heads, heads_grad, lse, cos, sin, share)
    omine, oother = data_parts(outproj_part)
    ocame = side(oother)
    mix.d_(3), mix.x_(2), mix.y_(2), mix.y_in(1)
    dq, dk, dv, ocame, omine, st = meet(dq, dk, dv, ocame, omine, mix.state())
    mix.put(st)
    osums = plus(omine, ocame)
    ohere = [osums[0]] + [onward(osums[r], -r) for r in range(1, count)]
    dqkv = jnp.concatenate([dq, dk, dv], axis=1)
    near0, near1, far0, far1 = project(at, dqkv, packed, in_cols)
    far1 = core(far1)
    qkv_part = mm(attn_in, dqkv, TN)
    gain_attn_part = jnp.sum(packed[:, :wide].astype(F32) * qkv_part, axis=1) / gain_attn[0]
    gain_rows = jnp.stack([gain_attn_part, gain_part]).reshape(2, 2 * count, -1)
    gain_rows = jnp.pad(gain_rows.transpose(1, 0, 2), ((0, 0), (0, 6), (0, wide - gain_rows.shape[2])))
    qkv_part = qkv_part.astype(BF).reshape(2 * count, -1, wide)
    qkv_part = jnp.concatenate([qkv_part, gain_rows.astype(BF)], axis=1)
    qmine, qother = data_parts(qkv_part.reshape(-1, wide))
    near0, near1, far0, far1, qmine, qother, ohere, st = meet(
        near0, near1, far0, far1, qmine, qother, ohere, mix.state()
    )
    mix.put(st)
    sent, near1 = across(plus(far0, far1)), core(near1)
    qcame = side(qother)
    mix.on(2, count)
    weights(4, 2)
    sent, near0, near1, qcame, qmine, turn, st = meet(
        sent, near0, near1, qcame, qmine, turn, mix.state()
    )
    mix.put(st)
    attn_grad = plus(near0, near1).astype(F32) + sent.astype(F32)
    rms_attn, normed_attn = normed(hidden)
    input_grad = middle_grad + norm_back(attn_grad, gain_attn, rms_attn, normed_attn)
    qsums = plus(qmine, qcame)
    here = [qsums[0]] + [onward(qsums[r], -r) for r in range(1, count)]
    mix.x_(3), mix.y_(3)
    weights(6, 2)
    here, turn, st = meet(here, turn, mix.state())
    mix.put(st)
    mix.on(3, count), mix.x_(0), mix.y_(0)
    here = functools.reduce(lambda a, b: a + b, [h.astype(F32) for h in here])
    own_rows = norm_gains.shape[1]
    qkv_sum = here[:own_rows]
    outproj_sum = functools.reduce(lambda a, b: a + b, [o.astype(F32) for o in ohere]).T
    gains_sum = here[own_rows : own_rows + 2, :own_rows]
    gains_sum = gains_sum + flip(gains_sum, "tensor", 1)
    gains_sum = gains_sum + flip(gains_sum, "tensor", 2)
    block_out = (middle + mix.plane(0)).astype(BF)
    return (
        block_out, input_grad, gate_grad, qkv_sum, outproj_sum, gains_sum,
        tuple(news[:4]), tuple(news[4:]),
    )


def many_groups(
    hidden_in, cotangent, lengths, routes, gate_values, target, live_rows, capacity,
    query_weight, keyvalue_matrix, outproj_weight, norm_gains, up, down,
):
    qw, kw = query_weight.shape[1], keyvalue_matrix.shape[2]
    share = qw // kw
    packed = pack_weights(query_weight, keyvalue_matrix, outproj_weight, norm_gains)
    packed = lax.all_gather(packed, "dp", axis=0, tiled=True)
    group = lax.all_gather(hidden_in, "tensor", axis=0, tiled=True)
    rows_of = [group[i * BLOCK : (i + 1) * BLOCK] for i in range(4)]
    at = jnp.concatenate([jnp.arange(4, dtype=jnp.int32), jnp.zeros((1,), jnp.int32)])
    cos, sin = rope_lanes(4 * BLOCK)
    attn_in, q, k, v, gains, packed = qkv(at, rows_of, [packed], qw, kw, cos, sin)
    wide = qw + 2 * kw
    qkv_low, outproj_low = packed[:, :wide], packed[:, wide : wide + qw]
    gain_attn, gain_moe = gains[0:1], gains[1:2]
    heads, lse = attend(lengths, q, k, v, share)

    def scattered(part):
        part = lax.psum_scatter(part.astype(BF), "tensor", scatter_dimension=0, tiled=True)
        return part.astype(F32)

    hidden = hidden_in.astype(F32)
    middle = hidden + scattered(mm(heads, outproj_low, NT))
    rms_moe, normed_moe = normed(middle)
    moe_in = (normed_moe * gain_moe).astype(BF)
    mixed, gate_grad, moe_grad, up_new, down_new = experts_by_slot(
        moe_in, cotangent, live_rows, target, gate_values, lengths, up, down, capacity,
        lax.axis_size("dp"),
    )
    block_out = (middle + mixed).astype(BF)
    seed_grad = cotangent.astype(F32) * live_rows[:, None].astype(F32)
    gain_moe_part = jnp.sum(moe_grad * normed_moe, axis=0)
    middle_grad = seed_grad + norm_back(moe_grad, gain_moe, rms_moe, normed_moe)
    middle_low = lax.all_gather(middle_grad.astype(BF), "tensor", axis=0, tiled=True)
    heads_grad = mm(middle_low, outproj_low).astype(BF)
    dq, dk, dv = attend_back(lengths, q, k, v, heads, heads_grad, lse, cos, sin, share)
    dqkv = jnp.concatenate([dq, dk, dv], axis=1)
    attn_grad = scattered(mm(dqkv, qkv_low, NT))
    rms_attn, normed_attn = normed(hidden)
    gain_attn_part = jnp.sum(attn_grad * normed_attn, axis=0)
    input_grad = middle_grad + norm_back(attn_grad, gain_attn, rms_attn, normed_attn)
    gains_sum = lax.psum(jnp.stack([gain_attn_part, gain_moe_part]), ("dp", "tensor"))
    own_cols = norm_gains.shape[1]
    gains_sum = lax.dynamic_slice_in_dim(gains_sum, lax.axis_index("dp") * own_cols, own_cols, 1)
    part = jnp.concatenate([mm(attn_in, dqkv, TN), mm(middle_low, heads, TN)], axis=1)
    summed = lax.psum_scatter(part, "dp", scatter_dimension=0, tiled=True)
    return (
        block_out, input_grad, gate_grad, summed[:, :wide], summed[:, wide:].T, gains_sum,
        up_new, down_new,
    )


def on_device(
    hidden_in,
    cotangent,
    lengths,
    routes,
    gate_values,
    pair_order,
    query_weight,
    keyvalue_matrix,
    outproj_weight,
    norm_gains,
    upgate_weight,
    downproj_weight,
    query_mean,
    query_sqmean,
    keyvalue_first_moment,
    keyvalue_second_moment,
    outproj_mean,
    outproj_sqmean,
    gains_mean,
    gains_sqmean,
    upgate_mean,
    upgate_sqmean,
    downproj_mean,
    downproj_sqmean,
):
    tensor_size = lax.axis_size("tensor")
    data_size = lax.axis_size("dp")
    own_rows, model_width = hidden_in.shape
    group_rows = own_rows * tensor_size
    qw = query_weight.shape[1]
    kw = keyvalue_matrix.shape[2]
    assert lengths.shape[0] == 1 and group_rows == SEQUENCE_SLOTS and own_rows == BLOCK

    tensor_index = lax.axis_index("tensor")
    row_ids = tensor_index * own_rows + jnp.arange(own_rows, dtype=jnp.int32)
    live_rows = row_ids < lengths[0]
    capacity = max(2, own_rows * TOP * 5 // (4 * upgate_weight.shape[1] * data_size))
    target = slot_targets(routes.reshape(-1), pair_order[0], jnp.repeat(live_rows, TOP), capacity)
    few = data_size * group_rows * model_width <= 1 << 24
    block_out, input_grad, gate_grad, qkv_sum, outproj_sum, gains_sum, up_new, down_new = (
        few_groups if few else many_groups
    )(
        hidden_in, cotangent, lengths, routes, gate_values, target, live_rows, capacity,
        query_weight, keyvalue_matrix, outproj_weight, norm_gains,
        (upgate_weight, upgate_mean, upgate_sqmean),
        (downproj_weight, downproj_mean, downproj_sqmean),
    )
    query_sum = qkv_sum[:, :qw]
    keyval_sum = jnp.stack([qkv_sum[:, qw : qw + kw], qkv_sum[:, qw + kw :]])
    return (
        (block_out, input_grad, gate_grad)
        + adam_step(query_weight, query_sum, query_mean, query_sqmean, WEIGHT_DECAY)
        + adam_step(
            keyvalue_matrix, keyval_sum, keyvalue_first_moment, keyvalue_second_moment, WEIGHT_DECAY
        )
        + adam_step(outproj_weight, outproj_sum, outproj_mean, outproj_sqmean, WEIGHT_DECAY)
        + adam_step(norm_gains, gains_sum, gains_mean, gains_sqmean, 0.0)
        + up_new
        + down_new
    )


def solution(mesh):
    placed = (
        P(("dp", "tensor"), None),
        P(("dp", "tensor"), None),
        P("dp"),
        P(("dp", "tensor"), None),
        P(("dp", "tensor"), None),
        P(("dp", "tensor"), None),
        P("dp", "tensor"),
        P(None, "dp", "tensor"),
        P("tensor", "dp"),
        P(None, "dp"),
        P(None, "dp", None, "tensor"),
        P("dp", "tensor", None),
        P("dp", "tensor"),
        P("dp", "tensor"),
        P(None, "dp", "tensor"),
        P(None, "dp", "tensor"),
        P("tensor", "dp"),
        P("tensor", "dp"),
        P(None, "dp"),
        P(None, "dp"),
        P(None, "dp", None, "tensor"),
        P(None, "dp", None, "tensor"),
        P("dp", "tensor", None),
        P("dp", "tensor", None),
    )
    return jax.shard_map(
        on_device,
        mesh=mesh,
        in_specs=placed,
        out_specs=(
            P(("dp", "tensor"), None),
            P(("dp", "tensor"), None),
            P(("dp", "tensor"), None),
            P("dp", "tensor"),
            P("dp", "tensor"),
            P("dp", "tensor"),
            P("dp", "tensor"),
            P(None, "dp", "tensor"),
            P(None, "dp", "tensor"),
            P(None, "dp", "tensor"),
            P(None, "dp", "tensor"),
            P("tensor", "dp"),
            P("tensor", "dp"),
            P("tensor", "dp"),
            P("tensor", "dp"),
            P(None, "dp"),
            P(None, "dp"),
            P(None, "dp"),
            P(None, "dp"),
            P(None, "dp", None, "tensor"),
            P(None, "dp", None, "tensor"),
            P(None, "dp", None, "tensor"),
            P(None, "dp", None, "tensor"),
            P("dp", "tensor", None),
            P("dp", "tensor", None),
            P("dp", "tensor", None),
            P("dp", "tensor", None),
        ),
        check_vma=False,
    )
```

```python
import functools
import jax
import jax.numpy as jnp
from jax import lax
from jax.experimental import pallas as pl
from jax.experimental.pallas import tpu as pltpu
from jax.sharding import PartitionSpec as P

HEAD_SIZE = 64
TOP = 8
SEQUENCE_SLOTS = 1024
ADAM_STEP = 5
NORM_EPS = 1e-05
ROPE_THETA = 10000.0
MASKED = -1e30
BETA_ONE = 0.9
BETA_TWO = 0.95
LEARN_RATE = 0.03
WEIGHT_DECAY = 0.1
ADAM_EPS = 1e-08
BF = jnp.bfloat16
F32 = jnp.float32
BLOCK = 256
NN = (((1,), (0,)), ((), ()))
NT = (((1,), (1,)), ((), ()))
TN = (((0,), (0,)), ((), ()))


def mm(a, b, dims=NN):
    return lax.dot_general(a, b, dims, preferred_element_type=F32)


def params(mib=58):
    return pltpu.CompilerParams(vmem_limit_bytes=mib << 20)


def adam_step(weight, gradient, first_old, second_old, decay_rate):
    first_new = BETA_ONE * first_old + (1.0 - BETA_ONE) * gradient
    second_new = BETA_TWO * second_old + (1.0 - BETA_TWO) * gradient * gradient
    first_hat = first_new / (1.0 - BETA_ONE**ADAM_STEP)
    second_hat = second_new / (1.0 - BETA_TWO**ADAM_STEP)
    update = -LEARN_RATE * (first_hat / (jnp.sqrt(second_hat) + ADAM_EPS) + decay_rate * weight)
    return (gradient, first_new, second_new, update)


def rank_body(cap, ecol, ocol, erow, orow, out):
    pairs = erow.shape[1]
    step = 64
    er, orr = erow[...], orow[...]

    def chunk(i, acc):
        rows = pl.ds(i * step, step)
        hit = (ecol[rows, :] == er) & (ocol[rows, :] < orr)
        return acc + jnp.sum(hit.astype(jnp.int32), axis=0, keepdims=True)

    rank = lax.fori_loop(0, pairs // step, chunk, jnp.zeros((1, pairs), jnp.int32))
    kept = (orr < pairs) & (rank < cap)
    out[...] = jnp.where(kept, er * cap + rank, -1)


def slot_targets(experts, order, live_pairs, cap):
    pairs = experts.shape[0]
    order = jnp.where(live_pairs, order, pairs)
    return pl.pallas_call(
        functools.partial(rank_body, cap),
        out_shape=jax.ShapeDtypeStruct((1, pairs), jnp.int32),
        compiler_params=params(16),
        name="slot_targets",
    )(experts[:, None], order[:, None], experts[None, :], order[None, :])[0]


def swap_halves(u):
    width = u.shape[1]
    lane = lax.broadcasted_iota(jnp.int32, u.shape, 1) % HEAD_SIZE
    half = HEAD_SIZE // 2
    return jnp.where(lane < half, pltpu.roll(u, width - half, 1), pltpu.roll(u, half, 1))


def rope(u, cos, sin):
    reps = u.shape[1] // cos.shape[1]
    if reps > 1:
        cos = jnp.concatenate([cos] * reps, axis=1)
        sin = jnp.concatenate([sin] * reps, axis=1)
    return u * cos + swap_halves(u) * sin


def rope_lanes(rows):
    lane = jnp.arange(128) % HEAD_SIZE
    half = HEAD_SIZE // 2
    positions = (jnp.arange(rows) % SEQUENCE_SLOTS).astype(F32)
    freqs = ROPE_THETA ** (-(2.0 * (lane % half).astype(F32)) / HEAD_SIZE)
    angles = positions[:, None] * freqs[None, :]
    return jnp.cos(angles), jnp.where(lane < half, -1.0, 1.0) * jnp.sin(angles)


ANY = pl.BlockSpec(memory_space=pltpu.HBM)


def cost(flops, nbytes):
    return pl.CostEstimate(flops=int(flops), bytes_accessed=int(nbytes), transcendentals=0)


def qkv_body(qw, kw, xn, wn, at, *refs):
    xs, ws, refs = refs[:xn], refs[xn : xn + wn], refs[xn + wn :]
    cos, sin, a_out, q_out, k_out, v_out, gains, w_out, x_scr, sem = refs
    step = ws[0].shape[0]
    copies = []
    for i, ref in enumerate(ws):
        rows = pl.ds(pl.multiple_of(at[xn + i] * step, 16), step)
        copies.append(pltpu.make_async_copy(ref, w_out.at[rows, :], sem.at[xn + i]))
    for i, ref in enumerate(xs):
        rows = pl.ds(pl.multiple_of(at[i] * BLOCK, BLOCK), BLOCK)
        copies.append(pltpu.make_async_copy(ref, x_scr.at[rows, :], sem.at[i]))
    for c in copies:
        c.start()
    for c in copies:
        c.wait()
    wide = qw + 2 * kw
    gains[...] = w_out[:, wide + qw :].astype(F32).T[0:8, :]

    def block(i, _):
        rows = pl.ds(pl.multiple_of(i * BLOCK, BLOCK), BLOCK)
        v = x_scr[rows, :].astype(F32)
        r = lax.rsqrt(jnp.mean(v * v, axis=-1, keepdims=True) + NORM_EPS)
        a = (v * r * gains[0:1, :]).astype(BF)
        a_out[rows, :] = a
        y = mm(a, w_out[:, :wide])
        c, s = cos[rows, :], sin[rows, :]
        q_out[rows, :] = rope(y[:, :qw], c, s).astype(BF)
        k_out[rows, :] = rope(y[:, qw : qw + kw], c, s).astype(BF)
        v_out[rows, :] = y[:, qw + kw :].astype(BF)
        return 0

    lax.fori_loop(0, len(xs), block, 0)


def qkv(at, xs, ws, qw, kw, cos, sin):
    rows, width = BLOCK * len(xs), xs[0].shape[1]
    cols = ws[0].shape[1]
    depth = ws[0].shape[0] * len(ws)
    vm = pl.BlockSpec(memory_space=pltpu.VMEM)
    return pl.pallas_call(
        functools.partial(qkv_body, qw, kw, len(xs), len(ws)),
        in_specs=[pl.BlockSpec(memory_space=pltpu.SMEM)]
        + [ANY] * (len(xs) + len(ws))
        + [vm, vm],
        out_specs=[vm] * 6,
        out_shape=[
            jax.ShapeDtypeStruct((rows, width), BF),
            jax.ShapeDtypeStruct((rows, qw), BF),
            jax.ShapeDtypeStruct((rows, kw), BF),
            jax.ShapeDtypeStruct((rows, kw), BF),
            jax.ShapeDtypeStruct((8, width), F32),
            jax.ShapeDtypeStruct((depth, cols), BF),
        ],
        scratch_shapes=[
            pltpu.VMEM((rows, width), BF),
            pltpu.SemaphoreType.DMA((len(xs) + len(ws),)),
        ],
        compiler_params=params(60),
        cost_estimate=cost(2 * rows * width * cols, 2e7),
        name="qkv",
    )(at, *xs, *ws, cos, sin)


def project_body(cols, at, v, w, *outs):
    for i, out in enumerate(outs):
        rows = pl.ds(pl.multiple_of(at[i] * BLOCK, BLOCK), BLOCK)
        out[...] = mm(v[rows, :], w[:, cols[0] : cols[1]], NT).astype(BF)


def project(at, v, w, cols):
    rows, depth = v.shape
    width = w.shape[0]
    vm = pl.BlockSpec(memory_space=pltpu.VMEM)
    return pl.pallas_call(
        functools.partial(project_body, cols),
        in_specs=[pl.BlockSpec(memory_space=pltpu.SMEM), vm, vm],
        out_specs=[vm] * 4,
        out_shape=[jax.ShapeDtypeStruct((BLOCK, width), BF)] * 4,
        compiler_params=params(32),
        cost_estimate=cost(2 * rows * depth * width, 1e7),
        name="project",
    )(at, v, w)


def heads_back_body(cols, at, m0, m1, m2, m3, w, h_out, m_out, sem):
    copies = []
    for i, ref in enumerate((m0, m1, m2, m3)):
        rows = pl.ds(pl.multiple_of(at[i] * BLOCK, BLOCK), BLOCK)
        copies.append(pltpu.make_async_copy(ref, m_out.at[rows, :], sem.at[i]))
    for c in copies:
        c.start()
    for c in copies:
        c.wait()

    def block(i, _):
        rows = pl.ds(pl.multiple_of(i * BLOCK, BLOCK), BLOCK)
        h_out[rows, :] = mm(m_out[rows, :], w[:, cols[0] : cols[1]]).astype(BF)
        return 0

    lax.fori_loop(0, 4, block, 0)


def heads_back(at, ms, w, cols):
    width, qw = w.shape[0], cols[1] - cols[0]
    rows = 4 * BLOCK
    vm = pl.BlockSpec(memory_space=pltpu.VMEM)
    return pl.pallas_call(
        functools.partial(heads_back_body, cols),
        in_specs=[pl.BlockSpec(memory_space=pltpu.SMEM)] + [ANY] * 4 + [vm],
        out_specs=[vm, vm],
        out_shape=[
            jax.ShapeDtypeStruct((rows, qw), BF),
            jax.ShapeDtypeStruct((rows, width), BF),
        ],
        scratch_shapes=[pltpu.SemaphoreType.DMA((4,))],
        compiler_params=params(32),
        cost_estimate=cost(2 * rows * qw * width, 1e7),
        name="heads_back",
    )(at, *ms, w)


def spread(pair_lanes, out):
    lane = lax.broadcasted_iota(jnp.int32, pair_lanes.shape, 1)
    full = pair_lanes.astype(F32)
    first = jnp.where(lane < HEAD_SIZE, full, 0.0)
    second = jnp.where(lane < HEAD_SIZE, 0.0, full)
    out[0] = first.astype(BF)
    out[1] = pltpu.roll(first, HEAD_SIZE, 1).astype(BF)
    out[2] = pltpu.roll(second, HEAD_SIZE, 1).astype(BF)
    out[3] = second.astype(BF)


def attend_body(share, length, q, k, v, o, lse, ks, vs):
    pair, qb = pl.program_id(0), pl.program_id(1)

    @pl.when((pair == 0) & (qb == 0))
    def _():
        spread(k[...], ks)
        spread(v[...], vs)

    scale = HEAD_SIZE**-0.5
    for j in range(SEQUENCE_SLOTS // BLOCK):

        @pl.when(qb == j)
        def _():
            keys = (j + 1) * BLOCK
            kpos = lax.broadcasted_iota(jnp.int32, (BLOCK, keys), 1)
            qpos = lax.broadcasted_iota(jnp.int32, (BLOCK, keys), 0) + j * BLOCK
            allowed = (kpos <= qpos) & (kpos < length[0])
            total = jnp.zeros((BLOCK, 128), F32)
            for u in range(2):
                which = 2 * ((2 * pair + u) // share) + u
                s = mm(q[...], ks[which, :keys, :], NT) * scale
                s = jnp.where(allowed, s, MASKED)
                top = jnp.max(s, axis=-1, keepdims=True)
                e = jnp.exp(s - top)
                den = jnp.sum(e, axis=-1, keepdims=True)
                total += mm(e.astype(BF), vs[which, :keys, :]) / den
                full = jnp.broadcast_to(top + jnp.log(den), (BLOCK, 128))
                lse[0, u : u + 1, :] = full.T[0:1, :]
            o[...] = total.astype(BF)


def attend(length, q, k, v, share):
    rows, qw = q.shape
    kw = k.shape[1]
    assert kw == 128 and rows == SEQUENCE_SLOTS
    pairs = qw // 128
    blocks = rows // BLOCK
    fix = lambda p, b, n: (0, 0)
    return pl.pallas_call(
        functools.partial(attend_body, share),
        grid_spec=pltpu.PrefetchScalarGridSpec(
            num_scalar_prefetch=1,
            grid=(pairs, blocks),
            in_specs=[
                pl.BlockSpec((BLOCK, 128), lambda p, b, n: (b, p)),
                pl.BlockSpec((rows, kw), fix),
                pl.BlockSpec((rows, kw), fix),
            ],
            out_specs=[
                pl.BlockSpec((BLOCK, 128), lambda p, b, n: (b, p)),
                pl.BlockSpec((1, 8, BLOCK), lambda p, b, n: (p, 0, b)),
            ],
            scratch_shapes=[pltpu.VMEM((4, rows, 128), BF), pltpu.VMEM((4, rows, 128), BF)],
        ),
        out_shape=[
            jax.ShapeDtypeStruct((rows, qw), BF),
            jax.ShapeDtypeStruct((pairs, 8, rows), F32),
        ],
        compiler_params=params(32),
        name="attend",
    )(length, q, k, v)


def attend_back_body(
    share, length, q, k, v, o, do, lse, cos, sin, coskv, sinkv, dq, dk, dv, ks, vs, kt, dka, dva
):
    pair, qb = pl.program_id(0), pl.program_id(1)
    scale = HEAD_SIZE**-0.5

    @pl.when((pair == 0) & (qb == 0))
    def _():
        spread(k[...], ks)
        spread(v[...], vs)
        for i in range(4):
            kt[i] = ks[i].astype(F32).T.astype(BF)
        dka[...] = jnp.zeros_like(dka)
        dva[...] = jnp.zeros_like(dva)

    live = length[0]

    @pl.when(qb * BLOCK >= live)
    def _():
        dq[...] = jnp.zeros_like(dq)

    @pl.when(qb * BLOCK < live)
    def _():
        qt, dot_ = q[...], do[...]
        lane = lax.broadcasted_iota(jnp.int32, (BLOCK, 128), 1)
        both = (dot_.astype(F32) * o[...].astype(F32)).T
        zero = jnp.zeros((), BF)
        mine = [lane < HEAD_SIZE, lane >= HEAD_SIZE]
        qm = [jnp.where(m, qt, zero) for m in mine]
        dm = [jnp.where(m, dot_, zero) for m in mine]
        delta = [
            jnp.sum(both[:HEAD_SIZE], axis=0, keepdims=True),
            jnp.sum(both[HEAD_SIZE:], axis=0, keepdims=True),
        ]

        def step(kb, acc):
            rows = pl.ds(pl.multiple_of(kb * BLOCK, BLOCK), BLOCK)
            kpos = lax.broadcasted_iota(jnp.int32, (BLOCK, BLOCK), 0) + kb * BLOCK
            qpos = lax.broadcasted_iota(jnp.int32, (BLOCK, BLOCK), 1) + qb * BLOCK
            allowed = (kpos <= qpos) & (kpos < live)
            for u in range(2):
                g = (2 * pair + u) // share
                which = 2 * g + u
                st = mm(ks[which, rows, :], qt, NT) * scale
                pt = jnp.where(allowed, jnp.exp(st - lse[0, u : u + 1, :]), 0.0)
                dpt = mm(vs[which, rows, :], dot_, NT)
                dst = (pt * (dpt - delta[u])).astype(BF)
                dka[g, rows, :] += mm(dst, qm[u])
                dva[g, rows, :] += mm(pt.astype(BF), dm[u])
                acc += mm(kt[which, :, rows], dst)
            return acc

        last = jnp.minimum(qb + 1, (live + BLOCK - 1) // BLOCK)
        acc = lax.fori_loop(0, last, step, jnp.zeros((128, BLOCK), F32))
        dq[...] = rope(acc.T * scale, cos[...], -sin[...]).astype(BF)

    @pl.when((pair == pl.num_programs(0) - 1) & (qb == pl.num_programs(1) - 1))
    def _():
        lane = lax.broadcasted_iota(jnp.int32, (SEQUENCE_SLOTS, 128), 1)

        def joined(acc):
            both = [acc[g] + pltpu.roll(acc[g], HEAD_SIZE, 1) for g in range(2)]
            return jnp.where(lane < HEAD_SIZE, both[0], both[1])

        dk[...] = rope(joined(dka) * scale, coskv[...], -sinkv[...]).astype(BF)
        dv[...] = joined(dva).astype(BF)


def attend_back(length, q, k, v, o, do, lse, cos, sin, share):
    rows, qw = q.shape
    kw = k.shape[1]
    pairs, blocks = qw // 128, rows // BLOCK
    fix = lambda p, b, n: (0, 0)
    tile = pl.BlockSpec((BLOCK, 128), lambda p, b, n: (b, p))
    whole = pl.BlockSpec((rows, kw), fix)
    part = pl.BlockSpec((BLOCK, 128), lambda p, b, n: (b, 0))
    return pl.pallas_call(
        functools.partial(attend_back_body, share),
        grid_spec=pltpu.PrefetchScalarGridSpec(
            num_scalar_prefetch=1,
            grid=(pairs, blocks),
            in_specs=[
                tile,
                whole,
                whole,
                tile,
                tile,
                pl.BlockSpec((1, 8, BLOCK), lambda p, b, n: (p, 0, b)),
                part,
                part,
                whole,
                whole,
            ],
            out_specs=[tile, whole, whole],
            scratch_shapes=[
                pltpu.VMEM((4, rows, 128), BF),
                pltpu.VMEM((4, rows, 128), BF),
                pltpu.VMEM((4, 128, rows), BF),
                pltpu.VMEM((2, rows, 128), F32),
                pltpu.VMEM((2, rows, 128), F32),
            ],
        ),
        out_shape=[
            jax.ShapeDtypeStruct((rows, qw), BF),
            jax.ShapeDtypeStruct((rows, kw), BF),
            jax.ShapeDtypeStruct((rows, kw), BF),
        ],
        compiler_params=params(32),
        name="attend_back",
    )(length, q, k, v, o, do, lse, cos, sin, cos, sin)


NB = 8


def local_slots(table, first, local):
    at = (lax.broadcasted_iota(jnp.int32, (local, BLOCK), 0) + first).astype(F32)
    slot = jnp.full((local, BLOCK), -1.0, F32)
    gate = jnp.zeros((local, BLOCK), F32)
    for k in range(TOP):
        row = table[k : k + 1, :]
        here = row[:, :BLOCK] == at
        slot = jnp.where(here, row[:, BLOCK : 2 * BLOCK], slot)
        gate = jnp.where(here, row[:, 2 * BLOCK : 3 * BLOCK] + row[:, 3 * BLOCK :], gate)
    return slot, gate


def one_hot(slot, cap):
    at = lax.broadcasted_iota(jnp.int32, (cap, BLOCK), 0).astype(F32)
    return jnp.concatenate(
        [jnp.where(at == slot[e : e + 1, :], 1.0, 0.0) for e in range(slot.shape[0])], axis=0
    )


def load_plane(own, sib, buf, sem):
    return [
        pltpu.make_async_copy(
            ref.at[n % 4, pl.ds(0, BLOCK), :], buf.at[n], sem.at[n]
        )
        for n in range(NB)
        for ref in (own if n < 4 else sib,)
    ]


def wait_pair(i, own, buf, sem):
    for n in (2 * i, 2 * i + 1):
        pltpu.make_async_copy(own.at[0, pl.ds(0, BLOCK), :], buf.at[n], sem.at[n]).wait()


def gather_pair(i, buf, hots, out, local, cap):
    width = buf.shape[2]
    cut = width // 3
    rows = pl.ds(pl.multiple_of(i * 2 * cap, 16), 2 * cap)
    for c in range(3):
        cols = slice(c * cut, (c + 1) * cut)
        got = [mm(hots[j], buf[2 * i + j, :, cols]) for j in range(2)]
        for e in range(local):
            mine = [g[e * cap : (e + 1) * cap, :] for g in got]
            out[e, rows, cols] = jnp.concatenate(mine, axis=0).astype(BF)


def seed_body(cap, plane, fresh, first, own, sib, *refs):
    down = refs[0]
    s_out, u_out, tab, buf, s_scr, d_scr, t_scr, sem, t_sem = refs[1 if fresh else 2 :]
    local = d_scr.shape[0]
    copies = load_plane(own, sib, buf, sem)
    tables = []
    for n in range(NB):
        ref = (own if n < 4 else sib).at[n % 4, pl.ds(BLOCK, TOP), :]
        tables.append(pltpu.make_async_copy(ref, t_scr.at[n], t_sem.at[n]))
    weights = pltpu.make_async_copy(down, d_scr, sem.at[NB + 2])
    for c in tables + copies:
        c.start()
    weights.start()
    for c in tables:
        c.wait()
    for n in range(NB):
        tab[n] = t_scr[n, :, : 4 * BLOCK].astype(F32)

    def gather(i, _):
        hots = []
        for j in range(2):
            slot, _g = local_slots(tab[2 * i + j], first[0], local)
            hots.append(one_hot(slot, cap).astype(BF))
        wait_pair(i, own, buf, sem)
        gather_pair(i, buf, hots, s_scr, local, cap)
        return 0

    lax.fori_loop(0, NB // 2, gather, 0, unroll=2)
    rows = NB * cap
    keep = pltpu.make_async_copy(s_scr, s_out.at[:, pl.ds(plane * rows, rows), :], sem.at[NB + 3])
    keep.start()
    weights.wait()

    def expert(e, _):
        u_out[e] = mm(s_scr[e], d_scr[e], NT)
        return 0

    lax.fori_loop(0, local, expert, 0, unroll=4 if local % 4 == 0 else 1)
    keep.wait()


def seed_rows(plane, planes, first, own, sib, down, kept, cap):
    local, hidden, width = down.shape
    rows = NB * cap
    vm = pl.BlockSpec(memory_space=pltpu.VMEM)
    smem = pl.BlockSpec(memory_space=pltpu.SMEM)
    fresh = kept is None
    more = () if fresh else (kept,)
    return pl.pallas_call(
        functools.partial(seed_body, cap, plane, fresh),
        in_specs=[smem] + [ANY] * (3 + len(more)),
        out_specs=[ANY, vm, vm],
        out_shape=[
            jax.ShapeDtypeStruct((local, planes * rows, width), BF),
            jax.ShapeDtypeStruct((local, rows, hidden), F32),
            jax.ShapeDtypeStruct((NB, TOP, 4 * BLOCK), F32),
        ],
        scratch_shapes=[
            pltpu.VMEM((NB, BLOCK, width), BF),
            pltpu.VMEM((local, rows, width), BF),
            pltpu.VMEM((local, hidden, width), BF),
            pltpu.VMEM((NB, TOP, width), BF),
            pltpu.SemaphoreType.DMA((NB + 4,)),
            pltpu.SemaphoreType.DMA((NB,)),
        ],
        input_output_aliases={} if fresh else {4: 0},
        compiler_params=params(50),
        cost_estimate=cost(2 * rows * local * (BLOCK + hidden) * width, 2e7),
        name="seed_rows",
    )(first, own, sib, down, *more)


def main_body(cap, plane, fresh, first, tab, u, own_in, sib_in, *refs):
    wgu = refs[0]
    refs = refs[1 if fresh else 4 :]
    x_out, d_out, a_out, own, sib = refs[:5]
    buf, x_scr, w_scr, z_scr, p_scr, g_scr, r_scr, d_scr, a_scr, m_scr, sem, out_sem = refs[5:]
    local, hidden = a_scr.shape[0], a_scr.shape[2]
    rows = NB * cap
    slots = local * cap
    copies = load_plane(own_in, sib_in, buf, sem)
    weights = pltpu.make_async_copy(wgu, w_scr, sem.at[NB + 2])
    for c in copies:
        c.start()
    weights.start()

    def gather(i, _):
        hots = []
        for j in range(2):
            b = 2 * i + j
            slot, gate = local_slots(tab[b], first[0], local)
            hot = one_hot(slot, cap)
            spread_gate = jnp.concatenate(
                [jnp.broadcast_to(gate[e : e + 1, :], (cap, BLOCK)) for e in range(local)], axis=0
            )
            weight = jnp.sum(hot * spread_gate, axis=1, keepdims=True)
            weight = jnp.broadcast_to(weight, (slots, hidden))
            for e in range(local):
                g_scr[e, pl.ds(b * cap, cap), :] = weight[e * cap : (e + 1) * cap, :]
            hots.append(hot.astype(BF))
            p_scr[b] = hots[-1]
        wait_pair(i, own_in, buf, sem)
        gather_pair(i, buf, hots, x_scr, local, cap)
        return 0

    lax.fori_loop(0, NB // 2, gather, 0, unroll=2)
    here = pl.ds(plane * rows, rows)
    keep_x = pltpu.make_async_copy(x_scr, x_out.at[:, here, :], sem.at[NB + 3])
    keep_x.start()
    weights.wait()

    def expert(e, _):
        gu = mm(x_scr[e], w_scr[e])
        gate, up = gu[:, :hidden], gu[:, hidden:]
        sig = 1.0 / (1.0 + jnp.exp(-gate))
        silu = gate * sig
        act = (silu * up).astype(BF).astype(F32)
        ue = u[e]
        w = g_scr[e]
        inner = w * ue
        dg = inner * up * sig * (1.0 + gate * (1.0 - sig))
        d = jnp.concatenate([dg, inner * silu], axis=1).astype(BF)
        d_scr[e] = d
        a_scr[e] = (act * w).astype(BF)
        r_scr[e] = act * ue
        z_scr[e] = mm(d, w_scr[e], NT)
        return 0

    lax.fori_loop(0, local, expert, 0, unroll=4 if local % 4 == 0 else 1)
    keep_d = pltpu.make_async_copy(d_scr, d_out.at[:, here, :], sem.at[NB + 4])
    keep_a = pltpu.make_async_copy(a_scr, a_out.at[:, here, :], sem.at[NB + 5])
    keep_d.start()
    keep_a.start()

    for half, out in ((1, sib), (0, own)):

        def combine(i, _):
            b = 4 * half + i
            at = pl.ds(b * cap, cap)
            zb = z_scr[:, at, :].reshape(slots, -1).astype(BF)
            m_scr[b, :BLOCK, :] = mm(p_scr[b], zb, TN).astype(BF)
            pair = jnp.sum(r_scr[:, at, :].reshape(slots, hidden), axis=1, keepdims=True)
            hot = p_scr[b].astype(F32) * pair
            per = jnp.concatenate(
                [
                    jnp.sum(hot[e * cap : (e + 1) * cap, :], axis=0, keepdims=True)
                    for e in range(local)
                ],
                axis=0,
            )
            ids = (lax.broadcasted_iota(jnp.int32, (local, BLOCK), 0) + first[0]).astype(F32)
            pairs = []
            for k in range(TOP):
                mine = tab[b, k : k + 1, :BLOCK] == ids
                pairs.append(jnp.sum(jnp.where(mine, per, 0.0), axis=0, keepdims=True))
            tail = jnp.zeros((TOP, m_scr.shape[2] - BLOCK), F32)
            pairs = jnp.concatenate([jnp.concatenate(pairs, axis=0), tail], axis=1)
            m_scr[b, BLOCK:, :] = pairs.astype(BF)
            pltpu.make_async_copy(m_scr.at[b], out.at[i], out_sem.at[b]).start()
            return 0

        lax.fori_loop(0, 4, combine, 0, unroll=2)
    for half, out in ((1, sib), (0, own)):
        for i in range(4):
            b = 4 * half + i
            pltpu.make_async_copy(m_scr.at[b], out.at[i], out_sem.at[b]).wait()
    keep_x.wait()
    keep_d.wait()
    keep_a.wait()


def expert_rows(plane, planes, first, tab, u, own, sib, wgu, kept, cap):
    local, width, two = wgu.shape
    hidden = two // 2
    rows = NB * cap
    vm = pl.BlockSpec(memory_space=pltpu.VMEM)
    smem = pl.BlockSpec(memory_space=pltpu.SMEM)
    fresh = kept is None
    more = () if fresh else tuple(kept)
    total = planes * rows
    return pl.pallas_call(
        functools.partial(main_body, cap, plane, fresh),
        in_specs=[smem, vm, vm] + [ANY] * (3 + len(more)),
        out_specs=[ANY] * 5,
        out_shape=[
            jax.ShapeDtypeStruct((local, total, width), BF),
            jax.ShapeDtypeStruct((local, total, two), BF),
            jax.ShapeDtypeStruct((local, total, hidden), BF),
            jax.ShapeDtypeStruct((4, BLOCK + TOP, width), BF),
            jax.ShapeDtypeStruct((4, BLOCK + TOP, width), BF),
        ],
        scratch_shapes=[
            pltpu.VMEM((NB, BLOCK, width), BF),
            pltpu.VMEM((local, rows, width), BF),
            pltpu.VMEM((local, width, two), BF),
            pltpu.VMEM((local, rows, width), F32),
            pltpu.VMEM((NB, local * cap, BLOCK), BF),
            pltpu.VMEM((local, rows, hidden), F32),
            pltpu.VMEM((local, rows, hidden), F32),
            pltpu.VMEM((local, rows, two), BF),
            pltpu.VMEM((local, rows, hidden), BF),
            pltpu.VMEM((NB, BLOCK + TOP, width), BF),
            pltpu.SemaphoreType.DMA((NB + 6,)),
            pltpu.SemaphoreType.DMA((NB,)),
        ],
        input_output_aliases={} if fresh else {6: 0, 7: 1, 8: 2},
        compiler_params=params(60),
        cost_estimate=cost(2 * rows * local * (2 * BLOCK + 2 * two) * width, 3e7),
        name="expert_rows",
    )(first, tab, u, own, sib, wgu, *more)


def mix_body(cap, plane, first, tab, a, down_in, own, sib, y_scr, a_scr, down, sem):
    local = down.shape[0]
    slots = local * cap
    rows = NB * cap
    load = pltpu.make_async_copy(a.at[:, pl.ds(plane * rows, rows), :], a_scr, sem.at[0])
    half = local // 2
    cuts = [pl.ds(0, half), pl.ds(half, local - half)] if half else [pl.ds(0, local)]
    weights = [
        pltpu.make_async_copy(down_in.at[c], down.at[c], sem.at[1 + i]) for i, c in enumerate(cuts)
    ]
    load.start()
    for w in weights:
        w.start()
    load.wait()
    for w in weights:
        w.wait()

    def expert(e, _):
        y_scr[e] = mm(a_scr[e], down[e])
        return 0

    lax.fori_loop(0, local, expert, 0, unroll=4 if local % 4 == 0 else 1)
    for half, out in ((1, sib), (0, own)):

        def combine(i, _):
            b = 4 * half + i
            slot, _g = local_slots(tab[b], first[0], local)
            hot = one_hot(slot, cap).astype(BF)
            yb = y_scr[:, pl.ds(b * cap, cap), :].reshape(slots, -1).astype(BF)
            out[i] = mm(hot, yb, TN).astype(BF)
            return 0

        lax.fori_loop(0, 4, combine, 0, unroll=2)


def mix_rows(plane, first, tab, a, down, cap):
    local, hidden, width = down.shape
    rows = NB * cap
    vm = pl.BlockSpec(memory_space=pltpu.VMEM)
    return pl.pallas_call(
        functools.partial(mix_body, cap, plane),
        in_specs=[pl.BlockSpec(memory_space=pltpu.SMEM), vm, ANY, ANY],
        out_specs=[vm, vm],
        out_shape=[jax.ShapeDtypeStruct((4, BLOCK, width), BF)] * 2,
        scratch_shapes=[
            pltpu.VMEM((local, rows, width), F32),
            pltpu.VMEM((local, rows, hidden), BF),
            pltpu.VMEM((local, hidden, width), BF),
            pltpu.SemaphoreType.DMA((3,)),
        ],
        compiler_params=params(34),
        cost_estimate=cost(2 * rows * local * (BLOCK + hidden) * width, 2e7),
        name="mix_rows",
    )(first, tab, a, down)


def round_body(turn, up, down, wgu, low):
    hidden = low.shape[1]
    for part in range(2):
        wgu[0, :, part * hidden : (part + 1) * hidden] = up[part, 0].astype(BF)
    low[0] = down[0].astype(BF)


def round_weights(turn, up, down):
    local, hidden, width = down.shape
    return pl.pallas_call(
        round_body,
        grid=(local,),
        in_specs=[
            pl.BlockSpec(memory_space=pltpu.SMEM),
            pl.BlockSpec((2, 1, width, hidden), lambda e: (0, e, 0, 0)),
            pl.BlockSpec((1, hidden, width), lambda e: (e, 0, 0)),
        ],
        out_specs=[
            pl.BlockSpec((1, width, 2 * hidden), lambda e: (e, 0, 0)),
            pl.BlockSpec((1, hidden, width), lambda e: (e, 0, 0)),
        ],
        out_shape=[
            jax.ShapeDtypeStruct((local, width, 2 * hidden), BF),
            jax.ShapeDtypeStruct((local, hidden, width), BF),
        ],
        compiler_params=params(32),
        cost_estimate=cost(0, 28e6),
        name="round_weights",
    )(turn, up, down)


def weights_body(older, turn, x, s, d, a, *refs):
    hidden = a.shape[2]
    ins, outs = refs[:6], refs[6 + older :]
    done = outs[-1]
    done[0] = turn[0]
    dgu = mm(d[0], x[0], TN).T
    for part in range(2):
        grad = dgu[:, part * hidden : (part + 1) * hidden]
        w, mean, sq = (r[part, 0] for r in ins[:3])
        for ref, val in zip(outs[:4], adam_step(w, grad, mean, sq, WEIGHT_DECAY)):
            ref[part, 0] = val
    ddown = mm(a[0], s[0], TN)
    w, mean, sq = (r[0] for r in ins[3:6])
    for ref, val in zip(outs[4:8], adam_step(w, ddown, mean, sq, WEIGHT_DECAY)):
        ref[0] = val


def weights_step(turn, begin, count, x, s, d, a, up, down, older, cuts=2):
    local, rows, width = x.shape
    hidden = a.shape[2]
    part = width // cuts
    wide = pl.BlockSpec((1, rows, part), lambda e, j: (e + begin, 0, j))
    slim = lambda n: pl.BlockSpec((1, rows, n), lambda e, j: (e + begin, 0, 0))
    ups = pl.BlockSpec((2, 1, part, hidden), lambda e, j: (0, e + begin, j, 0))
    downs = pl.BlockSpec((1, hidden, part), lambda e, j: (e + begin, 0, j))
    smem = pl.BlockSpec(memory_space=pltpu.SMEM)
    out = pl.pallas_call(
        functools.partial(weights_body, len(older)),
        grid=(count, cuts),
        in_specs=[smem, wide, wide, slim(2 * hidden), slim(hidden)]
        + [ups] * 3
        + [downs] * 3
        + [ANY] * len(older),
        out_specs=[ups] * 4 + [downs] * 4 + [smem],
        out_shape=[jax.ShapeDtypeStruct(up[0].shape, F32)] * 4
        + [jax.ShapeDtypeStruct(down[0].shape, F32)] * 4
        + [jax.ShapeDtypeStruct((1,), jnp.int32)],
        input_output_aliases={11 + i: i for i in range(len(older))},
        compiler_params=params(),
        cost_estimate=cost(2 * count * rows * width * 3 * hidden, 26e6 * count),
        name="weights_step",
    )(turn, x, s, d, a, *up, *down, *older)
    return list(out[:8]), out[8]


def experts_by_slot(
    moe_in, cotangent, live_rows, target, gate_values, lengths, up, down, capacity, data_size
):
    tensor_size = lax.axis_size("tensor")
    own_rows, model_width = moe_in.shape
    upgate_low, downproj_low = up[0].astype(BF), down[0].astype(BF)
    local_blocks = upgate_low.shape[1]
    expert_total = local_blocks * data_size
    slots = local_blocks * capacity
    kept = target >= 0
    put_at = jnp.where(kept, target, expert_total * capacity)
    fetch_at = jnp.where(kept, target, 0)
    pair_weight = jnp.where(kept, gate_values.reshape(-1), 0.0)

    def send(pair_rows):
        empty = jnp.zeros((expert_total * capacity, model_width), BF)
        filled = empty.at[put_at].set(pair_rows, mode="drop")
        filled = filled.reshape(1, data_size, slots, model_width)
        wide = lax.all_gather(filled, "tensor", axis=0, tiled=True)
        wide = lax.all_to_all(wide, "dp", split_axis=1, concat_axis=1, tiled=True)
        return wide.reshape(tensor_size, data_size, local_blocks, capacity, model_width)

    def bring(parts):
        parts = parts.reshape(tensor_size, data_size, slots, model_width)
        wide = lax.all_to_all(parts.astype(BF), "dp", split_axis=1, concat_axis=1, tiled=True)
        wide = lax.all_to_all(wide, "tensor", split_axis=0, concat_axis=0, tiled=True)
        summed = jnp.sum(wide.astype(F32), axis=0).astype(BF)
        return summed.reshape(expert_total * capacity, model_width)

    def dot(spec, a, b):
        return jnp.einsum(spec, a, b, preferred_element_type=F32)

    rows_in = send(jnp.repeat(moe_in, TOP, axis=0))
    gate_pre = dot("abecd,edf->abecf", rows_in, upgate_low[0])
    up_pre = dot("abecd,edf->abecf", rows_in, upgate_low[1])
    inner_act = (jax.nn.silu(gate_pre) * up_pre).astype(BF)
    pair_out = bring(dot("abecf,efd->abecd", inner_act, downproj_low))[fetch_at].astype(F32)
    mixed = jnp.sum((pair_weight[:, None] * pair_out).reshape(own_rows, TOP, model_width), axis=1)
    seed_grad = cotangent.astype(F32) * live_rows[:, None].astype(F32)
    seed_pairs = jnp.repeat(seed_grad, TOP, axis=0)
    gate_grad = jnp.where(kept, jnp.sum(pair_out * seed_pairs, axis=1), 0.0)
    out_seed = send((pair_weight[:, None] * seed_pairs).astype(BF))
    inner_grad = dot("abecd,efd->abecf", out_seed, downproj_low)
    down_grad = dot("abecf,abecd->efd", inner_act, out_seed)
    sig = jax.nn.sigmoid(gate_pre)
    gate_back = (inner_grad * up_pre * sig * (1.0 + gate_pre * (1.0 - sig))).astype(BF)
    up_back = (inner_grad * gate_pre * sig).astype(BF)
    up_grad = jnp.stack(
        [
            dot("abecd,abecf->edf", rows_in, gate_back),
            dot("abecd,abecf->edf", rows_in, up_back),
        ]
    )
    rows_grad = dot("abecf,edf->abecd", gate_back, upgate_low[0])
    rows_grad = rows_grad + dot("abecf,edf->abecd", up_back, upgate_low[1])
    back = bring(rows_grad)[fetch_at].astype(F32)
    back = jnp.where(kept[:, None], back, 0.0)
    moe_grad = jnp.sum(back.reshape(own_rows, TOP, model_width), axis=1)
    return (
        mixed,
        gate_grad.reshape(own_rows, TOP),
        moe_grad,
        adam_step(up[0], up_grad, *up[1:], WEIGHT_DECAY),
        adam_step(down[0], down_grad, *down[1:], WEIGHT_DECAY),
    )


def flip(v, axis, bit):
    return lax.ppermute(v, axis, [(i, i ^ bit) for i in range(lax.axis_size(axis))])


def core(v):
    return flip(v, "tensor", 1)


def across(v):
    return flip(v, "tensor", 2)


def side(v):
    return flip(v, "dp", 1)


def onward(v, planes=1):
    n = lax.axis_size("dp")
    return lax.ppermute(v, "dp", [(i, (i + 2 * planes) % n) for i in range(n)])


def plus(*vs):
    return functools.reduce(lambda a, b: a + b, [v.astype(F32) for v in vs]).astype(BF)


def meet(*vs):
    return lax.optimization_barrier(vs)


class Spread:
    def __init__(self, own):
        self.z, self.x, self.y, self.d, self.own, self.sib = {0: own}, {}, {}, {}, {}, {}

    def on(self, r):
        self.z[r] = onward(self.z[r - 1])

    def x_(self, r):
        self.x[r] = across(self.z[r])

    def y_(self, r):
        self.y[r] = side(self.z[r])

    def x_on(self, r):
        self.x[r] = onward(self.x[r - 1])

    def y_on(self, r):
        self.y[r] = onward(self.y[r - 1])

    def d_(self, r):
        self.d[r] = across(self.y[r]) if r % 2 else side(self.x[r])

    def cores(self, r):
        self.own[r] = jnp.stack([self.z[r], self.x[r], self.y[r], self.d.pop(r)])
        self.sib[r] = core(self.own[r])

    def state(self):
        return [self.z, self.x, self.y, self.d, self.own, self.sib]

    def put(self, state):
        self.z, self.x, self.y, self.d, self.own, self.sib = state


class Reduce:
    def __init__(self):
        self.own, self.sib, self.parts, self.d = {}, {}, {}, {}
        self.wx, self.wy, self.zx, self.zy, self.total = {}, {}, {}, {}, {}

    def cores(self, r):
        own, came = self.own.pop(r), core(self.sib.pop(r))
        self.parts[r] = [plus(own[i], came[i]) for i in range(4)]

    def part(self, r, i):
        vs = [self.parts[r][i]]
        if i == (2 if r % 2 else 1) and r in self.d:
            vs.append(self.d[r])
        if r == 0 and i == 1:
            vs.append(self.zx[1])
        if r == 0 and i == 2:
            vs.append(self.zy[1])
        return vs

    def d_(self, r):
        v = plus(*self.part(r, 3))
        self.d[r] = across(v) if r % 2 else side(v)

    def x_(self, r):
        self.wx[r] = across(plus(*self.part(r, 1)))

    def y_(self, r):
        self.wy[r] = side(plus(*self.part(r, 2)))

    def x_in(self, r):
        self.zx[r] = onward(plus(*self.part(r, 1)), -1)

    def y_in(self, r):
        self.zy[r] = onward(plus(*self.part(r, 2)), -1)

    def plane(self, r):
        vs = self.part(r, 0)
        vs = vs + [w.pop(r) for w in (self.wx, self.wy, self.total) if r in w]
        return functools.reduce(lambda a, b: a + b, [v.astype(F32) for v in vs])

    def on(self, r, count):
        self.total[(r + 1) % count] = onward(self.plane(r).astype(BF))

    def state(self):
        return [
            self.own, self.sib, self.parts, self.d,
            self.wx, self.wy, self.zx, self.zy, self.total,
        ]

    def put(self, state):
        (
            self.own, self.sib, self.parts, self.d,
            self.wx, self.wy, self.zx, self.zy, self.total,
        ) = state


def data_parts(part):
    n = lax.axis_size("dp")
    me = lax.axis_index("dp")
    planes = n // 2
    pairs = part.reshape((planes, 2, part.shape[0] // n) + part.shape[1:])
    mine = lax.dynamic_index_in_dim(pairs, me % 2, 1, keepdims=False)
    other = lax.dynamic_index_in_dim(pairs, 1 - me % 2, 1, keepdims=False)
    order = [((me // 2) + planes - r) % planes for r in range(planes)]
    at = lambda a, r: lax.dynamic_index_in_dim(a, order[r], 0, keepdims=False)
    return tuple(jnp.stack([at(a, r) for r in range(planes)]) for a in (mine, other))


def pack_weights(query_weight, keyvalue_matrix, outproj_weight, norm_gains):
    return jnp.concatenate(
        [
            query_weight.astype(BF),
            keyvalue_matrix[0].astype(BF),
            keyvalue_matrix[1].astype(BF),
            outproj_weight.astype(BF).T,
            jnp.pad(norm_gains.astype(BF).T, ((0, 0), (0, 126))),
        ],
        axis=1,
    )


def normed(v):
    rms = lax.rsqrt(jnp.mean(v * v, axis=-1, keepdims=True) + NORM_EPS)
    return rms, v * rms


def norm_back(grad, gain, rms, norm):
    scaled = grad * gain
    return rms * (scaled - norm * jnp.mean(scaled * norm, axis=-1, keepdims=True))


def few_groups(
    hidden_in, cotangent, lengths, routes, gate_values, target, live_rows, capacity,
    query_weight, keyvalue_matrix, outproj_weight, norm_gains, up, down,
):
    tensor_index, me = lax.axis_index("tensor"), lax.axis_index("dp")
    count = lax.axis_size("dp") // 2
    qw, kw = query_weight.shape[1], keyvalue_matrix.shape[2]
    share = qw // kw
    local = up[0].shape[1]
    width = hidden_in.shape[1]

    wide = qw + 2 * kw
    out_cols, in_cols = (wide, wide + qw), (0, wide)

    own_packed = pack_weights(query_weight, keyvalue_matrix, outproj_weight, norm_gains)
    w = [own_packed]
    hx, hc = across(hidden_in), core(hidden_in)
    sides = []
    for r in range(count - 1):
        sides.append(side(w[r]))
        w.append(onward(w[r]))
        w[r + 1], sides[r] = meet(w[r + 1], sides[r])
    sides.append(side(w[-1]))
    hxc = core(hx)
    places = [(me + 2 * (count - r)) % (2 * count) for r in range(count)]
    weight_places = [p for r in range(count) for p in (places[r], places[r] ^ 1)]
    at = [tensor_index ^ j for j in range(4)] + weight_places
    at = jnp.stack([jnp.asarray(p, jnp.int32) for p in at])
    cos, sin = rope_lanes(4 * BLOCK)

    seeds = jnp.where(live_rows[:, None], cotangent, jnp.zeros((), BF))
    slot = jnp.where(target >= 0, target - routes.reshape(-1) * capacity, -1).reshape(-1, TOP)
    high = gate_values.astype(BF)
    low = (gate_values - high.astype(F32)).astype(BF)
    table = jnp.concatenate([routes.astype(BF).T, slot.astype(BF).T, high.T, low.T], axis=1)
    table = jnp.pad(table, ((0, 0), (0, width - table.shape[1])))
    first = (me * local).astype(jnp.int32).reshape(1)
    c = Spread(jnp.concatenate([seeds, table], axis=0))
    c.z[0], w[2], hx = meet(c.z[0], w[2], hx)
    c.x_(0)
    c.z[0], w[3] = meet(c.z[0], w[3])
    c.on(1)

    (rows_of, w, sides, cos, sin, st) = meet(
        [hidden_in, hc, hx, hxc], w, sides, cos, sin, c.state()
    )
    c.put(st)
    weight_blocks = [b for r in range(count) for b in (w[r], sides[r])]
    attn_in, q, k, v, gains, packed = qkv(at, rows_of, weight_blocks, qw, kw, cos, sin)
    c.x_(1), c.y_(0), c.on(2)
    q, k, v, gains, st = meet(q, k, v, gains, c.state())
    c.put(st)
    gain_attn, gain_moe = gains[0:1], gains[1:2]
    heads, lse = attend(lengths, q, k, v, share)
    c.x_(2), c.d_(0), c.on(3)
    heads, st = meet(heads, c.state())
    c.put(st)
    near0, near1, far0, far1 = project(at, heads, packed, out_cols)
    far1 = core(far1)
    c.y_(1), c.cores(0)
    near0, near1, far0, far1, st, first = meet(near0, near1, far0, far1, c.state(), first)
    c.put(st)
    sent, near1 = across(plus(far0, far1)), core(near1)
    us, tabs, kept_s = {}, {}, None

    def seed(r):
        nonlocal kept_s
        kept_s, us[r], tabs[r] = seed_rows(
            r, count, first, c.own.pop(r), c.sib.pop(r), down_low, kept_s, capacity
        )

    c.d_(2), c.y_on(2)
    wgu, down_low = round_weights(first, up[0], down[0])
    sent, near0, near1, wgu, down_low, st = meet(sent, near0, near1, wgu, down_low, c.state())
    c.put(st)
    attn_own = plus(near0, near1).astype(F32) + sent.astype(F32)
    hidden = hidden_in.astype(F32)
    middle = hidden + attn_own
    rms_moe, normed_moe = normed(middle)
    m = Spread((normed_moe * gain_moe).astype(BF))
    back, mix = Reduce(), Reduce()
    kept, news, turn = None, [], first

    def expert(r):
        nonlocal kept
        x, dgu, act, back.own[r], back.sib[r] = expert_rows(
            r, count, first, tabs[r], us[r], m.own.pop(r), m.sib.pop(r), wgu, kept, capacity
        )
        kept = (x, dgu, act)

    def mixes(r):
        mix.own[r], mix.sib[r] = mix_rows(r, first, tabs[r], kept[2], down_low, capacity)

    def weights(begin, size):
        nonlocal news, turn
        news, turn = weights_step(
            turn, begin, size, kept[0], kept_s, kept[1], kept[2], up, down, news
        )

    def step():
        nonlocal first, us, tabs, turn
        first, turn, us, tabs, sc, sm, sb, sx = meet(
            first, turn, us, tabs, c.state(), m.state(), back.state(), mix.state()
        )
        c.put(sc), m.put(sm), back.put(sb), mix.put(sx)

    m.z[0], st = meet(m.z[0], c.state())
    c.put(st)
    m.x_(0), m.y_(0), m.on(1)
    seed(0)
    step()
    c.d_(1), m.d_(0), m.y_on(1)
    step()
    m.d_(1), c.y_(3), m.on(2), c.cores(1), m.cores(0)
    step()
    m.x_(2), m.y_(2), m.x_on(1), c.cores(2)
    expert(0)
    step()
    c.d_(3), m.d_(2), m.on(3), m.cores(1)
    seed(1)
    seed(2)
    step()
    m.x_(3), m.y_(3), c.x_on(3), m.cores(2), back.cores(0)
    expert(1)
    step()
    m.d_(3), back.d_(0), back.cores(1), c.cores(3)
    expert(2)
    step()
    back.d_(1), back.x_in(1), back.cores(2), m.cores(3)
    seed(3)
    mixes(0)
    step()
    back.x_(0), back.d_(2), back.on(1, count), mix.cores(0)
    expert(3)
    step()
    back.x_(2), back.y_(2), back.y_in(1), back.cores(3)
    mixes(1)
    step()
    back.d_(3), mix.d_(0), back.on(2, count), mix.cores(1)
    mixes(2)
    step()
    back.x_(3), back.y_(3), mix.x_in(1), mix.cores(2)
    mixes(3)
    weights(0, 1)
    step()
    mix.d_(1), back.y_(0), back.on(3, count), mix.cores(3)
    weights(1, 1)
    step()
    whole = back.plane(0)
    gate_grad, moe_grad = whole[BLOCK:, :BLOCK].T, whole[:BLOCK]

    seed_grad = cotangent.astype(F32) * live_rows[:, None].astype(F32)
    gain_part = jnp.sum(moe_grad * normed_moe, axis=0)
    middle_grad = seed_grad + norm_back(moe_grad, gain_moe, rms_moe, normed_moe)
    mid, turn, st = meet(middle_grad.astype(BF), turn, mix.state())
    mix.put(st)
    mx, mc = across(mid), core(mid)
    mix.d_(2), mix.on(1, count)
    weights(2, 2)
    mx, mc, turn, st, gain_part = meet(mx, mc, turn, mix.state(), gain_part)
    mix.put(st)
    mxc = core(mx)
    heads_grad, middle_low = heads_back(at, [mid, mc, mx, mxc], packed, out_cols)
    outproj_part = mm(middle_low, heads, TN).astype(BF)
    heads_grad, outproj_part, st = meet(heads_grad, outproj_part, mix.state())
    mix.put(st)
    dq, dk, dv = attend_back(lengths, q, k, v, heads, heads_grad, lse, cos, sin, share)
    omine, oother = data_parts(outproj_part)
    ocame = side(oother)
    mix.d_(3), mix.x_(2), mix.y_(2), mix.y_in(1)
    dq, dk, dv, ocame, omine, st = meet(dq, dk, dv, ocame, omine, mix.state())
    mix.put(st)
    osums = plus(omine, ocame)
    ohere = [osums[0]] + [onward(osums[r], -r) for r in range(1, count)]
    dqkv = jnp.concatenate([dq, dk, dv], axis=1)
    near0, near1, far0, far1 = project(at, dqkv, packed, in_cols)
    far1 = core(far1)
    qkv_part = mm(attn_in, dqkv, TN)
    gain_attn_part = jnp.sum(packed[:, :wide].astype(F32) * qkv_part, axis=1) / gain_attn[0]
    gain_rows = jnp.stack([gain_attn_part, gain_part]).reshape(2, 2 * count, -1)
    gain_rows = jnp.pad(gain_rows.transpose(1, 0, 2), ((0, 0), (0, 6), (0, wide - gain_rows.shape[2])))
    qkv_part = qkv_part.astype(BF).reshape(2 * count, -1, wide)
    qkv_part = jnp.concatenate([qkv_part, gain_rows.astype(BF)], axis=1)
    qmine, qother = data_parts(qkv_part.reshape(-1, wide))
    near0, near1, far0, far1, qmine, qother, ohere, st = meet(
        near0, near1, far0, far1, qmine, qother, ohere, mix.state()
    )
    mix.put(st)
    sent, near1 = across(plus(far0, far1)), core(near1)
    qcame = side(qother)
    mix.on(2, count)
    weights(4, 2)
    sent, near0, near1, qcame, qmine, turn, st = meet(
        sent, near0, near1, qcame, qmine, turn, mix.state()
    )
    mix.put(st)
    attn_grad = plus(near0, near1).astype(F32) + sent.astype(F32)
    rms_attn, normed_attn = normed(hidden)
    input_grad = middle_grad + norm_back(attn_grad, gain_attn, rms_attn, normed_attn)
    qsums = plus(qmine, qcame)
    here = [qsums[0]] + [onward(qsums[r], -r) for r in range(1, count)]
    mix.x_(3), mix.y_(3)
    weights(6, 1)
    here, turn, st = meet(here, turn, mix.state())
    mix.put(st)
    mix.on(3, count), mix.x_(0), mix.y_(0)
    weights(7, 1)
    here = functools.reduce(lambda a, b: a + b, [h.astype(F32) for h in here])
    own_rows = norm_gains.shape[1]
    qkv_sum = here[:own_rows]
    outproj_sum = functools.reduce(lambda a, b: a + b, [o.astype(F32) for o in ohere]).T
    gains_sum = here[own_rows : own_rows + 2, :own_rows]
    gains_sum = gains_sum + flip(gains_sum, "tensor", 1)
    gains_sum = gains_sum + flip(gains_sum, "tensor", 2)
    block_out = (middle + mix.plane(0)).astype(BF)
    return (
        block_out, input_grad, gate_grad, qkv_sum, outproj_sum, gains_sum,
        tuple(news[:4]), tuple(news[4:]),
    )


def many_groups(
    hidden_in, cotangent, lengths, routes, gate_values, target, live_rows, capacity,
    query_weight, keyvalue_matrix, outproj_weight, norm_gains, up, down,
):
    qw, kw = query_weight.shape[1], keyvalue_matrix.shape[2]
    share = qw // kw
    packed = pack_weights(query_weight, keyvalue_matrix, outproj_weight, norm_gains)
    packed = lax.all_gather(packed, "dp", axis=0, tiled=True)
    group = lax.all_gather(hidden_in, "tensor", axis=0, tiled=True)
    rows_of = [group[i * BLOCK : (i + 1) * BLOCK] for i in range(4)]
    at = jnp.concatenate([jnp.arange(4, dtype=jnp.int32), jnp.zeros((1,), jnp.int32)])
    cos, sin = rope_lanes(4 * BLOCK)
    attn_in, q, k, v, gains, packed = qkv(at, rows_of, [packed], qw, kw, cos, sin)
    wide = qw + 2 * kw
    qkv_low, outproj_low = packed[:, :wide], packed[:, wide : wide + qw]
    gain_attn, gain_moe = gains[0:1], gains[1:2]
    heads, lse = attend(lengths, q, k, v, share)

    def scattered(part):
        part = lax.psum_scatter(part.astype(BF), "tensor", scatter_dimension=0, tiled=True)
        return part.astype(F32)

    hidden = hidden_in.astype(F32)
    middle = hidden + scattered(mm(heads, outproj_low, NT))
    rms_moe, normed_moe = normed(middle)
    moe_in = (normed_moe * gain_moe).astype(BF)
    mixed, gate_grad, moe_grad, up_new, down_new = experts_by_slot(
        moe_in, cotangent, live_rows, target, gate_values, lengths, up, down, capacity,
        lax.axis_size("dp"),
    )
    block_out = (middle + mixed).astype(BF)
    seed_grad = cotangent.astype(F32) * live_rows[:, None].astype(F32)
    gain_moe_part = jnp.sum(moe_grad * normed_moe, axis=0)
    middle_grad = seed_grad + norm_back(moe_grad, gain_moe, rms_moe, normed_moe)
    middle_low = lax.all_gather(middle_grad.astype(BF), "tensor", axis=0, tiled=True)
    heads_grad = mm(middle_low, outproj_low).astype(BF)
    dq, dk, dv = attend_back(lengths, q, k, v, heads, heads_grad, lse, cos, sin, share)
    dqkv = jnp.concatenate([dq, dk, dv], axis=1)
    attn_grad = scattered(mm(dqkv, qkv_low, NT))
    rms_attn, normed_attn = normed(hidden)
    gain_attn_part = jnp.sum(attn_grad * normed_attn, axis=0)
    input_grad = middle_grad + norm_back(attn_grad, gain_attn, rms_attn, normed_attn)
    gains_sum = lax.psum(jnp.stack([gain_attn_part, gain_moe_part]), ("dp", "tensor"))
    own_cols = norm_gains.shape[1]
    gains_sum = lax.dynamic_slice_in_dim(gains_sum, lax.axis_index("dp") * own_cols, own_cols, 1)
    part = jnp.concatenate([mm(attn_in, dqkv, TN), mm(middle_low, heads, TN)], axis=1)
    summed = lax.psum_scatter(part, "dp", scatter_dimension=0, tiled=True)
    return (
        block_out, input_grad, gate_grad, summed[:, :wide], summed[:, wide:].T, gains_sum,
        up_new, down_new,
    )


def on_device(
    hidden_in,
    cotangent,
    lengths,
    routes,
    gate_values,
    pair_order,
    query_weight,
    keyvalue_matrix,
    outproj_weight,
    norm_gains,
    upgate_weight,
    downproj_weight,
    query_mean,
    query_sqmean,
    keyvalue_first_moment,
    keyvalue_second_moment,
    outproj_mean,
    outproj_sqmean,
    gains_mean,
    gains_sqmean,
    upgate_mean,
    upgate_sqmean,
    downproj_mean,
    downproj_sqmean,
):
    tensor_size = lax.axis_size("tensor")
    data_size = lax.axis_size("dp")
    own_rows, model_width = hidden_in.shape
    group_rows = own_rows * tensor_size
    qw = query_weight.shape[1]
    kw = keyvalue_matrix.shape[2]
    assert lengths.shape[0] == 1 and group_rows == SEQUENCE_SLOTS and own_rows == BLOCK

    tensor_index = lax.axis_index("tensor")
    row_ids = tensor_index * own_rows + jnp.arange(own_rows, dtype=jnp.int32)
    live_rows = row_ids < lengths[0]
    capacity = max(2, own_rows * TOP * 5 // (4 * upgate_weight.shape[1] * data_size))
    target = slot_targets(routes.reshape(-1), pair_order[0], jnp.repeat(live_rows, TOP), capacity)
    few = data_size * group_rows * model_width <= 1 << 24
    block_out, input_grad, gate_grad, qkv_sum, outproj_sum, gains_sum, up_new, down_new = (
        few_groups if few else many_groups
    )(
        hidden_in, cotangent, lengths, routes, gate_values, target, live_rows, capacity,
        query_weight, keyvalue_matrix, outproj_weight, norm_gains,
        (upgate_weight, upgate_mean, upgate_sqmean),
        (downproj_weight, downproj_mean, downproj_sqmean),
    )
    query_sum = qkv_sum[:, :qw]
    keyval_sum = jnp.stack([qkv_sum[:, qw : qw + kw], qkv_sum[:, qw + kw :]])
    return (
        (block_out, input_grad, gate_grad)
        + adam_step(query_weight, query_sum, query_mean, query_sqmean, WEIGHT_DECAY)
        + adam_step(
            keyvalue_matrix, keyval_sum, keyvalue_first_moment, keyvalue_second_moment, WEIGHT_DECAY
        )
        + adam_step(outproj_weight, outproj_sum, outproj_mean, outproj_sqmean, WEIGHT_DECAY)
        + adam_step(norm_gains, gains_sum, gains_mean, gains_sqmean, 0.0)
        + up_new
        + down_new
    )


def solution(mesh):
    placed = (
        P(("dp", "tensor"), None),
        P(("dp", "tensor"), None),
        P("dp"),
        P(("dp", "tensor"), None),
        P(("dp", "tensor"), None),
        P(("dp", "tensor"), None),
        P("dp", "tensor"),
        P(None, "dp", "tensor"),
        P("tensor", "dp"),
        P(None, "dp"),
        P(None, "dp", None, "tensor"),
        P("dp", "tensor", None),
        P("dp", "tensor"),
        P("dp", "tensor"),
        P(None, "dp", "tensor"),
        P(None, "dp", "tensor"),
        P("tensor", "dp"),
        P("tensor", "dp"),
        P(None, "dp"),
        P(None, "dp"),
        P(None, "dp", None, "tensor"),
        P(None, "dp", None, "tensor"),
        P("dp", "tensor", None),
        P("dp", "tensor", None),
    )
    return jax.shard_map(
        on_device,
        mesh=mesh,
        in_specs=placed,
        out_specs=(
            P(("dp", "tensor"), None),
            P(("dp", "tensor"), None),
            P(("dp", "tensor"), None),
            P("dp", "tensor"),
            P("dp", "tensor"),
            P("dp", "tensor"),
            P("dp", "tensor"),
            P(None, "dp", "tensor"),
            P(None, "dp", "tensor"),
            P(None, "dp", "tensor"),
            P(None, "dp", "tensor"),
            P("tensor", "dp"),
            P("tensor", "dp"),
            P("tensor", "dp"),
            P("tensor", "dp"),
            P(None, "dp"),
            P(None, "dp"),
            P(None, "dp"),
            P(None, "dp"),
            P(None, "dp", None, "tensor"),
            P(None, "dp", None, "tensor"),
            P(None, "dp", None, "tensor"),
            P(None, "dp", None, "tensor"),
            P("dp", "tensor", None),
            P("dp", "tensor", None),
            P("dp", "tensor", None),
            P("dp", "tensor", None),
        ),
        check_vma=False,
    )
```

```python
import functools
import jax
import jax.numpy as jnp
from jax import lax
from jax.experimental import pallas as pl
from jax.experimental.pallas import tpu as pltpu
from jax.sharding import PartitionSpec as P

HEAD_SIZE = 64
TOP = 8
SEQUENCE_SLOTS = 1024
ADAM_STEP = 5
NORM_EPS = 1e-05
ROPE_THETA = 10000.0
MASKED = -1e30
BETA_ONE = 0.9
BETA_TWO = 0.95
LEARN_RATE = 0.03
WEIGHT_DECAY = 0.1
ADAM_EPS = 1e-08
BF = jnp.bfloat16
F32 = jnp.float32
BLOCK = 256
NN = (((1,), (0,)), ((), ()))
NT = (((1,), (1,)), ((), ()))
TN = (((0,), (0,)), ((), ()))


def mm(a, b, dims=NN):
    return lax.dot_general(a, b, dims, preferred_element_type=F32)


def params(mib=58):
    return pltpu.CompilerParams(vmem_limit_bytes=mib << 20)


def adam_step(weight, gradient, first_old, second_old, decay_rate):
    first_new = BETA_ONE * first_old + (1.0 - BETA_ONE) * gradient
    second_new = BETA_TWO * second_old + (1.0 - BETA_TWO) * gradient * gradient
    first_hat = first_new / (1.0 - BETA_ONE**ADAM_STEP)
    second_hat = second_new / (1.0 - BETA_TWO**ADAM_STEP)
    update = -LEARN_RATE * (first_hat / (jnp.sqrt(second_hat) + ADAM_EPS) + decay_rate * weight)
    return (gradient, first_new, second_new, update)


def rank_body(cap, ecol, ocol, erow, orow, out):
    pairs = erow.shape[1]
    step = 64
    er, orr = erow[...], orow[...]

    def chunk(i, acc):
        rows = pl.ds(i * step, step)
        hit = (ecol[rows, :] == er) & (ocol[rows, :] < orr)
        return acc + jnp.sum(hit.astype(jnp.int32), axis=0, keepdims=True)

    rank = lax.fori_loop(0, pairs // step, chunk, jnp.zeros((1, pairs), jnp.int32))
    kept = (orr < pairs) & (rank < cap)
    out[...] = jnp.where(kept, er * cap + rank, -1)


def slot_targets(experts, order, live_pairs, cap):
    pairs = experts.shape[0]
    order = jnp.where(live_pairs, order, pairs)
    return pl.pallas_call(
        functools.partial(rank_body, cap),
        out_shape=jax.ShapeDtypeStruct((1, pairs), jnp.int32),
        compiler_params=params(16),
        name="slot_targets",
    )(experts[:, None], order[:, None], experts[None, :], order[None, :])[0]


def swap_halves(u):
    width = u.shape[1]
    lane = lax.broadcasted_iota(jnp.int32, u.shape, 1) % HEAD_SIZE
    half = HEAD_SIZE // 2
    return jnp.where(lane < half, pltpu.roll(u, width - half, 1), pltpu.roll(u, half, 1))


def rope(u, cos, sin):
    reps = u.shape[1] // cos.shape[1]
    if reps > 1:
        cos = jnp.concatenate([cos] * reps, axis=1)
        sin = jnp.concatenate([sin] * reps, axis=1)
    return u * cos + swap_halves(u) * sin


def rope_lanes(rows):
    lane = jnp.arange(128) % HEAD_SIZE
    half = HEAD_SIZE // 2
    positions = (jnp.arange(rows) % SEQUENCE_SLOTS).astype(F32)
    freqs = ROPE_THETA ** (-(2.0 * (lane % half).astype(F32)) / HEAD_SIZE)
    angles = positions[:, None] * freqs[None, :]
    return jnp.cos(angles), jnp.where(lane < half, -1.0, 1.0) * jnp.sin(angles)


ANY = pl.BlockSpec(memory_space=pltpu.HBM)


def cost(flops, nbytes):
    return pl.CostEstimate(flops=int(flops), bytes_accessed=int(nbytes), transcendentals=0)


def qkv_body(qw, kw, xn, wn, at, *refs):
    xs, ws, refs = refs[:xn], refs[xn : xn + wn], refs[xn + wn :]
    cos, sin, a_out, q_out, k_out, v_out, gains, w_out, x_scr, sem = refs
    step = ws[0].shape[0]
    copies = []
    for i, ref in enumerate(ws):
        rows = pl.ds(pl.multiple_of(at[xn + i] * step, 16), step)
        copies.append(pltpu.make_async_copy(ref, w_out.at[rows, :], sem.at[xn + i]))
    for i, ref in enumerate(xs):
        rows = pl.ds(pl.multiple_of(at[i] * BLOCK, BLOCK), BLOCK)
        copies.append(pltpu.make_async_copy(ref, x_scr.at[rows, :], sem.at[i]))
    for c in copies:
        c.start()
    for c in copies:
        c.wait()
    wide = qw + 2 * kw
    gains[...] = w_out[:, wide + qw :].astype(F32).T[0:8, :]

    def block(i, _):
        rows = pl.ds(pl.multiple_of(i * BLOCK, BLOCK), BLOCK)
        v = x_scr[rows, :].astype(F32)
        r = lax.rsqrt(jnp.mean(v * v, axis=-1, keepdims=True) + NORM_EPS)
        a = (v * r * gains[0:1, :]).astype(BF)
        a_out[rows, :] = a
        y = mm(a, w_out[:, :wide])
        c, s = cos[rows, :], sin[rows, :]
        q_out[rows, :] = rope(y[:, :qw], c, s).astype(BF)
        k_out[rows, :] = rope(y[:, qw : qw + kw], c, s).astype(BF)
        v_out[rows, :] = y[:, qw + kw :].astype(BF)
        return 0

    lax.fori_loop(0, len(xs), block, 0)


def qkv(at, xs, ws, qw, kw, cos, sin):
    rows, width = BLOCK * len(xs), xs[0].shape[1]
    cols = ws[0].shape[1]
    depth = ws[0].shape[0] * len(ws)
    vm = pl.BlockSpec(memory_space=pltpu.VMEM)
    return pl.pallas_call(
        functools.partial(qkv_body, qw, kw, len(xs), len(ws)),
        in_specs=[pl.BlockSpec(memory_space=pltpu.SMEM)]
        + [ANY] * (len(xs) + len(ws))
        + [vm, vm],
        out_specs=[vm] * 6,
        out_shape=[
            jax.ShapeDtypeStruct((rows, width), BF),
            jax.ShapeDtypeStruct((rows, qw), BF),
            jax.ShapeDtypeStruct((rows, kw), BF),
            jax.ShapeDtypeStruct((rows, kw), BF),
            jax.ShapeDtypeStruct((8, width), F32),
            jax.ShapeDtypeStruct((depth, cols), BF),
        ],
        scratch_shapes=[
            pltpu.VMEM((rows, width), BF),
            pltpu.SemaphoreType.DMA((len(xs) + len(ws),)),
        ],
        compiler_params=params(60),
        cost_estimate=cost(2 * rows * width * cols, 2e7),
        name="qkv",
    )(at, *xs, *ws, cos, sin)


def project_body(cols, at, v, w, *outs):
    for i, out in enumerate(outs):
        rows = pl.ds(pl.multiple_of(at[i] * BLOCK, BLOCK), BLOCK)
        out[...] = mm(v[rows, :], w[:, cols[0] : cols[1]], NT).astype(BF)


def project(at, v, w, cols):
    rows, depth = v.shape
    width = w.shape[0]
    vm = pl.BlockSpec(memory_space=pltpu.VMEM)
    return pl.pallas_call(
        functools.partial(project_body, cols),
        in_specs=[pl.BlockSpec(memory_space=pltpu.SMEM), vm, vm],
        out_specs=[vm] * 4,
        out_shape=[jax.ShapeDtypeStruct((BLOCK, width), BF)] * 4,
        compiler_params=params(32),
        cost_estimate=cost(2 * rows * depth * width, 1e7),
        name="project",
    )(at, v, w)


def heads_back_body(cols, at, m0, m1, m2, m3, w, h_out, m_out, sem):
    copies = []
    for i, ref in enumerate((m0, m1, m2, m3)):
        rows = pl.ds(pl.multiple_of(at[i] * BLOCK, BLOCK), BLOCK)
        copies.append(pltpu.make_async_copy(ref, m_out.at[rows, :], sem.at[i]))
    for c in copies:
        c.start()
    for c in copies:
        c.wait()

    def block(i, _):
        rows = pl.ds(pl.multiple_of(i * BLOCK, BLOCK), BLOCK)
        h_out[rows, :] = mm(m_out[rows, :], w[:, cols[0] : cols[1]]).astype(BF)
        return 0

    lax.fori_loop(0, 4, block, 0)


def heads_back(at, ms, w, cols):
    width, qw = w.shape[0], cols[1] - cols[0]
    rows = 4 * BLOCK
    vm = pl.BlockSpec(memory_space=pltpu.VMEM)
    return pl.pallas_call(
        functools.partial(heads_back_body, cols),
        in_specs=[pl.BlockSpec(memory_space=pltpu.SMEM)] + [ANY] * 4 + [vm],
        out_specs=[vm, vm],
        out_shape=[
            jax.ShapeDtypeStruct((rows, qw), BF),
            jax.ShapeDtypeStruct((rows, width), BF),
        ],
        scratch_shapes=[pltpu.SemaphoreType.DMA((4,))],
        compiler_params=params(32),
        cost_estimate=cost(2 * rows * qw * width, 1e7),
        name="heads_back",
    )(at, *ms, w)


def spread(pair_lanes, out):
    lane = lax.broadcasted_iota(jnp.int32, pair_lanes.shape, 1)
    full = pair_lanes.astype(F32)
    first = jnp.where(lane < HEAD_SIZE, full, 0.0)
    second = jnp.where(lane < HEAD_SIZE, 0.0, full)
    out[0] = first.astype(BF)
    out[1] = pltpu.roll(first, HEAD_SIZE, 1).astype(BF)
    out[2] = pltpu.roll(second, HEAD_SIZE, 1).astype(BF)
    out[3] = second.astype(BF)


def attend_body(share, length, q, k, v, o, lse, ks, vs):
    pair, qb = pl.program_id(0), pl.program_id(1)

    @pl.when((pair == 0) & (qb == 0))
    def _():
        spread(k[...], ks)
        spread(v[...], vs)

    scale = HEAD_SIZE**-0.5
    for j in range(SEQUENCE_SLOTS // BLOCK):

        @pl.when(qb == j)
        def _():
            keys = (j + 1) * BLOCK
            kpos = lax.broadcasted_iota(jnp.int32, (BLOCK, keys), 1)
            qpos = lax.broadcasted_iota(jnp.int32, (BLOCK, keys), 0) + j * BLOCK
            allowed = (kpos <= qpos) & (kpos < length[0])
            total = jnp.zeros((BLOCK, 128), F32)
            for u in range(2):
                which = 2 * ((2 * pair + u) // share) + u
                s = mm(q[...], ks[which, :keys, :], NT) * scale
                s = jnp.where(allowed, s, MASKED)
                top = jnp.max(s, axis=-1, keepdims=True)
                e = jnp.exp(s - top)
                den = jnp.sum(e, axis=-1, keepdims=True)
                total += mm(e.astype(BF), vs[which, :keys, :]) / den
                full = jnp.broadcast_to(top + jnp.log(den), (BLOCK, 128))
                lse[0, u : u + 1, :] = full.T[0:1, :]
            o[...] = total.astype(BF)


def attend(length, q, k, v, share):
    rows, qw = q.shape
    kw = k.shape[1]
    assert kw == 128 and rows == SEQUENCE_SLOTS
    pairs = qw // 128
    blocks = rows // BLOCK
    fix = lambda p, b, n: (0, 0)
    return pl.pallas_call(
        functools.partial(attend_body, share),
        grid_spec=pltpu.PrefetchScalarGridSpec(
            num_scalar_prefetch=1,
            grid=(pairs, blocks),
            in_specs=[
                pl.BlockSpec((BLOCK, 128), lambda p, b, n: (b, p)),
                pl.BlockSpec((rows, kw), fix),
                pl.BlockSpec((rows, kw), fix),
            ],
            out_specs=[
                pl.BlockSpec((BLOCK, 128), lambda p, b, n: (b, p)),
                pl.BlockSpec((1, 8, BLOCK), lambda p, b, n: (p, 0, b)),
            ],
            scratch_shapes=[pltpu.VMEM((4, rows, 128), BF), pltpu.VMEM((4, rows, 128), BF)],
        ),
        out_shape=[
            jax.ShapeDtypeStruct((rows, qw), BF),
            jax.ShapeDtypeStruct((pairs, 8, rows), F32),
        ],
        compiler_params=params(32),
        name="attend",
    )(length, q, k, v)


def attend_back_body(
    share, length, q, k, v, o, do, lse, cos, sin, coskv, sinkv, dq, dk, dv, ks, vs, kt, dka, dva
):
    pair, qb = pl.program_id(0), pl.program_id(1)
    scale = HEAD_SIZE**-0.5

    @pl.when((pair == 0) & (qb == 0))
    def _():
        spread(k[...], ks)
        spread(v[...], vs)
        for i in range(4):
            kt[i] = ks[i].astype(F32).T.astype(BF)
        dka[...] = jnp.zeros_like(dka)
        dva[...] = jnp.zeros_like(dva)

    live = length[0]

    @pl.when(qb * BLOCK >= live)
    def _():
        dq[...] = jnp.zeros_like(dq)

    @pl.when(qb * BLOCK < live)
    def _():
        qt, dot_ = q[...], do[...]
        lane = lax.broadcasted_iota(jnp.int32, (BLOCK, 128), 1)
        both = (dot_.astype(F32) * o[...].astype(F32)).T
        zero = jnp.zeros((), BF)
        mine = [lane < HEAD_SIZE, lane >= HEAD_SIZE]
        qm = [jnp.where(m, qt, zero) for m in mine]
        dm = [jnp.where(m, dot_, zero) for m in mine]
        delta = [
            jnp.sum(both[:HEAD_SIZE], axis=0, keepdims=True),
            jnp.sum(both[HEAD_SIZE:], axis=0, keepdims=True),
        ]

        def step(kb, acc):
            rows = pl.ds(pl.multiple_of(kb * BLOCK, BLOCK), BLOCK)
            kpos = lax.broadcasted_iota(jnp.int32, (BLOCK, BLOCK), 0) + kb * BLOCK
            qpos = lax.broadcasted_iota(jnp.int32, (BLOCK, BLOCK), 1) + qb * BLOCK
            allowed = (kpos <= qpos) & (kpos < live)
            for u in range(2):
                g = (2 * pair + u) // share
                which = 2 * g + u
                st = mm(ks[which, rows, :], qt, NT) * scale
                pt = jnp.where(allowed, jnp.exp(st - lse[0, u : u + 1, :]), 0.0)
                dpt = mm(vs[which, rows, :], dot_, NT)
                dst = (pt * (dpt - delta[u])).astype(BF)
                dka[g, rows, :] += mm(dst, qm[u])
                dva[g, rows, :] += mm(pt.astype(BF), dm[u])
                acc += mm(kt[which, :, rows], dst)
            return acc

        last = jnp.minimum(qb + 1, (live + BLOCK - 1) // BLOCK)
        acc = lax.fori_loop(0, last, step, jnp.zeros((128, BLOCK), F32))
        dq[...] = rope(acc.T * scale, cos[...], -sin[...]).astype(BF)

    @pl.when((pair == pl.num_programs(0) - 1) & (qb == pl.num_programs(1) - 1))
    def _():
        lane = lax.broadcasted_iota(jnp.int32, (SEQUENCE_SLOTS, 128), 1)

        def joined(acc):
            both = [acc[g] + pltpu.roll(acc[g], HEAD_SIZE, 1) for g in range(2)]
            return jnp.where(lane < HEAD_SIZE, both[0], both[1])

        dk[...] = rope(joined(dka) * scale, coskv[...], -sinkv[...]).astype(BF)
        dv[...] = joined(dva).astype(BF)


def attend_back(length, q, k, v, o, do, lse, cos, sin, share):
    rows, qw = q.shape
    kw = k.shape[1]
    pairs, blocks = qw // 128, rows // BLOCK
    fix = lambda p, b, n: (0, 0)
    tile = pl.BlockSpec((BLOCK, 128), lambda p, b, n: (b, p))
    whole = pl.BlockSpec((rows, kw), fix)
    part = pl.BlockSpec((BLOCK, 128), lambda p, b, n: (b, 0))
    return pl.pallas_call(
        functools.partial(attend_back_body, share),
        grid_spec=pltpu.PrefetchScalarGridSpec(
            num_scalar_prefetch=1,
            grid=(pairs, blocks),
            in_specs=[
                tile,
                whole,
                whole,
                tile,
                tile,
                pl.BlockSpec((1, 8, BLOCK), lambda p, b, n: (p, 0, b)),
                part,
                part,
                whole,
                whole,
            ],
            out_specs=[tile, whole, whole],
            scratch_shapes=[
                pltpu.VMEM((4, rows, 128), BF),
                pltpu.VMEM((4, rows, 128), BF),
                pltpu.VMEM((4, 128, rows), BF),
                pltpu.VMEM((2, rows, 128), F32),
                pltpu.VMEM((2, rows, 128), F32),
            ],
        ),
        out_shape=[
            jax.ShapeDtypeStruct((rows, qw), BF),
            jax.ShapeDtypeStruct((rows, kw), BF),
            jax.ShapeDtypeStruct((rows, kw), BF),
        ],
        compiler_params=params(32),
        name="attend_back",
    )(length, q, k, v, o, do, lse, cos, sin, cos, sin)


NB = 8


def local_slots(table, first, local):
    at = (lax.broadcasted_iota(jnp.int32, (local, BLOCK), 0) + first).astype(F32)
    slot = jnp.full((local, BLOCK), -1.0, F32)
    gate = jnp.zeros((local, BLOCK), F32)
    for k in range(TOP):
        row = table[k : k + 1, :]
        here = row[:, :BLOCK] == at
        slot = jnp.where(here, row[:, BLOCK : 2 * BLOCK], slot)
        gate = jnp.where(here, row[:, 2 * BLOCK : 3 * BLOCK] + row[:, 3 * BLOCK :], gate)
    return slot, gate


def one_hot(slot, cap):
    at = lax.broadcasted_iota(jnp.int32, (cap, BLOCK), 0).astype(F32)
    return jnp.concatenate(
        [jnp.where(at == slot[e : e + 1, :], 1.0, 0.0) for e in range(slot.shape[0])], axis=0
    )


def load_plane(own, sib, buf, sem):
    return [
        pltpu.make_async_copy(
            ref.at[n % 4, pl.ds(0, BLOCK), :], buf.at[n], sem.at[n]
        )
        for n in range(NB)
        for ref in (own if n < 4 else sib,)
    ]


def wait_pair(i, own, buf, sem):
    for n in (2 * i, 2 * i + 1):
        pltpu.make_async_copy(own.at[0, pl.ds(0, BLOCK), :], buf.at[n], sem.at[n]).wait()


def gather_pair(i, buf, hots, out, local, cap):
    width = buf.shape[2]
    cut = width // 3
    rows = pl.ds(pl.multiple_of(i * 2 * cap, 16), 2 * cap)
    for c in range(3):
        cols = slice(c * cut, (c + 1) * cut)
        got = [mm(hots[j], buf[2 * i + j, :, cols]) for j in range(2)]
        for e in range(local):
            mine = [g[e * cap : (e + 1) * cap, :] for g in got]
            out[e, rows, cols] = jnp.concatenate(mine, axis=0).astype(BF)


def seed_body(cap, plane, fresh, first, own, sib, *refs):
    down = refs[0]
    s_out, u_out, tab, buf, s_scr, d_scr, t_scr, sem, t_sem = refs[1 if fresh else 2 :]
    local = d_scr.shape[0]
    copies = load_plane(own, sib, buf, sem)
    tables = []
    for n in range(NB):
        ref = (own if n < 4 else sib).at[n % 4, pl.ds(BLOCK, TOP), :]
        tables.append(pltpu.make_async_copy(ref, t_scr.at[n], t_sem.at[n]))
    weights = pltpu.make_async_copy(down, d_scr, sem.at[NB + 2])
    for c in tables + copies:
        c.start()
    weights.start()
    for c in tables:
        c.wait()
    for n in range(NB):
        tab[n] = t_scr[n, :, : 4 * BLOCK].astype(F32)

    def gather(i, _):
        hots = []
        for j in range(2):
            slot, _g = local_slots(tab[2 * i + j], first[0], local)
            hots.append(one_hot(slot, cap).astype(BF))
        wait_pair(i, own, buf, sem)
        gather_pair(i, buf, hots, s_scr, local, cap)
        return 0

    lax.fori_loop(0, NB // 2, gather, 0)
    rows = NB * cap
    keep = pltpu.make_async_copy(s_scr, s_out.at[:, pl.ds(plane * rows, rows), :], sem.at[NB + 3])
    keep.start()
    weights.wait()

    def expert(e, _):
        u_out[e] = mm(s_scr[e], d_scr[e], NT)
        return 0

    lax.fori_loop(0, local, expert, 0)
    keep.wait()


def seed_rows(plane, planes, first, own, sib, down, kept, cap):
    local, hidden, width = down.shape
    rows = NB * cap
    vm = pl.BlockSpec(memory_space=pltpu.VMEM)
    smem = pl.BlockSpec(memory_space=pltpu.SMEM)
    fresh = kept is None
    more = () if fresh else (kept,)
    return pl.pallas_call(
        functools.partial(seed_body, cap, plane, fresh),
        in_specs=[smem] + [ANY] * (3 + len(more)),
        out_specs=[ANY, vm, vm],
        out_shape=[
            jax.ShapeDtypeStruct((local, planes * rows, width), BF),
            jax.ShapeDtypeStruct((local, rows, hidden), F32),
            jax.ShapeDtypeStruct((NB, TOP, 4 * BLOCK), F32),
        ],
        scratch_shapes=[
            pltpu.VMEM((NB, BLOCK, width), BF),
            pltpu.VMEM((local, rows, width), BF),
            pltpu.VMEM((local, hidden, width), BF),
            pltpu.VMEM((NB, TOP, width), BF),
            pltpu.SemaphoreType.DMA((NB + 4,)),
            pltpu.SemaphoreType.DMA((NB,)),
        ],
        input_output_aliases={} if fresh else {4: 0},
        compiler_params=params(50),
        cost_estimate=cost(2 * rows * local * (BLOCK + hidden) * width, 2e7),
        name="seed_rows",
    )(first, own, sib, down, *more)


def main_body(cap, plane, fresh, first, tab, u, own_in, sib_in, *refs):
    wgu = refs[0]
    refs = refs[1 if fresh else 4 :]
    x_out, d_out, a_out, own, sib = refs[:5]
    buf, x_scr, w_scr, z_scr, p_scr, g_scr, r_scr, d_scr, a_scr, m_scr, sem, out_sem = refs[5:]
    local, hidden = a_scr.shape[0], a_scr.shape[2]
    rows = NB * cap
    slots = local * cap
    copies = load_plane(own_in, sib_in, buf, sem)
    weights = pltpu.make_async_copy(wgu, w_scr, sem.at[NB + 2])
    for c in copies:
        c.start()
    weights.start()

    def gather(i, _):
        hots = []
        for j in range(2):
            b = 2 * i + j
            slot, gate = local_slots(tab[b], first[0], local)
            hot = one_hot(slot, cap)
            spread_gate = jnp.concatenate(
                [jnp.broadcast_to(gate[e : e + 1, :], (cap, BLOCK)) for e in range(local)], axis=0
            )
            weight = jnp.sum(hot * spread_gate, axis=1, keepdims=True)
            weight = jnp.broadcast_to(weight, (slots, hidden))
            for e in range(local):
                g_scr[e, pl.ds(b * cap, cap), :] = weight[e * cap : (e + 1) * cap, :]
            hots.append(hot.astype(BF))
            p_scr[b] = hots[-1]
        wait_pair(i, own_in, buf, sem)
        gather_pair(i, buf, hots, x_scr, local, cap)
        return 0

    lax.fori_loop(0, NB // 2, gather, 0)
    here = pl.ds(plane * rows, rows)
    keep_x = pltpu.make_async_copy(x_scr, x_out.at[:, here, :], sem.at[NB + 3])
    keep_x.start()
    weights.wait()

    def expert(e, _):
        gu = mm(x_scr[e], w_scr[e])
        gate, up = gu[:, :hidden], gu[:, hidden:]
        sig = 1.0 / (1.0 + jnp.exp(-gate))
        silu = gate * sig
        act = (silu * up).astype(BF).astype(F32)
        ue = u[e]
        w = g_scr[e]
        inner = w * ue
        dg = inner * up * sig * (1.0 + gate * (1.0 - sig))
        d = jnp.concatenate([dg, inner * silu], axis=1).astype(BF)
        d_scr[e] = d
        a_scr[e] = (act * w).astype(BF)
        r_scr[e] = act * ue
        z_scr[e] = mm(d, w_scr[e], NT)
        return 0

    lax.fori_loop(0, local, expert, 0, unroll=4 if local % 4 == 0 else 1)
    keep_d = pltpu.make_async_copy(d_scr, d_out.at[:, here, :], sem.at[NB + 4])
    keep_a = pltpu.make_async_copy(a_scr, a_out.at[:, here, :], sem.at[NB + 5])
    keep_d.start()
    keep_a.start()

    for half, out in ((1, sib), (0, own)):

        def combine(i, _):
            b = 4 * half + i
            at = pl.ds(b * cap, cap)
            zb = z_scr[:, at, :].reshape(slots, -1).astype(BF)
            m_scr[b, :BLOCK, :] = mm(p_scr[b], zb, TN).astype(BF)
            pair = jnp.sum(r_scr[:, at, :].reshape(slots, hidden), axis=1, keepdims=True)
            hot = p_scr[b].astype(F32) * pair
            per = jnp.concatenate(
                [
                    jnp.sum(hot[e * cap : (e + 1) * cap, :], axis=0, keepdims=True)
                    for e in range(local)
                ],
                axis=0,
            )
            ids = (lax.broadcasted_iota(jnp.int32, (local, BLOCK), 0) + first[0]).astype(F32)
            pairs = []
            for k in range(TOP):
                mine = tab[b, k : k + 1, :BLOCK] == ids
                pairs.append(jnp.sum(jnp.where(mine, per, 0.0), axis=0, keepdims=True))
            tail = jnp.zeros((TOP, m_scr.shape[2] - BLOCK), F32)
            pairs = jnp.concatenate([jnp.concatenate(pairs, axis=0), tail], axis=1)
            m_scr[b, BLOCK:, :] = pairs.astype(BF)
            pltpu.make_async_copy(m_scr.at[b], out.at[i], out_sem.at[b]).start()
            return 0

        lax.fori_loop(0, 4, combine, 0, unroll=2)
    for half, out in ((1, sib), (0, own)):
        for i in range(4):
            b = 4 * half + i
            pltpu.make_async_copy(m_scr.at[b], out.at[i], out_sem.at[b]).wait()
    keep_x.wait()
    keep_d.wait()
    keep_a.wait()


def expert_rows(plane, planes, first, tab, u, own, sib, wgu, kept, cap):
    local, width, two = wgu.shape
    hidden = two // 2
    rows = NB * cap
    vm = pl.BlockSpec(memory_space=pltpu.VMEM)
    smem = pl.BlockSpec(memory_space=pltpu.SMEM)
    fresh = kept is None
    more = () if fresh else tuple(kept)
    total = planes * rows
    return pl.pallas_call(
        functools.partial(main_body, cap, plane, fresh),
        in_specs=[smem, vm, vm] + [ANY] * (3 + len(more)),
        out_specs=[ANY] * 5,
        out_shape=[
            jax.ShapeDtypeStruct((local, total, width), BF),
            jax.ShapeDtypeStruct((local, total, two), BF),
            jax.ShapeDtypeStruct((local, total, hidden), BF),
            jax.ShapeDtypeStruct((4, BLOCK + TOP, width), BF),
            jax.ShapeDtypeStruct((4, BLOCK + TOP, width), BF),
        ],
        scratch_shapes=[
            pltpu.VMEM((NB, BLOCK, width), BF),
            pltpu.VMEM((local, rows, width), BF),
            pltpu.VMEM((local, width, two), BF),
            pltpu.VMEM((local, rows, width), F32),
            pltpu.VMEM((NB, local * cap, BLOCK), BF),
            pltpu.VMEM((local, rows, hidden), F32),
            pltpu.VMEM((local, rows, hidden), F32),
            pltpu.VMEM((local, rows, two), BF),
            pltpu.VMEM((local, rows, hidden), BF),
            pltpu.VMEM((NB, BLOCK + TOP, width), BF),
            pltpu.SemaphoreType.DMA((NB + 6,)),
            pltpu.SemaphoreType.DMA((NB,)),
        ],
        input_output_aliases={} if fresh else {6: 0, 7: 1, 8: 2},
        compiler_params=params(60),
        cost_estimate=cost(2 * rows * local * (2 * BLOCK + 2 * two) * width, 3e7),
        name="expert_rows",
    )(first, tab, u, own, sib, wgu, *more)


def mix_body(cap, plane, first, tab, a, down_in, own, sib, y_scr, a_scr, down, sem):
    local = down.shape[0]
    slots = local * cap
    rows = NB * cap
    load = pltpu.make_async_copy(a.at[:, pl.ds(plane * rows, rows), :], a_scr, sem.at[0])
    half = local // 2
    cuts = [pl.ds(0, half), pl.ds(half, local - half)] if half else [pl.ds(0, local)]
    weights = [
        pltpu.make_async_copy(down_in.at[c], down.at[c], sem.at[1 + i]) for i, c in enumerate(cuts)
    ]
    load.start()
    for w in weights:
        w.start()
    load.wait()
    for w in weights:
        w.wait()

    def expert(e, _):
        y_scr[e] = mm(a_scr[e], down[e])
        return 0

    lax.fori_loop(0, local, expert, 0, unroll=2 if local % 2 == 0 else 1)
    for half, out in ((1, sib), (0, own)):

        def combine(i, _):
            b = 4 * half + i
            slot, _g = local_slots(tab[b], first[0], local)
            hot = one_hot(slot, cap).astype(BF)
            yb = y_scr[:, pl.ds(b * cap, cap), :].reshape(slots, -1).astype(BF)
            out[i] = mm(hot, yb, TN).astype(BF)
            return 0

        lax.fori_loop(0, 4, combine, 0, unroll=2)


def mix_rows(plane, first, tab, a, down, cap):
    local, hidden, width = down.shape
    rows = NB * cap
    vm = pl.BlockSpec(memory_space=pltpu.VMEM)
    return pl.pallas_call(
        functools.partial(mix_body, cap, plane),
        in_specs=[pl.BlockSpec(memory_space=pltpu.SMEM), vm, ANY, ANY],
        out_specs=[vm, vm],
        out_shape=[jax.ShapeDtypeStruct((4, BLOCK, width), BF)] * 2,
        scratch_shapes=[
            pltpu.VMEM((local, rows, width), F32),
            pltpu.VMEM((local, rows, hidden), BF),
            pltpu.VMEM((local, hidden, width), BF),
            pltpu.SemaphoreType.DMA((3,)),
        ],
        compiler_params=params(34),
        cost_estimate=cost(2 * rows * local * (BLOCK + hidden) * width, 2e7),
        name="mix_rows",
    )(first, tab, a, down)


def round_body(turn, up, down, wgu, low):
    hidden = low.shape[1]
    for part in range(2):
        wgu[0, :, part * hidden : (part + 1) * hidden] = up[part, 0].astype(BF)
    low[0] = down[0].astype(BF)


def round_weights(turn, up, down):
    local, hidden, width = down.shape
    return pl.pallas_call(
        round_body,
        grid=(local,),
        in_specs=[
            pl.BlockSpec(memory_space=pltpu.SMEM),
            pl.BlockSpec((2, 1, width, hidden), lambda e: (0, e, 0, 0)),
            pl.BlockSpec((1, hidden, width), lambda e: (e, 0, 0)),
        ],
        out_specs=[
            pl.BlockSpec((1, width, 2 * hidden), lambda e: (e, 0, 0)),
            pl.BlockSpec((1, hidden, width), lambda e: (e, 0, 0)),
        ],
        out_shape=[
            jax.ShapeDtypeStruct((local, width, 2 * hidden), BF),
            jax.ShapeDtypeStruct((local, hidden, width), BF),
        ],
        compiler_params=params(32),
        cost_estimate=cost(0, 28e6),
        name="round_weights",
    )(turn, up, down)


def weights_body(older, turn, x, s, d, a, *refs):
    hidden = a.shape[2]
    ins, outs = refs[:6], refs[6 + older :]
    done = outs[-1]
    done[0] = turn[0]
    dgu = mm(d[0], x[0], TN).T
    for part in range(2):
        grad = dgu[:, part * hidden : (part + 1) * hidden]
        w, mean, sq = (r[part, 0] for r in ins[:3])
        for ref, val in zip(outs[:4], adam_step(w, grad, mean, sq, WEIGHT_DECAY)):
            ref[part, 0] = val
    ddown = mm(a[0], s[0], TN)
    w, mean, sq = (r[0] for r in ins[3:6])
    for ref, val in zip(outs[4:8], adam_step(w, ddown, mean, sq, WEIGHT_DECAY)):
        ref[0] = val


def weights_step(turn, begin, count, x, s, d, a, up, down, older, cuts=2):
    local, rows, width = x.shape
    hidden = a.shape[2]
    part = width // cuts
    wide = pl.BlockSpec((1, rows, part), lambda e, j: (e + begin, 0, j))
    slim = lambda n: pl.BlockSpec((1, rows, n), lambda e, j: (e + begin, 0, 0))
    ups = pl.BlockSpec((2, 1, part, hidden), lambda e, j: (0, e + begin, j, 0))
    downs = pl.BlockSpec((1, hidden, part), lambda e, j: (e + begin, 0, j))
    smem = pl.BlockSpec(memory_space=pltpu.SMEM)
    out = pl.pallas_call(
        functools.partial(weights_body, len(older)),
        grid=(count, cuts),
        in_specs=[smem, wide, wide, slim(2 * hidden), slim(hidden)]
        + [ups] * 3
        + [downs] * 3
        + [ANY] * len(older),
        out_specs=[ups] * 4 + [downs] * 4 + [smem],
        out_shape=[jax.ShapeDtypeStruct(up[0].shape, F32)] * 4
        + [jax.ShapeDtypeStruct(down[0].shape, F32)] * 4
        + [jax.ShapeDtypeStruct((1,), jnp.int32)],
        input_output_aliases={11 + i: i for i in range(len(older))},
        compiler_params=params(),
        cost_estimate=cost(2 * count * rows * width * 3 * hidden, 26e6 * count),
        name="weights_step",
    )(turn, x, s, d, a, *up, *down, *older)
    return list(out[:8]), out[8]


def experts_by_slot(
    moe_in, cotangent, live_rows, target, gate_values, lengths, up, down, capacity, data_size
):
    tensor_size = lax.axis_size("tensor")
    own_rows, model_width = moe_in.shape
    upgate_low, downproj_low = up[0].astype(BF), down[0].astype(BF)
    local_blocks = upgate_low.shape[1]
    expert_total = local_blocks * data_size
    slots = local_blocks * capacity
    kept = target >= 0
    put_at = jnp.where(kept, target, expert_total * capacity)
    fetch_at = jnp.where(kept, target, 0)
    pair_weight = jnp.where(kept, gate_values.reshape(-1), 0.0)

    def send(pair_rows):
        empty = jnp.zeros((expert_total * capacity, model_width), BF)
        filled = empty.at[put_at].set(pair_rows, mode="drop")
        filled = filled.reshape(1, data_size, slots, model_width)
        wide = lax.all_gather(filled, "tensor", axis=0, tiled=True)
        wide = lax.all_to_all(wide, "dp", split_axis=1, concat_axis=1, tiled=True)
        return wide.reshape(tensor_size, data_size, local_blocks, capacity, model_width)

    def bring(parts):
        parts = parts.reshape(tensor_size, data_size, slots, model_width)
        wide = lax.all_to_all(parts.astype(BF), "dp", split_axis=1, concat_axis=1, tiled=True)
        wide = lax.all_to_all(wide, "tensor", split_axis=0, concat_axis=0, tiled=True)
        summed = jnp.sum(wide.astype(F32), axis=0).astype(BF)
        return summed.reshape(expert_total * capacity, model_width)

    def dot(spec, a, b):
        return jnp.einsum(spec, a, b, preferred_element_type=F32)

    rows_in = send(jnp.repeat(moe_in, TOP, axis=0))
    gate_pre = dot("abecd,edf->abecf", rows_in, upgate_low[0])
    up_pre = dot("abecd,edf->abecf", rows_in, upgate_low[1])
    inner_act = (jax.nn.silu(gate_pre) * up_pre).astype(BF)
    pair_out = bring(dot("abecf,efd->abecd", inner_act, downproj_low))[fetch_at].astype(F32)
    mixed = jnp.sum((pair_weight[:, None] * pair_out).reshape(own_rows, TOP, model_width), axis=1)
    seed_grad = cotangent.astype(F32) * live_rows[:, None].astype(F32)
    seed_pairs = jnp.repeat(seed_grad, TOP, axis=0)
    gate_grad = jnp.where(kept, jnp.sum(pair_out * seed_pairs, axis=1), 0.0)
    out_seed = send((pair_weight[:, None] * seed_pairs).astype(BF))
    inner_grad = dot("abecd,efd->abecf", out_seed, downproj_low)
    down_grad = dot("abecf,abecd->efd", inner_act, out_seed)
    sig = jax.nn.sigmoid(gate_pre)
    gate_back = (inner_grad * up_pre * sig * (1.0 + gate_pre * (1.0 - sig))).astype(BF)
    up_back = (inner_grad * gate_pre * sig).astype(BF)
    up_grad = jnp.stack(
        [
            dot("abecd,abecf->edf", rows_in, gate_back),
            dot("abecd,abecf->edf", rows_in, up_back),
        ]
    )
    rows_grad = dot("abecf,edf->abecd", gate_back, upgate_low[0])
    rows_grad = rows_grad + dot("abecf,edf->abecd", up_back, upgate_low[1])
    back = bring(rows_grad)[fetch_at].astype(F32)
    back = jnp.where(kept[:, None], back, 0.0)
    moe_grad = jnp.sum(back.reshape(own_rows, TOP, model_width), axis=1)
    return (
        mixed,
        gate_grad.reshape(own_rows, TOP),
        moe_grad,
        adam_step(up[0], up_grad, *up[1:], WEIGHT_DECAY),
        adam_step(down[0], down_grad, *down[1:], WEIGHT_DECAY),
    )


def flip(v, axis, bit):
    return lax.ppermute(v, axis, [(i, i ^ bit) for i in range(lax.axis_size(axis))])


def core(v):
    return flip(v, "tensor", 1)


def across(v):
    return flip(v, "tensor", 2)


def side(v):
    return flip(v, "dp", 1)


def onward(v, planes=1):
    n = lax.axis_size("dp")
    return lax.ppermute(v, "dp", [(i, (i + 2 * planes) % n) for i in range(n)])


def plus(*vs):
    return functools.reduce(lambda a, b: a + b, [v.astype(F32) for v in vs]).astype(BF)


def meet(*vs):
    return lax.optimization_barrier(vs)


class Spread:
    def __init__(self, own):
        self.z, self.x, self.y, self.d, self.own, self.sib = {0: own}, {}, {}, {}, {}, {}

    def on(self, r):
        self.z[r] = onward(self.z[r - 1])

    def x_(self, r):
        self.x[r] = across(self.z[r])

    def y_(self, r):
        self.y[r] = side(self.z[r])

    def x_on(self, r):
        self.x[r] = onward(self.x[r - 1])

    def y_on(self, r):
        self.y[r] = onward(self.y[r - 1])

    def d_(self, r):
        self.d[r] = across(self.y[r]) if r % 2 else side(self.x[r])

    def cores(self, r):
        self.own[r] = jnp.stack([self.z[r], self.x[r], self.y[r], self.d.pop(r)])
        self.sib[r] = core(self.own[r])

    def state(self):
        return [self.z, self.x, self.y, self.d, self.own, self.sib]

    def put(self, state):
        self.z, self.x, self.y, self.d, self.own, self.sib = state


class Reduce:
    def __init__(self):
        self.own, self.sib, self.parts, self.d = {}, {}, {}, {}
        self.wx, self.wy, self.zx, self.zy, self.total = {}, {}, {}, {}, {}

    def cores(self, r):
        own, came = self.own.pop(r), core(self.sib.pop(r))
        self.parts[r] = [plus(own[i], came[i]) for i in range(4)]

    def part(self, r, i):
        vs = [self.parts[r][i]]
        if i == (2 if r % 2 else 1) and r in self.d:
            vs.append(self.d[r])
        if r == 0 and i == 1:
            vs.append(self.zx[1])
        if r == 0 and i == 2:
            vs.append(self.zy[1])
        return vs

    def d_(self, r):
        v = plus(*self.part(r, 3))
        self.d[r] = across(v) if r % 2 else side(v)

    def x_(self, r):
        self.wx[r] = across(plus(*self.part(r, 1)))

    def y_(self, r):
        self.wy[r] = side(plus(*self.part(r, 2)))

    def x_in(self, r):
        self.zx[r] = onward(plus(*self.part(r, 1)), -1)

    def y_in(self, r):
        self.zy[r] = onward(plus(*self.part(r, 2)), -1)

    def plane(self, r):
        vs = self.part(r, 0)
        vs = vs + [w.pop(r) for w in (self.wx, self.wy, self.total) if r in w]
        return functools.reduce(lambda a, b: a + b, [v.astype(F32) for v in vs])

    def on(self, r, count):
        self.total[(r + 1) % count] = onward(self.plane(r).astype(BF))

    def state(self):
        return [
            self.own, self.sib, self.parts, self.d,
            self.wx, self.wy, self.zx, self.zy, self.total,
        ]

    def put(self, state):
        (
            self.own, self.sib, self.parts, self.d,
            self.wx, self.wy, self.zx, self.zy, self.total,
        ) = state


def data_parts(part):
    n = lax.axis_size("dp")
    me = lax.axis_index("dp")
    planes = n // 2
    pairs = part.reshape((planes, 2, part.shape[0] // n) + part.shape[1:])
    mine = lax.dynamic_index_in_dim(pairs, me % 2, 1, keepdims=False)
    other = lax.dynamic_index_in_dim(pairs, 1 - me % 2, 1, keepdims=False)
    order = [((me // 2) + planes - r) % planes for r in range(planes)]
    at = lambda a, r: lax.dynamic_index_in_dim(a, order[r], 0, keepdims=False)
    return tuple(jnp.stack([at(a, r) for r in range(planes)]) for a in (mine, other))


def pack_weights(query_weight, keyvalue_matrix, outproj_weight, norm_gains):
    return jnp.concatenate(
        [
            query_weight.astype(BF),
            keyvalue_matrix[0].astype(BF),
            keyvalue_matrix[1].astype(BF),
            outproj_weight.astype(BF).T,
            jnp.pad(norm_gains.astype(BF).T, ((0, 0), (0, 126))),
        ],
        axis=1,
    )


def normed(v):
    rms = lax.rsqrt(jnp.mean(v * v, axis=-1, keepdims=True) + NORM_EPS)
    return rms, v * rms


def norm_back(grad, gain, rms, norm):
    scaled = grad * gain
    return rms * (scaled - norm * jnp.mean(scaled * norm, axis=-1, keepdims=True))


def few_groups(
    hidden_in, cotangent, lengths, routes, gate_values, target, live_rows, capacity,
    query_weight, keyvalue_matrix, outproj_weight, norm_gains, up, down,
):
    tensor_index, me = lax.axis_index("tensor"), lax.axis_index("dp")
    count = lax.axis_size("dp") // 2
    qw, kw = query_weight.shape[1], keyvalue_matrix.shape[2]
    share = qw // kw
    local = up[0].shape[1]
    width = hidden_in.shape[1]

    wide = qw + 2 * kw
    out_cols, in_cols = (wide, wide + qw), (0, wide)

    own_packed = pack_weights(query_weight, keyvalue_matrix, outproj_weight, norm_gains)
    w = [own_packed]
    hx, hc = across(hidden_in), core(hidden_in)
    sides = []
    for r in range(count - 1):
        sides.append(side(w[r]))
        w.append(onward(w[r]))
        w[r + 1], sides[r] = meet(w[r + 1], sides[r])
    sides.append(side(w[-1]))
    hxc = core(hx)
    places = [(me + 2 * (count - r)) % (2 * count) for r in range(count)]
    weight_places = [p for r in range(count) for p in (places[r], places[r] ^ 1)]
    at = [tensor_index ^ j for j in range(4)] + weight_places
    at = jnp.stack([jnp.asarray(p, jnp.int32) for p in at])
    cos, sin = rope_lanes(4 * BLOCK)

    seeds = jnp.where(live_rows[:, None], cotangent, jnp.zeros((), BF))
    slot = jnp.where(target >= 0, target - routes.reshape(-1) * capacity, -1).reshape(-1, TOP)
    high = gate_values.astype(BF)
    low = (gate_values - high.astype(F32)).astype(BF)
    table = jnp.concatenate([routes.astype(BF).T, slot.astype(BF).T, high.T, low.T], axis=1)
    table = jnp.pad(table, ((0, 0), (0, width - table.shape[1])))
    first = (me * local).astype(jnp.int32).reshape(1)
    c = Spread(jnp.concatenate([seeds, table], axis=0))
    c.z[0], w[2], hx = meet(c.z[0], w[2], hx)
    c.x_(0)
    c.z[0], w[3] = meet(c.z[0], w[3])
    c.on(1)

    (rows_of, w, sides, cos, sin, st) = meet(
        [hidden_in, hc, hx, hxc], w, sides, cos, sin, c.state()
    )
    c.put(st)
    weight_blocks = [b for r in range(count) for b in (w[r], sides[r])]
    attn_in, q, k, v, gains, packed = qkv(at, rows_of, weight_blocks, qw, kw, cos, sin)
    c.x_(1), c.y_(0), c.on(2)
    q, k, v, gains, st = meet(q, k, v, gains, c.state())
    c.put(st)
    gain_attn, gain_moe = gains[0:1], gains[1:2]
    heads, lse = attend(lengths, q, k, v, share)
    c.x_(2), c.d_(0), c.on(3)
    heads, st = meet(heads, c.state())
    c.put(st)
    near0, near1, far0, far1 = project(at, heads, packed, out_cols)
    far1 = core(far1)
    c.y_(1), c.cores(0)
    near0, near1, far0, far1, st, first = meet(near0, near1, far0, far1, c.state(), first)
    c.put(st)
    sent, near1 = across(plus(far0, far1)), core(near1)
    us, tabs, kept_s = {}, {}, None

    def seed(r):
        nonlocal kept_s
        kept_s, us[r], tabs[r] = seed_rows(
            r, count, first, c.own.pop(r), c.sib.pop(r), down_low, kept_s, capacity
        )

    c.d_(2), c.y_on(2)
    wgu, down_low = round_weights(first, up[0], down[0])
    sent, near0, near1, wgu, down_low, st = meet(sent, near0, near1, wgu, down_low, c.state())
    c.put(st)
    attn_own = plus(near0, near1).astype(F32) + sent.astype(F32)
    hidden = hidden_in.astype(F32)
    middle = hidden + attn_own
    rms_moe, normed_moe = normed(middle)
    m = Spread((normed_moe * gain_moe).astype(BF))
    back, mix = Reduce(), Reduce()
    kept, news, turn = None, [], first

    def expert(r):
        nonlocal kept
        x, dgu, act, back.own[r], back.sib[r] = expert_rows(
            r, count, first, tabs[r], us[r], m.own.pop(r), m.sib.pop(r), wgu, kept, capacity
        )
        kept = (x, dgu, act)

    def mixes(r):
        mix.own[r], mix.sib[r] = mix_rows(r, first, tabs[r], kept[2], down_low, capacity)

    def weights(begin, size):
        nonlocal news, turn
        news, turn = weights_step(
            turn, begin, size, kept[0], kept_s, kept[1], kept[2], up, down, news
        )

    def step():
        nonlocal first, us, tabs, turn
        first, turn, us, tabs, sc, sm, sb, sx = meet(
            first, turn, us, tabs, c.state(), m.state(), back.state(), mix.state()
        )
        c.put(sc), m.put(sm), back.put(sb), mix.put(sx)

    m.z[0], st = meet(m.z[0], c.state())
    c.put(st)
    m.x_(0), m.y_(0), m.on(1)
    seed(0)
    step()
    c.d_(1), m.d_(0), m.y_on(1)
    step()
    m.d_(1), c.y_(3), m.on(2), c.cores(1), m.cores(0)
    step()
    m.x_(2), m.y_(2), m.x_on(1), c.cores(2)
    expert(0)
    step()
    c.d_(3), m.d_(2), m.on(3), m.cores(1)
    seed(1)
    seed(2)
    step()
    m.x_(3), m.y_(3), c.x_on(3), m.cores(2), back.cores(0)
    expert(1)
    step()
    m.d_(3), back.d_(0), back.cores(1), c.cores(3)
    expert(2)
    step()
    back.d_(1), back.x_in(1), back.cores(2), m.cores(3)
    seed(3)
    mixes(0)
    step()
    back.x_(0), back.d_(2), back.on(1, count), mix.cores(0)
    expert(3)
    step()
    back.x_(2), back.y_(2), back.y_in(1), back.cores(3)
    mixes(1)
    step()
    back.d_(3), mix.d_(0), back.on(2, count), mix.cores(1)
    mixes(2)
    step()
    back.x_(3), back.y_(3), mix.x_in(1), mix.cores(2)
    mixes(3)
    weights(0, 1)
    step()
    mix.d_(1), back.y_(0), back.on(3, count), mix.cores(3)
    weights(1, 1)
    step()
    whole = back.plane(0)
    gate_grad, moe_grad = whole[BLOCK:, :BLOCK].T, whole[:BLOCK]

    seed_grad = cotangent.astype(F32) * live_rows[:, None].astype(F32)
    gain_part = jnp.sum(moe_grad * normed_moe, axis=0)
    middle_grad = seed_grad + norm_back(moe_grad, gain_moe, rms_moe, normed_moe)
    mid, turn, st = meet(middle_grad.astype(BF), turn, mix.state())
    mix.put(st)
    mx, mc = across(mid), core(mid)
    mix.d_(2), mix.on(1, count)
    weights(2, 2)
    mx, mc, turn, st, gain_part = meet(mx, mc, turn, mix.state(), gain_part)
    mix.put(st)
    mxc = core(mx)
    heads_grad, middle_low = heads_back(at, [mid, mc, mx, mxc], packed, out_cols)
    outproj_part = mm(middle_low, heads, TN).astype(BF)
    heads_grad, outproj_part, st = meet(heads_grad, outproj_part, mix.state())
    mix.put(st)
    dq, dk, dv = attend_back(lengths, q, k, v, heads, heads_grad, lse, cos, sin, share)
    omine, oother = data_parts(outproj_part)
    ocame = side(oother)
    mix.d_(3), mix.x_(2), mix.y_(2), mix.y_in(1)
    dq, dk, dv, ocame, omine, st = meet(dq, dk, dv, ocame, omine, mix.state())
    mix.put(st)
    osums = plus(omine, ocame)
    ohere = [osums[0]] + [onward(osums[r], -r) for r in range(1, count)]
    dqkv = jnp.concatenate([dq, dk, dv], axis=1)
    near0, near1, far0, far1 = project(at, dqkv, packed, in_cols)
    far1 = core(far1)
    qkv_part = mm(attn_in, dqkv, TN)
    gain_attn_part = jnp.sum(packed[:, :wide].astype(F32) * qkv_part, axis=1) / gain_attn[0]
    gain_rows = jnp.stack([gain_attn_part, gain_part]).reshape(2, 2 * count, -1)
    gain_rows = jnp.pad(gain_rows.transpose(1, 0, 2), ((0, 0), (0, 6), (0, wide - gain_rows.shape[2])))
    qkv_part = qkv_part.astype(BF).reshape(2 * count, -1, wide)
    qkv_part = jnp.concatenate([qkv_part, gain_rows.astype(BF)], axis=1)
    qmine, qother = data_parts(qkv_part.reshape(-1, wide))
    near0, near1, far0, far1, qmine, qother, ohere, st = meet(
        near0, near1, far0, far1, qmine, qother, ohere, mix.state()
    )
    mix.put(st)
    sent, near1 = across(plus(far0, far1)), core(near1)
    qcame = side(qother)
    mix.on(2, count)
    weights(4, 2)
    sent, near0, near1, qcame, qmine, turn, st = meet(
        sent, near0, near1, qcame, qmine, turn, mix.state()
    )
    mix.put(st)
    attn_grad = plus(near0, near1).astype(F32) + sent.astype(F32)
    rms_attn, normed_attn = normed(hidden)
    input_grad = middle_grad + norm_back(attn_grad, gain_attn, rms_attn, normed_attn)
    qsums = plus(qmine, qcame)
    here = [qsums[0]] + [onward(qsums[r], -r) for r in range(1, count)]
    mix.x_(3), mix.y_(3)
    weights(6, 1)
    here, turn, st = meet(here, turn, mix.state())
    mix.put(st)
    mix.on(3, count), mix.x_(0), mix.y_(0)
    weights(7, 1)
    here = functools.reduce(lambda a, b: a + b, [h.astype(F32) for h in here])
    own_rows = norm_gains.shape[1]
    qkv_sum = here[:own_rows]
    outproj_sum = functools.reduce(lambda a, b: a + b, [o.astype(F32) for o in ohere]).T
    gains_sum = here[own_rows : own_rows + 2, :own_rows]
    gains_sum = gains_sum + flip(gains_sum, "tensor", 1)
    gains_sum = gains_sum + flip(gains_sum, "tensor", 2)
    block_out = (middle + mix.plane(0)).astype(BF)
    return (
        block_out, input_grad, gate_grad, qkv_sum, outproj_sum, gains_sum,
        tuple(news[:4]), tuple(news[4:]),
    )


def many_groups(
    hidden_in, cotangent, lengths, routes, gate_values, target, live_rows, capacity,
    query_weight, keyvalue_matrix, outproj_weight, norm_gains, up, down,
):
    qw, kw = query_weight.shape[1], keyvalue_matrix.shape[2]
    share = qw // kw
    packed = pack_weights(query_weight, keyvalue_matrix, outproj_weight, norm_gains)
    packed = lax.all_gather(packed, "dp", axis=0, tiled=True)
    group = lax.all_gather(hidden_in, "tensor", axis=0, tiled=True)
    rows_of = [group[i * BLOCK : (i + 1) * BLOCK] for i in range(4)]
    at = jnp.concatenate([jnp.arange(4, dtype=jnp.int32), jnp.zeros((1,), jnp.int32)])
    cos, sin = rope_lanes(4 * BLOCK)
    attn_in, q, k, v, gains, packed = qkv(at, rows_of, [packed], qw, kw, cos, sin)
    wide = qw + 2 * kw
    qkv_low, outproj_low = packed[:, :wide], packed[:, wide : wide + qw]
    gain_attn, gain_moe = gains[0:1], gains[1:2]
    heads, lse = attend(lengths, q, k, v, share)

    def scattered(part):
        part = lax.psum_scatter(part.astype(BF), "tensor", scatter_dimension=0, tiled=True)
        return part.astype(F32)

    hidden = hidden_in.astype(F32)
    middle = hidden + scattered(mm(heads, outproj_low, NT))
    rms_moe, normed_moe = normed(middle)
    moe_in = (normed_moe * gain_moe).astype(BF)
    mixed, gate_grad, moe_grad, up_new, down_new = experts_by_slot(
        moe_in, cotangent, live_rows, target, gate_values, lengths, up, down, capacity,
        lax.axis_size("dp"),
    )
    block_out = (middle + mixed).astype(BF)
    seed_grad = cotangent.astype(F32) * live_rows[:, None].astype(F32)
    gain_moe_part = jnp.sum(moe_grad * normed_moe, axis=0)
    middle_grad = seed_grad + norm_back(moe_grad, gain_moe, rms_moe, normed_moe)
    middle_low = lax.all_gather(middle_grad.astype(BF), "tensor", axis=0, tiled=True)
    heads_grad = mm(middle_low, outproj_low).astype(BF)
    dq, dk, dv = attend_back(lengths, q, k, v, heads, heads_grad, lse, cos, sin, share)
    dqkv = jnp.concatenate([dq, dk, dv], axis=1)
    attn_grad = scattered(mm(dqkv, qkv_low, NT))
    rms_attn, normed_attn = normed(hidden)
    gain_attn_part = jnp.sum(attn_grad * normed_attn, axis=0)
    input_grad = middle_grad + norm_back(attn_grad, gain_attn, rms_attn, normed_attn)
    gains_sum = lax.psum(jnp.stack([gain_attn_part, gain_moe_part]), ("dp", "tensor"))
    own_cols = norm_gains.shape[1]
    gains_sum = lax.dynamic_slice_in_dim(gains_sum, lax.axis_index("dp") * own_cols, own_cols, 1)
    part = jnp.concatenate([mm(attn_in, dqkv, TN), mm(middle_low, heads, TN)], axis=1)
    summed = lax.psum_scatter(part, "dp", scatter_dimension=0, tiled=True)
    return (
        block_out, input_grad, gate_grad, summed[:, :wide], summed[:, wide:].T, gains_sum,
        up_new, down_new,
    )


def on_device(
    hidden_in,
    cotangent,
    lengths,
    routes,
    gate_values,
    pair_order,
    query_weight,
    keyvalue_matrix,
    outproj_weight,
    norm_gains,
    upgate_weight,
    downproj_weight,
    query_mean,
    query_sqmean,
    keyvalue_first_moment,
    keyvalue_second_moment,
    outproj_mean,
    outproj_sqmean,
    gains_mean,
    gains_sqmean,
    upgate_mean,
    upgate_sqmean,
    downproj_mean,
    downproj_sqmean,
):
    tensor_size = lax.axis_size("tensor")
    data_size = lax.axis_size("dp")
    own_rows, model_width = hidden_in.shape
    group_rows = own_rows * tensor_size
    qw = query_weight.shape[1]
    kw = keyvalue_matrix.shape[2]
    assert lengths.shape[0] == 1 and group_rows == SEQUENCE_SLOTS and own_rows == BLOCK

    tensor_index = lax.axis_index("tensor")
    row_ids = tensor_index * own_rows + jnp.arange(own_rows, dtype=jnp.int32)
    live_rows = row_ids < lengths[0]
    capacity = max(2, own_rows * TOP * 5 // (4 * upgate_weight.shape[1] * data_size))
    target = slot_targets(routes.reshape(-1), pair_order[0], jnp.repeat(live_rows, TOP), capacity)
    few = data_size * group_rows * model_width <= 1 << 24
    block_out, input_grad, gate_grad, qkv_sum, outproj_sum, gains_sum, up_new, down_new = (
        few_groups if few else many_groups
    )(
        hidden_in, cotangent, lengths, routes, gate_values, target, live_rows, capacity,
        query_weight, keyvalue_matrix, outproj_weight, norm_gains,
        (upgate_weight, upgate_mean, upgate_sqmean),
        (downproj_weight, downproj_mean, downproj_sqmean),
    )
    query_sum = qkv_sum[:, :qw]
    keyval_sum = jnp.stack([qkv_sum[:, qw : qw + kw], qkv_sum[:, qw + kw :]])
    return (
        (block_out, input_grad, gate_grad)
        + adam_step(query_weight, query_sum, query_mean, query_sqmean, WEIGHT_DECAY)
        + adam_step(
            keyvalue_matrix, keyval_sum, keyvalue_first_moment, keyvalue_second_moment, WEIGHT_DECAY
        )
        + adam_step(outproj_weight, outproj_sum, outproj_mean, outproj_sqmean, WEIGHT_DECAY)
        + adam_step(norm_gains, gains_sum, gains_mean, gains_sqmean, 0.0)
        + up_new
        + down_new
    )


def solution(mesh):
    placed = (
        P(("dp", "tensor"), None),
        P(("dp", "tensor"), None),
        P("dp"),
        P(("dp", "tensor"), None),
        P(("dp", "tensor"), None),
        P(("dp", "tensor"), None),
        P("dp", "tensor"),
        P(None, "dp", "tensor"),
        P("tensor", "dp"),
        P(None, "dp"),
        P(None, "dp", None, "tensor"),
        P("dp", "tensor", None),
        P("dp", "tensor"),
        P("dp", "tensor"),
        P(None, "dp", "tensor"),
        P(None, "dp", "tensor"),
        P("tensor", "dp"),
        P("tensor", "dp"),
        P(None, "dp"),
        P(None, "dp"),
        P(None, "dp", None, "tensor"),
        P(None, "dp", None, "tensor"),
        P("dp", "tensor", None),
        P("dp", "tensor", None),
    )
    return jax.shard_map(
        on_device,
        mesh=mesh,
        in_specs=placed,
        out_specs=(
            P(("dp", "tensor"), None),
            P(("dp", "tensor"), None),
            P(("dp", "tensor"), None),
            P("dp", "tensor"),
            P("dp", "tensor"),
            P("dp", "tensor"),
            P("dp", "tensor"),
            P(None, "dp", "tensor"),
            P(None, "dp", "tensor"),
            P(None, "dp", "tensor"),
            P(None, "dp", "tensor"),
            P("tensor", "dp"),
            P("tensor", "dp"),
            P("tensor", "dp"),
            P("tensor", "dp"),
            P(None, "dp"),
            P(None, "dp"),
            P(None, "dp"),
            P(None, "dp"),
            P(None, "dp", None, "tensor"),
            P(None, "dp", None, "tensor"),
            P(None, "dp", None, "tensor"),
            P(None, "dp", None, "tensor"),
            P("dp", "tensor", None),
            P("dp", "tensor", None),
            P("dp", "tensor", None),
            P("dp", "tensor", None),
        ),
        check_vma=False,
    )
```
